256 devices in a mesh: gx: 8 (over x_lo, y), gy: 8 (over z), gz: 4 (over x_hi, core).
Axes of the slice: x: 4 (x_hi: 2, x_lo: 2; x = x_hi * 2 + x_lo), y: 4, z: 8, core: 2. Of those that a mesh axis runs over, the one named last changes fastest.
Arguments:
- checkpoint_store: bfloat16 [32, 9, 1, 64, 1024], P('gz', None, None, 'gy', 'gx'), may hold values from -6 to 6
- holder_peer: int32 [8, 8, 4, 8], P('gx', 'gy'), may hold values from 0 to 3, as said below
- holder_slot: int32 [8, 8, 4, 8], P('gx', 'gy'), may hold values from 0 to 7, as said below
- adjoint_state: float32 [9, 32, 64, 1024], P(None, 'gz', 'gy', 'gx'), may hold values from -6 to 6
- lame_lambda: float32 [32, 64, 1024], P('gz', 'gy', 'gx'), may hold values from 0.1 to 0.3
- lame_mu: float32 [32, 64, 1024], P('gz', 'gy', 'gx'), may hold values from 0.05 to 0.15
- buoyancy: float32 [32, 64, 1024], P('gz', 'gy', 'gx'), may hold values from 0.25 to 0.5
- source_cell: int32 [4, 8, 8, 4], P('gz', 'gy', 'gx'), may hold values from 0 to 8191
- wavelet: float32 [64], replicated, may hold values from -6 to 6
- receiver_cell: int32 [4, 8, 8, 64], P('gz', 'gy', 'gx'), may hold values from 0 to 8191
- traces: float32 [4, 8, 8, 64, 64], P('gz', 'gy', 'gx'), may hold values from -6 to 6
- plan: int32 [2], replicated, may hold values from 0 to 63
Outputs:
- adjoint_final: float32 [9, 32, 64, 1024], P(None, 'gz', 'gy', 'gx')
- image_lambda: float32 [32, 64, 1024], P('gz', 'gy', 'gx')
- image_mu: float32 [32, 64, 1024], P('gz', 'gy', 'gx')
The draws below stay inside these ranges and needn't reach their ends.
Inputs may be any that keep to these rules, and one draw needn't show every extreme that they name: `holder_peer`: within each group of bricks sharing x and y bricks, every holder's 8 slots hold exactly one piece each; for every brick one holder supplies exactly 5 of its pieces and each other holder exactly one. `holder_slot`: slots of one holder are distinct over the pieces it holds.
All inputs are finite; a program needn't handle non-finite values.
Results may differ from the reference program's by a relative error of at most 0.0003.
Values may be sent and summed in bfloat16 or wider, within the bound.
A program may use at most 128 MiB of HBM per device.

```python
import jax
import jax.numpy as jnp

CX = 128
CY = 8
CZ = 8
PIECES = 8
STEPS = 2
NT = 64
SRC_DEV = 4
REC_DEV = 64
LAYERS = 1
CAP = 5
SLOTS = 32
NX = 1024
NY = 64
NZ = 32
N_GX = 8
N_GY = 8
N_GZ = 4


def holder_tables(key):
    base_key = jax.random.fold_in(key, 11)
    key_rotation, key_ordering, key_slotting = jax.random.split(base_key, 3)
    groups = N_GX * N_GY
    rotation = jax.random.randint(key_rotation, (groups, 1, 1), 0, N_GZ)
    requester = jnp.arange(N_GZ, dtype=jnp.int32)[None, :, None]
    piece_index = jnp.arange(PIECES, dtype=jnp.int32)[None, None, :]
    favoured = (requester + rotation) % N_GZ
    others = (requester + rotation + 1 + piece_index - CAP) % N_GZ
    listed = jnp.where(piece_index < CAP, favoured, others)
    listed = jnp.broadcast_to(listed, (groups, N_GZ, PIECES))
    scores = jax.random.randint(key_ordering, (groups, N_GZ, PIECES), 0, 65536) * PIECES + piece_index
    ordering = jnp.argsort(scores, axis=-1)
    peers = jnp.take_along_axis(listed, ordering, axis=-1)
    item_count = N_GZ * PIECES
    flat_peers = peers.reshape(groups, item_count)
    slot_scores = jax.random.randint(key_slotting, (groups, item_count), 0, 65536) * item_count + jnp.arange(item_count, dtype=jnp.int32)[None, :]
    same_holder = flat_peers[:, :, None] == flat_peers[:, None, :]
    earlier = slot_scores[:, None, :] < slot_scores[:, :, None]
    slots = jnp.sum((same_holder & earlier).astype(jnp.int32), axis=2)
    return (peers.reshape(N_GX, N_GY, N_GZ, PIECES).astype(jnp.int32), slots.reshape(N_GX, N_GY, N_GZ, PIECES).astype(jnp.int32))


def draw_holder_peer(key, part):
    return holder_tables(key)[0]


def draw_holder_slot(key, part):
    return holder_tables(key)[1]


def place_ends(result, rng, least, high):
    shape = result.shape
    place = [jax.random.randint(jax.random.fold_in(rng, axis), (), 0, shape[axis]) for axis in range(len(shape))]
    result = result.at[tuple(place)].set(least)
    longest = shape.index(max(shape))
    place[longest] = (place[longest] + 1) % shape[longest]
    return result.at[tuple(place)].set(high)


def block_scale(own_key, shape, cuts, least, high):
    loudness, own = 1.0, jax.random.fold_in(own_key, 6)
    for dim, blocks in cuts:
        steps = jnp.exp(jax.random.uniform(jax.random.fold_in(own, dim), (blocks,), jnp.float32, least / len(cuts), high / len(cuts)))
        loudness = loudness * jnp.repeat(steps, shape[dim] // blocks).reshape([-1 if axis == dim else 1 for axis in range(len(shape))])
    return loudness


def bell_draw(rng, dims, width, most, cuts=(), held_as=jnp.bfloat16):
    factor_of = block_scale(rng, dims, cuts, -0.22, 0.18) if cuts else 1.0
    values = jax.random.normal(rng, dims, jnp.float32) * width * factor_of
    return jnp.minimum(jnp.maximum(values, -most), most).astype(held_as)


def setup_inputs(seed: int = 0) -> dict:
    key_of = jax.random.split(jax.random.key(seed), 13)
    checkpoint_store = bell_draw(key_of[0], (SLOTS, 9, LAYERS, NY, NX), 1.0, 6.0, ((0, 4), (3, 8), (4, 8)))
    holder_peer = draw_holder_peer(jax.random.fold_in(key_of[12], 71), 0)
    holder_slot = draw_holder_slot(jax.random.fold_in(key_of[12], 71), 0)
    adjoint_state = bell_draw(key_of[3], (9, NZ, NY, NX), 1.0, 6.0, ((1, 4), (2, 8), (3, 8)), jnp.float32)
    lame_lambda = jnp.clip(0.1 + 0.20000001043081284 * jax.random.uniform(key_of[4], (NZ, NY, NX), jnp.float32) ** block_scale(key_of[4], (NZ, NY, NX), ((0, 4), (1, 8), (2, 8)), -0.2, 0.2), 0.1, 0.3)
    lame_mu = jnp.clip(0.05 + 0.10000001 * jax.random.uniform(key_of[5], (NZ, NY, NX), jnp.float32) ** block_scale(key_of[5], (NZ, NY, NX), ((0, 4), (1, 8), (2, 8)), -0.2, 0.2), 0.05, 0.15)
    buoyancy = jnp.clip(0.25 + 0.25 * jax.random.uniform(key_of[6], (NZ, NY, NX), jnp.float32) ** block_scale(key_of[6], (NZ, NY, NX), ((0, 4), (1, 8), (2, 8)), -0.2, 0.2), 0.25, 0.5)
    source_cell = place_ends(jax.random.randint(key_of[7], (N_GZ, N_GY, N_GX, SRC_DEV), 0, CZ * CY * CX), jax.random.fold_in(key_of[7], 1), 0, (CZ * CY * CX) - 1).astype(jnp.int32)
    wavelet = bell_draw(key_of[8], (NT,), 1.0, 6.0, (), jnp.float32)
    receiver_cell = place_ends(jax.random.randint(key_of[9], (N_GZ, N_GY, N_GX, REC_DEV), 0, CZ * CY * CX), jax.random.fold_in(key_of[9], 1), 0, (CZ * CY * CX) - 1).astype(jnp.int32)
    traces = bell_draw(key_of[10], (N_GZ, N_GY, N_GX, NT, REC_DEV), 1.0, 6.0, ((0, 4), (1, 8), (2, 8)), jnp.float32)
    plan = jax.random.randint(key_of[11], (STEPS,), 0, NT).astype(jnp.int32)
    return dict(checkpoint_store=checkpoint_store, holder_peer=holder_peer, holder_slot=holder_slot, adjoint_state=adjoint_state, lame_lambda=lame_lambda, lame_mu=lame_mu, buoyancy=buoyancy, source_cell=source_cell, wavelet=wavelet, receiver_cell=receiver_cell, traces=traces, plan=plan)


along_z = 0
along_y = 1
along_x = 2


def shifted(padded, which_axis, offset):
    extents = padded.shape[-3:]
    starts = [1, 1, 1]
    starts[which_axis] = 1 + offset
    return padded[..., starts[0]:starts[0] + extents[0] - 2, starts[1]:starts[1] + extents[1] - 2, starts[2]:starts[2] + extents[2] - 2]


def ahead(padded, which_axis):
    return shifted(padded, which_axis, 1) - shifted(padded, which_axis, 0)


def behind(padded, which_axis):
    return shifted(padded, which_axis, 0) - shifted(padded, which_axis, -1)


def velocity_rates(stress_pad, buoyancy):
    rate_x = buoyancy * (ahead(stress_pad[0], along_x) + behind(stress_pad[3], along_y) + behind(stress_pad[4], along_z))
    rate_y = buoyancy * (behind(stress_pad[3], along_x) + ahead(stress_pad[1], along_y) + behind(stress_pad[5], along_z))
    rate_z = buoyancy * (behind(stress_pad[4], along_x) + behind(stress_pad[5], along_y) + ahead(stress_pad[2], along_z))
    return jnp.stack([rate_x, rate_y, rate_z])


def stress_rates(velocity_pad, lame_lambda, lame_mu):
    strain_xx = behind(velocity_pad[0], along_x)
    strain_yy = behind(velocity_pad[1], along_y)
    strain_zz = behind(velocity_pad[2], along_z)
    dilation = strain_xx + strain_yy + strain_zz
    rate_xx = lame_lambda * dilation + 2.0 * lame_mu * strain_xx
    rate_yy = lame_lambda * dilation + 2.0 * lame_mu * strain_yy
    rate_zz = lame_lambda * dilation + 2.0 * lame_mu * strain_zz
    rate_xy = lame_mu * (ahead(velocity_pad[0], along_y) + ahead(velocity_pad[1], along_x))
    rate_xz = lame_mu * (ahead(velocity_pad[0], along_z) + ahead(velocity_pad[2], along_x))
    rate_yz = lame_mu * (ahead(velocity_pad[1], along_z) + ahead(velocity_pad[2], along_y))
    return jnp.stack([rate_xx, rate_yy, rate_zz, rate_xy, rate_xz, rate_yz])


def imaging_terms(forward_stress, adjoint_stress):
    pressure_fwd = forward_stress[0] + forward_stress[1] + forward_stress[2]
    pressure_adj = adjoint_stress[0] + adjoint_stress[1] + adjoint_stress[2]
    term_lambda = pressure_fwd * pressure_adj
    term_mu = (forward_stress[0] * adjoint_stress[0] + forward_stress[1] * adjoint_stress[1]
               + forward_stress[2] * adjoint_stress[2]
               + 2.0 * (forward_stress[3] * adjoint_stress[3] + forward_stress[4] * adjoint_stress[4]
                        + forward_stress[5] * adjoint_stress[5]))
    return term_lambda, term_mu


def pad_whole(stack):
    return jnp.pad(stack, ((0, 0), (1, 1), (1, 1), (1, 1)))


def global_cells(cells):
    brick_z = jnp.arange(N_GZ, dtype=jnp.int32)[:, None, None, None]
    brick_y = jnp.arange(N_GY, dtype=jnp.int32)[None, :, None, None]
    brick_x = jnp.arange(N_GX, dtype=jnp.int32)[None, None, :, None]
    plane = CY * CX
    z_index = brick_z * CZ + cells // plane
    y_index = brick_y * CY + (cells // CX) % CY
    x_index = brick_x * CX + cells % CX
    return z_index.reshape(-1), y_index.reshape(-1), x_index.reshape(-1)


def inject(stress, cell_lists, values):
    z_index, y_index, x_index = cell_lists
    normal = stress[:3].at[:, z_index, y_index, x_index].add(values)
    return jnp.concatenate([normal, stress[3:]], axis=0)


def reference(checkpoint_store, holder_peer, holder_slot, adjoint_state, lame_lambda, lame_mu, buoyancy,
              source_cell, wavelet, receiver_cell, traces, plan):
    store_view = checkpoint_store.reshape(N_GZ * PIECES, 9, LAYERS, N_GY, CY, N_GX, CX)
    rows = jnp.transpose(holder_peer * PIECES + holder_slot, (2, 3, 1, 0)).astype(jnp.int32)
    brick_y = jnp.arange(N_GY, dtype=jnp.int32)[None, None, :, None]
    brick_x = jnp.arange(N_GX, dtype=jnp.int32)[None, None, None, :]
    picked = store_view[rows, :, :, brick_y, :, brick_x, :]
    state = jnp.transpose(picked, (4, 0, 1, 5, 2, 6, 3, 7)).reshape(9, NZ, NY, NX).astype(jnp.float32)
    source_lists = global_cells(source_cell)
    receiver_lists = global_cells(receiver_cell)
    snapshots = [state[3:]]
    for step_now in range(STEPS):
        velocity = state[:3] + velocity_rates(pad_whole(state[3:]), buoyancy)
        stress = state[3:] + stress_rates(pad_whole(velocity), lame_lambda, lame_mu)
        stress = inject(stress, source_lists, wavelet[plan[step_now]])
        state = jnp.concatenate([velocity, stress], axis=0)
        snapshots.append(stress)
    adjoint = adjoint_state
    image_lambda = jnp.zeros((NZ, NY, NX), jnp.float32)
    image_mu = jnp.zeros((NZ, NY, NX), jnp.float32)
    for step_now in reversed(range(STEPS)):
        samples = traces[:, :, :, plan[step_now], :].reshape(-1)
        stress = inject(adjoint[3:], receiver_lists, samples)
        term_lambda, term_mu = imaging_terms(snapshots[step_now + 1], stress)
        image_lambda = image_lambda + term_lambda
        image_mu = image_mu + term_mu
        stress = stress - stress_rates(pad_whole(adjoint[:3]), lame_lambda, lame_mu)
        velocity = adjoint[:3] - velocity_rates(pad_whole(stress), buoyancy)
        adjoint = jnp.concatenate([velocity, stress], axis=0)
    return adjoint, image_lambda, image_mu
```

```python
import functools

import jax
import jax.numpy as jnp
from jax import lax
from jax.experimental import pallas as pl
from jax.experimental.pallas import tpu as pltpu
from jax.sharding import PartitionSpec as P

MESH = pl.DeviceIdType.MESH
STEPS = 2

ADJ, FWD = 0, 4


def iota3(dim):
    return lax.broadcasted_iota(jnp.int32, (8, 8, 128), dim)


def pack_columns(fields, lane):
    lanes = lax.broadcasted_iota(jnp.int32, (8, 128), 1)
    packed = jnp.zeros((8, 128), jnp.float32)
    for number, field in enumerate(fields):
        for z in range(8):
            at = number * 8 + z
            moved = pltpu.roll(field[z], (at - lane) % 128, 1)
            packed = jnp.where(lanes == at, moved, packed)
    return packed


def unpack_columns(packed, number, lane):
    return jnp.stack([pltpu.roll(packed, (lane - number * 8 - z) % 128, 1) for z in range(8)])


class Halo:
    def __init__(self, xl, xr, yl, yr, zl, zr):
        self.xl, self.xr, self.yl, self.yr, self.zl, self.zr = xl, xr, yl, yr, zl, zr

    def behind_x(self, f, i):
        before = jnp.where(iota3(2) == 0, unpack_columns(self.xl, i, 0), pltpu.roll(f, 1, 2))
        return f - before

    def ahead_x(self, f, i):
        after = jnp.where(iota3(2) == 127, unpack_columns(self.xr, i, 127), pltpu.roll(f, 127, 2))
        return after - f

    def behind_y(self, f, i):
        face = jnp.broadcast_to(self.yl[i], (8, 8, 128))
        return f - jnp.where(iota3(1) == 0, face, pltpu.roll(f, 1, 1))

    def ahead_y(self, f, i):
        face = jnp.broadcast_to(self.yr[i], (8, 8, 128))
        return jnp.where(iota3(1) == 7, face, pltpu.roll(f, 7, 1)) - f

    def behind_z(self, f, i):
        return f - jnp.concatenate([self.zl[i][None], f[:7]], axis=0)

    def ahead_z(self, f, i):
        return jnp.concatenate([f[1:], self.zr[i][None]], axis=0) - f


def kernel(
    sizes,
    store,
    hpeer,
    hslot,
    adj_in,
    lam_in,
    mu_in,
    buoy_in,
    src_in,
    wav_in,
    rec_in,
    tr_in,
    plan_in,
    adj_out,
    il_out,
    im_out,
    lam,
    mu,
    buoy,
    rec,
    traces,
    t_peer,
    t_slot,
    t_src,
    t_wav,
    t_plan,
    gath_s,
    gath_v,
    fv,
    fs,
    av,
    as_,
    a1,
    a0,
    s_xl,
    s_xr,
    s_yl,
    s_yr,
    s_zl,
    s_zr,
    r_xl,
    r_xr,
    r_yl,
    r_yr,
    r_zl,
    r_zr,
    in_sem,
    send_sem,
    recv_sem,
    rs_send,
    rs_recv,
):
    ngx, ngy, ngz = sizes
    gx, gy, gz = lax.axis_index("gx"), lax.axis_index("gy"), lax.axis_index("gz")
    partner = gz + 1 - 2 * lax.rem(gz, 2)
    cross = lax.rem(gz + 2, 4)

    def local(src, dst, n):
        return pltpu.make_async_copy(src, dst, in_sem.at[n])

    loads = dict(
        av=local(adj_in.at[pl.ds(0, 3)], av, 0),
        as_=local(adj_in.at[pl.ds(3, 6)], as_, 1),
        lam=local(lam_in, lam, 2),
        mu=local(mu_in, mu, 3),
        buoy=local(buoy_in, buoy, 4),
        rec=local(rec_in.at[0, 0], rec, 5),
        traces=local(tr_in.at[0, 0, 0], traces, 6),
        plan=local(plan_in, t_plan, 7),
        wav=local(wav_in, t_wav, 8),
        src=local(src_in.at[0, 0, 0], t_src, 9),
        peer=local(hpeer.at[0, 0], t_peer, 10),
        slot=local(hslot.at[0, 0], t_slot, 11),
        own_s=local(store.at[:, pl.ds(3, 6), 0], gath_s.at[pl.ds(gz * 8, 8)], 12),
        own_v=local(store.at[:, pl.ds(0, 3), 0], gath_v.at[pl.ds(gz * 8, 8)], 13),
    )
    for copy in loads.values():
        copy.start()

    barrier = pltpu.get_barrier_semaphore()

    def at(**axes):
        return dict(axes)

    def greet(where):
        pl.semaphore_signal(barrier, inc=1, device_id=where, device_id_type=MESH)

    greeted = 3
    for axis, index, count in (("gx", gx, ngx), ("gy", gy, ngy)):
        for step, exists in ((-1, index > 0), (1, index < count - 1)):

            @pl.when(exists)
            def _():
                greet({axis: index + step})

            greeted = greeted + exists.astype(jnp.int32)
    for d in (1, 2, 3):
        greet({"gz": lax.rem(gz + d, 4)})

    for exists, ref in (
        (gx > 0, r_xl),
        (gx < ngx - 1, r_xr),
        (gy > 0, r_yl),
        (gy < ngy - 1, r_yr),
        (gz > 0, r_zl),
        (gz < ngz - 1, r_zr),
    ):

        @pl.when(jnp.logical_not(exists))
        def _():
            ref[...] = jnp.zeros(ref.shape, jnp.float32)

    pl.semaphore_wait(barrier, greeted)

    def remote(src, dst, n, where):
        return pltpu.make_async_remote_copy(
            src_ref=src,
            dst_ref=dst,
            send_sem=rs_send.at[n],
            recv_sem=rs_recv.at[n],
            device_id={"gz": where},
            device_id_type=MESH,
        )

    mine, theirs = pl.ds(gz * 8, 8), pl.ds(cross * 8, 8)
    st_s, st_v = store.at[:, pl.ds(3, 6), 0], store.at[:, pl.ds(0, 3), 0]
    cross_s = remote(st_s, gath_s.at[mine], 0, cross)
    cross_v = remote(st_v, gath_v.at[mine], 1, cross)
    pair_s = remote(st_s, gath_s.at[mine], 2, partner)
    pair_v = remote(st_v, gath_v.at[mine], 3, partner)
    relay_s = remote(gath_s.at[theirs], gath_s.at[theirs], 4, partner)
    relay_v = remote(gath_v.at[theirs], gath_v.at[theirs], 5, partner)
    cross_s.start()
    cross_v.start()
    pair_s.start()
    pair_v.start()

    ends = (
        ("gx", gx, 1, ngx, s_xr, r_xl),
        ("gx", gx, -1, ngx, s_xl, r_xr),
        ("gy", gy, 1, ngy, s_yr, r_yl),
        ("gy", gy, -1, ngy, s_yl, r_yr),
        ("gz", gz, 1, ngz, s_zr, r_zl),
        ("gz", gz, -1, ngz, s_zl, r_zr),
    )

    def face(r, d, fields):
        axis, index, step, count, source, target = ends[d]
        if axis == "gx":
            src, dst = source.at[r], target.at[r]
        else:
            src, dst = source.at[r, pl.ds(0, fields)], target.at[r, pl.ds(0, fields)]
        copy = pltpu.make_async_remote_copy(
            src_ref=src,
            dst_ref=dst,
            send_sem=send_sem.at[r, d],
            recv_sem=recv_sem.at[r, d],
            device_id={axis: index + step},
            device_id_type=MESH,
        )
        goes = index < count - 1 if step > 0 else index > 0
        comes = index > 0 if step > 0 else index < count - 1
        return copy, goes, comes

    STRESS, VELOCITY = (2, 1, 2, 1, 2, 1), (1, 2, 1, 2, 1, 2)

    def send_faces(r, up, down, counts):
        (xu, yu, zu), (xd, yd, zd) = up, down
        for i, f in enumerate(zu):
            s_zr[r, i] = f[7]
        for i, f in enumerate(zd):
            s_zl[r, i] = f[0]
        for d in (4, 5):
            start(r, d, counts)
        for i, f in enumerate(yu):
            s_yr[r, i] = f[:, 7:8, :]
        for i, f in enumerate(yd):
            s_yl[r, i] = f[:, 0:1, :]
        for d in (2, 3):
            start(r, d, counts)
        s_xr[r] = pack_columns(xu, 127)
        s_xl[r] = pack_columns(xd, 0)
        for d in (0, 1):
            start(r, d, counts)

    def start(r, d, counts):
        copy, goes, _ = face(r, d, counts[d])

        @pl.when(goes)
        def _():
            copy.start()

    def send_stress(r, s):
        send_faces(r, ((s[3], s[4]), (s[3], s[5]), (s[4], s[5])), ((s[0],), (s[1],), (s[2],)), STRESS)

    def send_velocity(r, v):
        send_faces(r, ((v[0],), (v[1],), (v[2],)), ((v[1], v[2]), (v[0], v[2]), (v[0], v[1])), VELOCITY)

    def receive(r, counts):
        for d in range(6):
            copy, _, comes = face(r, d, counts[d])

            @pl.when(comes)
            def _():
                copy.wait_recv()

        return Halo(r_xl[r], r_xr[r], r_yl[r], r_yr[r], r_zl[r], r_zr[r])

    def velocity_rates(s, h):
        b = buoy[...]
        rx = b * (h.ahead_x(s[0], 0) + h.behind_y(s[3], 0) + h.behind_z(s[4], 0))
        ry = b * (h.behind_x(s[3], 0) + h.ahead_y(s[1], 0) + h.behind_z(s[5], 1))
        rz = b * (h.behind_x(s[4], 1) + h.behind_y(s[5], 1) + h.ahead_z(s[2], 0))
        return rx, ry, rz

    def stress_rates(v, h):
        exx, eyy, ezz = h.behind_x(v[0], 0), h.behind_y(v[1], 0), h.behind_z(v[2], 0)
        m = mu[...]
        spread = lam[...] * (exx + eyy + ezz)
        twice = 2.0 * m
        return (
            spread + twice * exx,
            spread + twice * eyy,
            spread + twice * ezz,
            m * (h.ahead_y(v[0], 0) + h.ahead_x(v[1], 0)),
            m * (h.ahead_z(v[0], 0) + h.ahead_x(v[2], 1)),
            m * (h.ahead_z(v[1], 1) + h.ahead_y(v[2], 1)),
        )

    loads["av"].wait()
    send_velocity(ADJ, [av[i] for i in range(3)])

    for name in ("rec", "traces", "plan", "as_", "lam", "mu", "buoy"):
        loads[name].wait()
    cells = rec[0]
    row_of, x_of = lax.shift_right_logical(cells, 7), lax.bitwise_and(cells, 127)
    rows = lax.broadcasted_iota(jnp.int32, (64, 64), 0)
    hit = rows == jnp.broadcast_to(row_of, (64, 64))
    samples = [jnp.broadcast_to(traces[pl.ds(t_plan[k], 1), :], (64, 64)) for k in range(STEPS)]
    left = jnp.concatenate([jnp.where(hit, samples[k], 0.0) for k in range(STEPS)], axis=0)
    columns = lax.broadcasted_iota(jnp.int32, (128, 64), 0)
    right = jnp.where(columns == jnp.broadcast_to(x_of, (128, 64)), 1.0, 0.0)
    spread = lax.dot_general(
        left, right, (((1,), (1,)), ((), ())), precision=lax.Precision.HIGHEST, preferred_element_type=jnp.float32
    )
    spread = spread.reshape(STEPS, 8, 8, 128)
    for i in range(3):
        a1[i] = as_[i] + spread[1]
        a0[i] = spread[0]
    for i in range(3, 6):
        a1[i] = as_[i]

    h = receive(ADJ, VELOCITY)
    rates = stress_rates([av[i] for i in range(3)], h)
    for i in range(6):
        as_[i] = a1[i] - rates[i]
    send_stress(ADJ + 1, [as_[i] for i in range(6)])

    cross_s.wait_recv()
    relay_s.start()
    cross_v.wait_recv()
    relay_v.start()

    h = receive(ADJ + 1, STRESS)
    rates = velocity_rates([as_[i] for i in range(6)], h)
    for i in range(3):
        av[i] = av[i] - rates[i]
    send_velocity(ADJ + 2, [av[i] for i in range(3)])
    for i in range(3):
        a0[i] = a0[i] + as_[i]
    for i in range(3, 6):
        a0[i] = as_[i]

    for name in ("peer", "slot", "own_s", "own_v", "wav", "src"):
        loads[name].wait()
    pair_s.wait_recv()
    relay_s.wait_recv()
    where_is = [t_peer[gz, p] * 8 + t_slot[gz, p] for p in range(8)]
    for p in range(8):
        fs[:, p] = gath_s[where_is[p]].astype(jnp.float32)
    send_stress(FWD, [fs[i] for i in range(6)])

    h = receive(ADJ + 2, VELOCITY)
    rates = stress_rates([av[i] for i in range(3)], h)
    for i in range(6):
        as_[i] = a0[i] - rates[i]
    send_stress(ADJ + 3, [as_[i] for i in range(6)])

    pair_v.wait_recv()
    relay_v.wait_recv()
    for p in range(8):
        fv[:, p] = gath_v[where_is[p]].astype(jnp.float32)
    flat = iota3(0) * 1024 + iota3(1) * 128 + iota3(2)
    hits = jnp.zeros((8, 8, 128), jnp.float32)
    for j in range(t_src.shape[0]):
        hits = hits + jnp.where(flat == t_src[j], 1.0, 0.0)

    h = receive(FWD, STRESS)
    rates = velocity_rates([fs[i] for i in range(6)], h)
    for i in range(3):
        fv[i] = fv[i] + rates[i]
    send_velocity(FWD + 1, [fv[i] for i in range(3)])

    h = receive(ADJ + 3, STRESS)
    rates = velocity_rates([as_[i] for i in range(6)], h)
    for i in range(3):
        adj_out[i] = av[i] - rates[i]
    for i in range(6):
        adj_out[3 + i] = as_[i]

    h = receive(FWD + 1, VELOCITY)
    rates = stress_rates([fv[i] for i in range(3)], h)
    pulse = hits * t_wav[t_plan[0]]
    for i in range(3):
        fs[i] = fs[i] + rates[i] + pulse
    for i in range(3, 6):
        fs[i] = fs[i] + rates[i]
    send_stress(FWD + 2, [fs[i] for i in range(6)])

    def image(s, a):
        by_lambda = (s[0] + s[1] + s[2]) * (a[0] + a[1] + a[2])
        by_mu = s[0] * a[0] + s[1] * a[1] + s[2] * a[2] + 2.0 * (s[3] * a[3] + s[4] * a[4] + s[5] * a[5])
        return by_lambda, by_mu

    by_lambda, by_mu = image(fs, a0)
    il_out[...] = by_lambda
    im_out[...] = by_mu

    h = receive(FWD + 2, STRESS)
    rates = velocity_rates([fs[i] for i in range(6)], h)
    for i in range(3):
        fv[i] = fv[i] + rates[i]
    send_velocity(FWD + 3, [fv[i] for i in range(3)])

    h = receive(FWD + 3, VELOCITY)
    rates = stress_rates([fv[i] for i in range(3)], h)
    pulse = hits * t_wav[t_plan[1]]
    last = [fs[i] + rates[i] + pulse for i in range(3)] + [fs[i] + rates[i] for i in range(3, 6)]
    by_lambda, by_mu = image(last, a1)
    il_out[...] += by_lambda
    im_out[...] += by_mu

    for copy in (cross_s, cross_v, pair_s, pair_v, relay_s, relay_v):
        copy.wait_send()
    for r in range(8):
        counts = VELOCITY if r in (0, 2, 5, 7) else STRESS
        for d in range(6):
            copy, goes, _ = face(r, d, counts[d])

            @pl.when(goes)
            def _():
                copy.wait_send()


def solution(mesh):
    sizes = (mesh.shape["gx"], mesh.shape["gy"], mesh.shape["gz"])
    f32, i32, bf16 = jnp.float32, jnp.int32, jnp.bfloat16
    brick = (8, 8, 128)

    def on_device(*args):
        nt, nrec = args[10].shape[-2:]
        nsrc = args[7].shape[-1]
        vmem = pltpu.VMEM
        scratch = [
            vmem(brick, f32),
            vmem(brick, f32),
            vmem(brick, f32),
            vmem((1, nrec), i32),
            vmem((nt, nrec), f32),
            pltpu.SMEM((4, 8), i32),
            pltpu.SMEM((4, 8), i32),
            pltpu.SMEM((nsrc,), i32),
            pltpu.SMEM((nt,), f32),
            pltpu.SMEM((STEPS,), i32),
            vmem((32, 6, 8, 128), bf16),
            vmem((32, 3, 8, 128), bf16),
            vmem((3,) + brick, f32),
            vmem((6,) + brick, f32),
            vmem((3,) + brick, f32),
            vmem((6,) + brick, f32),
            vmem((6,) + brick, f32),
            vmem((6,) + brick, f32),
        ]
        for _ in range(2):
            scratch += [vmem((8, 8, 128), f32)] * 2 + [vmem((8, 2, 8, 1, 128), f32)] * 2 + [vmem((8, 2, 8, 128), f32)] * 2
        dma = pltpu.SemaphoreType.DMA
        scratch += [dma((14,)), dma((8, 6)), dma((8, 6)), dma((6,)), dma((6,))]
        return pl.pallas_call(
            functools.partial(kernel, sizes),
            out_shape=(
                jax.ShapeDtypeStruct((9,) + brick, f32),
                jax.ShapeDtypeStruct(brick, f32),
                jax.ShapeDtypeStruct(brick, f32),
            ),
            in_specs=[pl.BlockSpec(memory_space=pl.ANY)] * 12,
            out_specs=(pl.BlockSpec(memory_space=pltpu.VMEM),) * 3,
            scratch_shapes=scratch,
            compiler_params=pltpu.CompilerParams(collective_id=0, has_side_effects=True),
            name="window",
        )(*args)

    return jax.shard_map(
        on_device,
        mesh=mesh,
        in_specs=(
            P("gz", None, None, "gy", "gx"),
            P("gx", "gy", None, None),
            P("gx", "gy", None, None),
            P(None, "gz", "gy", "gx"),
            P("gz", "gy", "gx"),
            P("gz", "gy", "gx"),
            P("gz", "gy", "gx"),
            P("gz", "gy", "gx", None),
            P(),
            P("gz", "gy", "gx", None),
            P("gz", "gy", "gx", None, None),
            P(),
        ),
        out_specs=(P(None, "gz", "gy", "gx"), P("gz", "gy", "gx"), P("gz", "gy", "gx")),
        check_vma=False,
    )
```

```python
import functools

import jax
import jax.numpy as jnp
from jax import lax
from jax.experimental import pallas as pl
from jax.experimental.pallas import tpu as pltpu
from jax.sharding import PartitionSpec as P

MESH = pl.DeviceIdType.MESH
STEPS = 2

ADJ, FWD = 0, 4


def iota3(dim):
    return lax.broadcasted_iota(jnp.int32, (8, 8, 128), dim)


def pack_columns(fields, lane):
    lanes = lax.broadcasted_iota(jnp.int32, (8, 128), 1)
    packed = jnp.zeros((8, 128), jnp.float32)
    for number, field in enumerate(fields):
        for z in range(8):
            at = number * 8 + z
            moved = pltpu.roll(field[z], (at - lane) % 128, 1)
            packed = jnp.where(lanes == at, moved, packed)
    return packed


def unpack_columns(packed, number, lane):
    return jnp.stack([pltpu.roll(packed, (lane - number * 8 - z) % 128, 1) for z in range(8)])


class Halo:
    def __init__(self, xl, xr, yl, yr, zl, zr):
        self.xl, self.xr, self.yl, self.yr, self.zl, self.zr = xl, xr, yl, yr, zl, zr

    def behind_x(self, f, i):
        before = jnp.where(iota3(2) == 0, unpack_columns(self.xl, i, 0), pltpu.roll(f, 1, 2))
        return f - before

    def ahead_x(self, f, i):
        after = jnp.where(iota3(2) == 127, unpack_columns(self.xr, i, 127), pltpu.roll(f, 127, 2))
        return after - f

    def behind_y(self, f, i):
        face = jnp.broadcast_to(self.yl[i], (8, 8, 128))
        return f - jnp.where(iota3(1) == 0, face, pltpu.roll(f, 1, 1))

    def ahead_y(self, f, i):
        face = jnp.broadcast_to(self.yr[i], (8, 8, 128))
        return jnp.where(iota3(1) == 7, face, pltpu.roll(f, 7, 1)) - f

    def behind_z(self, f, i):
        return f - jnp.concatenate([self.zl[i][None], f[:7]], axis=0)

    def ahead_z(self, f, i):
        return jnp.concatenate([f[1:], self.zr[i][None]], axis=0) - f


def kernel(
    sizes,
    store,
    hpeer,
    hslot,
    adj_in,
    lam_in,
    mu_in,
    buoy_in,
    src_in,
    wav_in,
    rec_in,
    tr_in,
    plan_in,
    adj_out,
    il_out,
    im_out,
    lam,
    mu,
    buoy,
    rec,
    traces,
    t_peer,
    t_slot,
    t_src,
    t_wav,
    t_plan,
    gath_s,
    gath_v,
    fv,
    fs,
    av,
    as_,
    a1,
    a0,
    s_xl,
    s_xr,
    s_yl,
    s_yr,
    s_zl,
    s_zr,
    r_xl,
    r_xr,
    r_yl,
    r_yr,
    r_zl,
    r_zr,
    in_sem,
    send_sem,
    recv_sem,
    rs_send,
    rs_recv,
):
    ngx, ngy, ngz = sizes
    gx, gy, gz = lax.axis_index("gx"), lax.axis_index("gy"), lax.axis_index("gz")
    partner = gz + 1 - 2 * lax.rem(gz, 2)
    cross = lax.rem(gz + 2, 4)

    def local(src, dst, n):
        return pltpu.make_async_copy(src, dst, in_sem.at[n])

    loads = dict(
        av=local(adj_in.at[pl.ds(0, 3)], av, 0),
        as_=local(adj_in.at[pl.ds(3, 6)], as_, 1),
        lam=local(lam_in, lam, 2),
        mu=local(mu_in, mu, 3),
        buoy=local(buoy_in, buoy, 4),
        rec=local(rec_in.at[0, 0], rec, 5),
        traces=local(tr_in.at[0, 0, 0], traces, 6),
        plan=local(plan_in, t_plan, 7),
        wav=local(wav_in, t_wav, 8),
        src=local(src_in.at[0, 0, 0], t_src, 9),
        peer=local(hpeer.at[0, 0], t_peer, 10),
        slot=local(hslot.at[0, 0], t_slot, 11),
        own_s=local(store.at[:, pl.ds(3, 6), 0], gath_s.at[pl.ds(gz * 8, 8)], 12),
        own_v=local(store.at[:, pl.ds(0, 3), 0], gath_v.at[pl.ds(gz * 8, 8)], 13),
    )
    for copy in loads.values():
        copy.start()

    barrier = pltpu.get_barrier_semaphore()

    def at(**axes):
        return dict(axes)

    def greet(where):
        pl.semaphore_signal(barrier, inc=1, device_id=where, device_id_type=MESH)

    greeted = 3
    for axis, index, count in (("gx", gx, ngx), ("gy", gy, ngy)):
        for step, exists in ((-1, index > 0), (1, index < count - 1)):

            @pl.when(exists)
            def _():
                greet({axis: index + step})

            greeted = greeted + exists.astype(jnp.int32)
    for d in (1, 2, 3):
        greet({"gz": lax.rem(gz + d, 4)})

    for exists, ref in (
        (gx > 0, r_xl),
        (gx < ngx - 1, r_xr),
        (gy > 0, r_yl),
        (gy < ngy - 1, r_yr),
        (gz > 0, r_zl),
        (gz < ngz - 1, r_zr),
    ):

        @pl.when(jnp.logical_not(exists))
        def _():
            ref[...] = jnp.zeros(ref.shape, jnp.float32)

    pl.semaphore_wait(barrier, greeted)

    def remote(src, dst, n, where):
        return pltpu.make_async_remote_copy(
            src_ref=src,
            dst_ref=dst,
            send_sem=rs_send.at[n],
            recv_sem=rs_recv.at[n],
            device_id={"gz": where},
            device_id_type=MESH,
        )

    mine, theirs = pl.ds(gz * 8, 8), pl.ds(cross * 8, 8)
    st_s, st_v = store.at[:, pl.ds(3, 6), 0], store.at[:, pl.ds(0, 3), 0]
    cross_s = remote(st_s, gath_s.at[mine], 0, cross)
    cross_v = remote(st_v, gath_v.at[mine], 1, cross)
    pair_s = remote(st_s, gath_s.at[mine], 2, partner)
    pair_v = remote(st_v, gath_v.at[mine], 3, partner)
    relay_s = remote(gath_s.at[theirs], gath_s.at[theirs], 4, partner)
    relay_v = remote(gath_v.at[theirs], gath_v.at[theirs], 5, partner)
    cross_s.start()
    cross_v.start()
    pair_s.start()
    pair_v.start()

    ends = (
        ("gx", gx, 1, ngx, s_xr, r_xl),
        ("gx", gx, -1, ngx, s_xl, r_xr),
        ("gy", gy, 1, ngy, s_yr, r_yl),
        ("gy", gy, -1, ngy, s_yl, r_yr),
        ("gz", gz, 1, ngz, s_zr, r_zl),
        ("gz", gz, -1, ngz, s_zl, r_zr),
    )

    def face(r, d, fields):
        axis, index, step, count, source, target = ends[d]
        if axis == "gx":
            src, dst = source.at[r], target.at[r]
        else:
            src, dst = source.at[r, pl.ds(0, fields)], target.at[r, pl.ds(0, fields)]
        copy = pltpu.make_async_remote_copy(
            src_ref=src,
            dst_ref=dst,
            send_sem=send_sem.at[r, d],
            recv_sem=recv_sem.at[r, d],
            device_id={axis: index + step},
            device_id_type=MESH,
        )
        goes = index < count - 1 if step > 0 else index > 0
        comes = index > 0 if step > 0 else index < count - 1
        return copy, goes, comes

    STRESS, VELOCITY = (2, 1, 2, 1, 2, 1), (1, 2, 1, 2, 1, 2)

    def send_faces(r, up, down, counts):
        (xu, yu, zu), (xd, yd, zd) = up, down
        for i, f in enumerate(zu):
            s_zr[r, i] = f[7]
        for i, f in enumerate(zd):
            s_zl[r, i] = f[0]
        for d in (4, 5):
            start(r, d, counts)
        for i, f in enumerate(yu):
            s_yr[r, i] = f[:, 7:8, :]
        for i, f in enumerate(yd):
            s_yl[r, i] = f[:, 0:1, :]
        for d in (2, 3):
            start(r, d, counts)
        s_xr[r] = pack_columns(xu, 127)
        s_xl[r] = pack_columns(xd, 0)
        for d in (0, 1):
            start(r, d, counts)

    def start(r, d, counts):
        copy, goes, _ = face(r, d, counts[d])

        @pl.when(goes)
        def _():
            copy.start()

    def send_stress(r, s):
        send_faces(r, ((s[3], s[4]), (s[3], s[5]), (s[4], s[5])), ((s[0],), (s[1],), (s[2],)), STRESS)

    def send_velocity(r, v):
        send_faces(r, ((v[0],), (v[1],), (v[2],)), ((v[1], v[2]), (v[0], v[2]), (v[0], v[1])), VELOCITY)

    def receive(r, counts):
        for d in range(6):
            copy, _, comes = face(r, d, counts[d])

            @pl.when(comes)
            def _():
                copy.wait_recv()

        return Halo(r_xl[r], r_xr[r], r_yl[r], r_yr[r], r_zl[r], r_zr[r])

    def velocity_rates(s, h):
        b = buoy[...]
        rx = b * (h.ahead_x(s[0], 0) + h.behind_y(s[3], 0) + h.behind_z(s[4], 0))
        ry = b * (h.behind_x(s[3], 0) + h.ahead_y(s[1], 0) + h.behind_z(s[5], 1))
        rz = b * (h.behind_x(s[4], 1) + h.behind_y(s[5], 1) + h.ahead_z(s[2], 0))
        return rx, ry, rz

    def stress_rates(v, h):
        exx, eyy, ezz = h.behind_x(v[0], 0), h.behind_y(v[1], 0), h.behind_z(v[2], 0)
        m = mu[...]
        spread = lam[...] * (exx + eyy + ezz)
        twice = 2.0 * m
        return (
            spread + twice * exx,
            spread + twice * eyy,
            spread + twice * ezz,
            m * (h.ahead_y(v[0], 0) + h.ahead_x(v[1], 0)),
            m * (h.ahead_z(v[0], 0) + h.ahead_x(v[2], 1)),
            m * (h.ahead_z(v[1], 1) + h.ahead_y(v[2], 1)),
        )

    loads["av"].wait()
    send_velocity(ADJ, [av[i] for i in range(3)])

    for name in ("rec", "traces", "plan", "as_", "lam", "mu", "buoy"):
        loads[name].wait()
    cells = rec[0]
    row_of, x_of = lax.shift_right_logical(cells, 7), lax.bitwise_and(cells, 127)
    rows = lax.broadcasted_iota(jnp.int32, (64, 64), 0)
    hit = rows == jnp.broadcast_to(row_of, (64, 64))
    samples = [jnp.broadcast_to(traces[pl.ds(t_plan[k], 1), :], (64, 64)) for k in range(STEPS)]
    left = jnp.concatenate([jnp.where(hit, samples[k], 0.0) for k in range(STEPS)], axis=0)
    columns = lax.broadcasted_iota(jnp.int32, (128, 64), 0)
    right = jnp.where(columns == jnp.broadcast_to(x_of, (128, 64)), 1.0, 0.0)
    spread = lax.dot_general(
        left, right, (((1,), (1,)), ((), ())), precision=lax.Precision.HIGHEST, preferred_element_type=jnp.float32
    )
    spread = spread.reshape(STEPS, 8, 8, 128)
    for i in range(3):
        a1[i] = as_[i] + spread[1]
        a0[i] = spread[0]
    for i in range(3, 6):
        a1[i] = as_[i]

    h = receive(ADJ, VELOCITY)
    rates = stress_rates([av[i] for i in range(3)], h)
    for i in range(6):
        as_[i] = a1[i] - rates[i]
    send_stress(ADJ + 1, [as_[i] for i in range(6)])

    cross_s.wait_recv()
    relay_s.start()
    cross_v.wait_recv()
    relay_v.start()

    for name in ("peer", "slot", "own_s", "own_v", "wav", "src"):
        loads[name].wait()
    pair_s.wait_recv()
    relay_s.wait_recv()
    where_is = [t_peer[gz, p] * 8 + t_slot[gz, p] for p in range(8)]
    for p in range(8):
        fs[:, p] = gath_s[where_is[p]].astype(jnp.float32)
    send_stress(FWD, [fs[i] for i in range(6)])

    h = receive(ADJ + 1, STRESS)
    rates = velocity_rates([as_[i] for i in range(6)], h)
    for i in range(3):
        av[i] = av[i] - rates[i]
    send_velocity(ADJ + 2, [av[i] for i in range(3)])
    for i in range(3):
        a0[i] = a0[i] + as_[i]
    for i in range(3, 6):
        a0[i] = as_[i]

    pair_v.wait_recv()
    relay_v.wait_recv()
    for p in range(8):
        fv[:, p] = gath_v[where_is[p]].astype(jnp.float32)
    flat = iota3(0) * 1024 + iota3(1) * 128 + iota3(2)
    hits = jnp.zeros((8, 8, 128), jnp.float32)
    for j in range(t_src.shape[0]):
        hits = hits + jnp.where(flat == t_src[j], 1.0, 0.0)

    h = receive(FWD, STRESS)
    rates = velocity_rates([fs[i] for i in range(6)], h)
    for i in range(3):
        fv[i] = fv[i] + rates[i]
    send_velocity(FWD + 1, [fv[i] for i in range(3)])

    h = receive(ADJ + 2, VELOCITY)
    rates = stress_rates([av[i] for i in range(3)], h)
    for i in range(6):
        as_[i] = a0[i] - rates[i]
    send_stress(ADJ + 3, [as_[i] for i in range(6)])

    h = receive(FWD + 1, VELOCITY)
    rates = stress_rates([fv[i] for i in range(3)], h)
    pulse = hits * t_wav[t_plan[0]]
    for i in range(3):
        fs[i] = fs[i] + rates[i] + pulse
    for i in range(3, 6):
        fs[i] = fs[i] + rates[i]
    send_stress(FWD + 2, [fs[i] for i in range(6)])

    h = receive(ADJ + 3, STRESS)
    rates = velocity_rates([as_[i] for i in range(6)], h)
    for i in range(3):
        adj_out[i] = av[i] - rates[i]
    for i in range(6):
        adj_out[3 + i] = as_[i]

    def image(s, a):
        by_lambda = (s[0] + s[1] + s[2]) * (a[0] + a[1] + a[2])
        by_mu = s[0] * a[0] + s[1] * a[1] + s[2] * a[2] + 2.0 * (s[3] * a[3] + s[4] * a[4] + s[5] * a[5])
        return by_lambda, by_mu

    by_lambda, by_mu = image(fs, a0)
    il_out[...] = by_lambda
    im_out[...] = by_mu

    h = receive(FWD + 2, STRESS)
    rates = velocity_rates([fs[i] for i in range(6)], h)
    for i in range(3):
        fv[i] = fv[i] + rates[i]
    send_velocity(FWD + 3, [fv[i] for i in range(3)])

    h = receive(FWD + 3, VELOCITY)
    rates = stress_rates([fv[i] for i in range(3)], h)
    pulse = hits * t_wav[t_plan[1]]
    last = [fs[i] + rates[i] + pulse for i in range(3)] + [fs[i] + rates[i] for i in range(3, 6)]
    by_lambda, by_mu = image(last, a1)
    il_out[...] += by_lambda
    im_out[...] += by_mu

    for copy in (cross_s, cross_v, pair_s, pair_v, relay_s, relay_v):
        copy.wait_send()
    for r in range(8):
        counts = VELOCITY if r in (0, 2, 5, 7) else STRESS
        for d in range(6):
            copy, goes, _ = face(r, d, counts[d])

            @pl.when(goes)
            def _():
                copy.wait_send()


def write_out(adj, il, im, adj_out, il_out, im_out, sem):
    copies = [
        pltpu.make_async_copy(src, dst, sem.at[n])
        for n, (src, dst) in enumerate(((adj, adj_out), (il, il_out), (im, im_out)))
    ]
    for copy in copies:
        copy.start()
    for copy in copies:
        copy.wait()


def solution(mesh):
    sizes = (mesh.shape["gx"], mesh.shape["gy"], mesh.shape["gz"])
    f32, i32, bf16 = jnp.float32, jnp.int32, jnp.bfloat16
    brick = (8, 8, 128)

    def on_device(*args):
        nt, nrec = args[10].shape[-2:]
        nsrc = args[7].shape[-1]
        vmem = pltpu.VMEM
        scratch = [
            vmem(brick, f32),
            vmem(brick, f32),
            vmem(brick, f32),
            vmem((1, nrec), i32),
            vmem((nt, nrec), f32),
            pltpu.SMEM((4, 8), i32),
            pltpu.SMEM((4, 8), i32),
            pltpu.SMEM((nsrc,), i32),
            pltpu.SMEM((nt,), f32),
            pltpu.SMEM((STEPS,), i32),
            vmem((32, 6, 8, 128), bf16),
            vmem((32, 3, 8, 128), bf16),
            vmem((3,) + brick, f32),
            vmem((6,) + brick, f32),
            vmem((3,) + brick, f32),
            vmem((6,) + brick, f32),
            vmem((6,) + brick, f32),
            vmem((6,) + brick, f32),
        ]
        for _ in range(2):
            scratch += [vmem((8, 8, 128), f32)] * 2 + [vmem((8, 2, 8, 1, 128), f32)] * 2 + [vmem((8, 2, 8, 128), f32)] * 2
        dma = pltpu.SemaphoreType.DMA
        scratch += [dma((14,)), dma((8, 6)), dma((8, 6)), dma((6,)), dma((6,))]
        shapes = ((9,) + brick, brick, brick)
        results = pl.pallas_call(
            functools.partial(kernel, sizes),
            out_shape=tuple(pltpu.VMEM(shape, f32) for shape in shapes),
            in_specs=[pl.BlockSpec(memory_space=pl.ANY)] * 12,
            out_specs=(pl.BlockSpec(memory_space=pltpu.VMEM),) * 3,
            scratch_shapes=scratch,
            compiler_params=pltpu.CompilerParams(
                collective_id=0, has_side_effects=True, vmem_limit_bytes=16 << 20
            ),
            name="window",
        )(*args)
        return pl.pallas_call(
            write_out,
            out_shape=tuple(jax.ShapeDtypeStruct(shape, f32) for shape in shapes),
            in_specs=[pl.BlockSpec(memory_space=pltpu.VMEM)] * 3,
            out_specs=(pl.BlockSpec(memory_space=pl.ANY),) * 3,
            scratch_shapes=[pltpu.SemaphoreType.DMA((3,))],
            compiler_params=pltpu.CompilerParams(vmem_limit_bytes=16 << 20),
            name="write_out",
        )(*results)

    return jax.shard_map(
        on_device,
        mesh=mesh,
        in_specs=(
            P("gz", None, None, "gy", "gx"),
            P("gx", "gy", None, None),
            P("gx", "gy", None, None),
            P(None, "gz", "gy", "gx"),
            P("gz", "gy", "gx"),
            P("gz", "gy", "gx"),
            P("gz", "gy", "gx"),
            P("gz", "gy", "gx", None),
            P(),
            P("gz", "gy", "gx", None),
            P("gz", "gy", "gx", None, None),
            P(),
        ),
        out_specs=(P(None, "gz", "gy", "gx"), P("gz", "gy", "gx"), P("gz", "gy", "gx")),
        check_vma=False,
    )
```

```python
import functools

import jax
import jax.numpy as jnp
from jax import lax
from jax.experimental import pallas as pl
from jax.experimental.pallas import tpu as pltpu
from jax.sharding import PartitionSpec as P

MESH = pl.DeviceIdType.MESH
STEPS = 2

ADJ, FWD = 0, 4


def iota3(dim):
    return lax.broadcasted_iota(jnp.int32, (8, 8, 128), dim)


def pack_columns(fields, lane):
    lanes = lax.broadcasted_iota(jnp.int32, (8, 128), 1)
    packed = jnp.zeros((8, 128), jnp.float32)
    for number, field in enumerate(fields):
        for z in range(8):
            at = number * 8 + z
            moved = pltpu.roll(field[z], (at - lane) % 128, 1)
            packed = jnp.where(lanes == at, moved, packed)
    return packed


def unpack_columns(packed, number, lane):
    return jnp.stack([pltpu.roll(packed, (lane - number * 8 - z) % 128, 1) for z in range(8)])


class Halo:
    def __init__(self, xl, xr, yl, yr, zl, zr):
        self.xl, self.xr, self.yl, self.yr, self.zl, self.zr = xl, xr, yl, yr, zl, zr

    def behind_x(self, f, i):
        before = jnp.where(iota3(2) == 0, unpack_columns(self.xl, i, 0), pltpu.roll(f, 1, 2))
        return f - before

    def ahead_x(self, f, i):
        after = jnp.where(iota3(2) == 127, unpack_columns(self.xr, i, 127), pltpu.roll(f, 127, 2))
        return after - f

    def behind_y(self, f, i):
        face = jnp.broadcast_to(self.yl[i], (8, 8, 128))
        return f - jnp.where(iota3(1) == 0, face, pltpu.roll(f, 1, 1))

    def ahead_y(self, f, i):
        face = jnp.broadcast_to(self.yr[i], (8, 8, 128))
        return jnp.where(iota3(1) == 7, face, pltpu.roll(f, 7, 1)) - f

    def behind_z(self, f, i):
        return f - jnp.concatenate([self.zl[i][None], f[:7]], axis=0)

    def ahead_z(self, f, i):
        return jnp.concatenate([f[1:], self.zr[i][None]], axis=0) - f


def kernel(
    sizes,
    store,
    hpeer,
    hslot,
    adj_in,
    lam_in,
    mu_in,
    buoy_in,
    src_in,
    wav_in,
    rec_in,
    tr_in,
    plan_in,
    adj_out,
    il_out,
    im_out,
    lam,
    mu,
    buoy,
    rec,
    traces,
    t_peer,
    t_slot,
    t_src,
    t_wav,
    t_plan,
    gath_s,
    gath_v,
    fv,
    fs,
    av,
    as_,
    a1,
    a0,
    s_xl,
    s_xr,
    s_yl,
    s_yr,
    s_zl,
    s_zr,
    r_xl,
    r_xr,
    r_yl,
    r_yr,
    r_zl,
    r_zr,
    in_sem,
    send_sem,
    recv_sem,
    rs_send,
    rs_recv,
):
    ngx, ngy, ngz = sizes
    gx, gy, gz = lax.axis_index("gx"), lax.axis_index("gy"), lax.axis_index("gz")
    partner = gz + 1 - 2 * lax.rem(gz, 2)
    cross = lax.rem(gz + 2, 4)

    barrier = pltpu.get_barrier_semaphore()

    def greet(where):
        pl.semaphore_signal(barrier, inc=1, device_id=where, device_id_type=MESH)

    greeted = 3
    for axis, index, count in (("gx", gx, ngx), ("gy", gy, ngy)):
        for step, exists in ((-1, index > 0), (1, index < count - 1)):

            @pl.when(exists)
            def _():
                greet({axis: index + step})

            greeted = greeted + exists.astype(jnp.int32)
    for d in (1, 2, 3):
        greet({"gz": lax.rem(gz + d, 4)})

    def local(src, dst, n):
        return pltpu.make_async_copy(src, dst, in_sem.at[n])

    loads = dict(
        av=local(adj_in.at[pl.ds(0, 3)], av, 0),
        as_=local(adj_in.at[pl.ds(3, 6)], as_, 1),
        lam=local(lam_in, lam, 2),
        mu=local(mu_in, mu, 3),
        buoy=local(buoy_in, buoy, 4),
        rec=local(rec_in.at[0, 0], rec, 5),
        traces=local(tr_in.at[0, 0, 0], traces, 6),
        plan=local(plan_in, t_plan, 7),
        wav=local(wav_in, t_wav, 8),
        src=local(src_in.at[0, 0, 0], t_src, 9),
        peer=local(hpeer.at[0, 0], t_peer, 10),
        slot=local(hslot.at[0, 0], t_slot, 11),
        own_s=local(store.at[:, pl.ds(3, 6), 0], gath_s.at[pl.ds(gz * 8, 8)], 12),
        own_v=local(store.at[:, pl.ds(0, 3), 0], gath_v.at[pl.ds(gz * 8, 8)], 13),
    )
    for copy in loads.values():
        copy.start()

    for exists, ref in (
        (gx > 0, r_xl),
        (gx < ngx - 1, r_xr),
        (gy > 0, r_yl),
        (gy < ngy - 1, r_yr),
        (gz > 0, r_zl),
        (gz < ngz - 1, r_zr),
    ):

        @pl.when(jnp.logical_not(exists))
        def _():
            ref[...] = jnp.zeros(ref.shape, jnp.float32)

    pl.semaphore_wait(barrier, greeted)

    def remote(src, dst, n, where):
        return pltpu.make_async_remote_copy(
            src_ref=src,
            dst_ref=dst,
            send_sem=rs_send.at[n],
            recv_sem=rs_recv.at[n],
            device_id={"gz": where},
            device_id_type=MESH,
        )

    mine, theirs = pl.ds(gz * 8, 8), pl.ds(cross * 8, 8)
    st_s, st_v = store.at[:, pl.ds(3, 6), 0], store.at[:, pl.ds(0, 3), 0]
    cross_s = remote(st_s, gath_s.at[mine], 0, cross)
    cross_v = remote(st_v, gath_v.at[mine], 1, cross)
    pair_s = remote(st_s, gath_s.at[mine], 2, partner)
    pair_v = remote(st_v, gath_v.at[mine], 3, partner)
    relay_s = remote(gath_s.at[theirs], gath_s.at[theirs], 4, partner)
    relay_v = remote(gath_v.at[theirs], gath_v.at[theirs], 5, partner)
    cross_s.start()
    cross_v.start()
    pair_s.start()
    pair_v.start()

    ends = (
        ("gx", gx, 1, ngx, s_xr, r_xl),
        ("gx", gx, -1, ngx, s_xl, r_xr),
        ("gy", gy, 1, ngy, s_yr, r_yl),
        ("gy", gy, -1, ngy, s_yl, r_yr),
        ("gz", gz, 1, ngz, s_zr, r_zl),
        ("gz", gz, -1, ngz, s_zl, r_zr),
    )

    def face(r, d, fields):
        axis, index, step, count, source, target = ends[d]
        if axis == "gx":
            src, dst = source.at[r], target.at[r]
        else:
            src, dst = source.at[r, pl.ds(0, fields)], target.at[r, pl.ds(0, fields)]
        copy = pltpu.make_async_remote_copy(
            src_ref=src,
            dst_ref=dst,
            send_sem=send_sem.at[r, d],
            recv_sem=recv_sem.at[r, d],
            device_id={axis: index + step},
            device_id_type=MESH,
        )
        goes = index < count - 1 if step > 0 else index > 0
        comes = index > 0 if step > 0 else index < count - 1
        return copy, goes, comes

    STRESS, VELOCITY = (2, 1, 2, 1, 2, 1), (1, 2, 1, 2, 1, 2)

    def send_faces(r, up, down, counts):
        (xu, yu, zu), (xd, yd, zd) = up, down
        for i, f in enumerate(zu):
            s_zr[r, i] = f[7]
        for i, f in enumerate(zd):
            s_zl[r, i] = f[0]
        for d in (4, 5):
            start(r, d, counts)
        for i, f in enumerate(yu):
            s_yr[r, i] = f[:, 7:8, :]
        for i, f in enumerate(yd):
            s_yl[r, i] = f[:, 0:1, :]
        for d in (2, 3):
            start(r, d, counts)
        s_xr[r] = pack_columns(xu, 127)
        s_xl[r] = pack_columns(xd, 0)
        for d in (0, 1):
            start(r, d, counts)

    def start(r, d, counts):
        copy, goes, _ = face(r, d, counts[d])

        @pl.when(goes)
        def _():
            copy.start()

    def send_stress(r, s):
        send_faces(r, ((s[3], s[4]), (s[3], s[5]), (s[4], s[5])), ((s[0],), (s[1],), (s[2],)), STRESS)

    def send_velocity(r, v):
        send_faces(r, ((v[0],), (v[1],), (v[2],)), ((v[1], v[2]), (v[0], v[2]), (v[0], v[1])), VELOCITY)

    def receive(r, counts):
        for d in range(6):
            copy, _, comes = face(r, d, counts[d])

            @pl.when(comes)
            def _():
                copy.wait_recv()

        return Halo(r_xl[r], r_xr[r], r_yl[r], r_yr[r], r_zl[r], r_zr[r])

    def velocity_rates(s, h):
        b = buoy[...]
        rx = b * (h.ahead_x(s[0], 0) + h.behind_y(s[3], 0) + h.behind_z(s[4], 0))
        ry = b * (h.behind_x(s[3], 0) + h.ahead_y(s[1], 0) + h.behind_z(s[5], 1))
        rz = b * (h.behind_x(s[4], 1) + h.behind_y(s[5], 1) + h.ahead_z(s[2], 0))
        return rx, ry, rz

    def stress_rates(v, h):
        exx, eyy, ezz = h.behind_x(v[0], 0), h.behind_y(v[1], 0), h.behind_z(v[2], 0)
        m = mu[...]
        spread = lam[...] * (exx + eyy + ezz)
        twice = 2.0 * m
        return (
            spread + twice * exx,
            spread + twice * eyy,
            spread + twice * ezz,
            m * (h.ahead_y(v[0], 0) + h.ahead_x(v[1], 0)),
            m * (h.ahead_z(v[0], 0) + h.ahead_x(v[2], 1)),
            m * (h.ahead_z(v[1], 1) + h.ahead_y(v[2], 1)),
        )

    loads["av"].wait()
    send_velocity(ADJ, [av[i] for i in range(3)])

    for name in ("rec", "traces", "plan", "as_", "lam", "mu", "buoy"):
        loads[name].wait()
    cells = rec[0]
    row_of, x_of = lax.shift_right_logical(cells, 7), lax.bitwise_and(cells, 127)
    rows = lax.broadcasted_iota(jnp.int32, (64, 64), 0)
    hit = rows == jnp.broadcast_to(row_of, (64, 64))
    samples = [jnp.broadcast_to(traces[pl.ds(t_plan[k], 1), :], (64, 64)) for k in range(STEPS)]
    left = jnp.concatenate([jnp.where(hit, samples[k], 0.0) for k in range(STEPS)], axis=0)
    columns = lax.broadcasted_iota(jnp.int32, (128, 64), 0)
    right = jnp.where(columns == jnp.broadcast_to(x_of, (128, 64)), 1.0, 0.0)
    spread = lax.dot_general(
        left, right, (((1,), (1,)), ((), ())), precision=lax.Precision.HIGHEST, preferred_element_type=jnp.float32
    )
    spread = spread.reshape(STEPS, 8, 8, 128)
    for i in range(3):
        a1[i] = as_[i] + spread[1]
        a0[i] = spread[0]
    for i in range(3, 6):
        a1[i] = as_[i]

    h = receive(ADJ, VELOCITY)
    rates = stress_rates([av[i] for i in range(3)], h)
    for i in range(6):
        as_[i] = a1[i] - rates[i]
    send_stress(ADJ + 1, [as_[i] for i in range(6)])

    cross_s.wait_recv()
    relay_s.start()
    cross_v.wait_recv()
    relay_v.start()

    for name in ("peer", "slot", "own_s", "own_v", "wav", "src"):
        loads[name].wait()
    pair_s.wait_recv()
    relay_s.wait_recv()
    where_is = [t_peer[gz, p] * 8 + t_slot[gz, p] for p in range(8)]
    for p in range(8):
        fs[:, p] = gath_s[where_is[p]].astype(jnp.float32)
    send_stress(FWD, [fs[i] for i in range(6)])

    h = receive(ADJ + 1, STRESS)
    rates = velocity_rates([as_[i] for i in range(6)], h)
    for i in range(3):
        av[i] = av[i] - rates[i]
    send_velocity(ADJ + 2, [av[i] for i in range(3)])
    for i in range(3):
        a0[i] = a0[i] + as_[i]
    for i in range(3, 6):
        a0[i] = as_[i]

    pair_v.wait_recv()
    relay_v.wait_recv()
    for p in range(8):
        fv[:, p] = gath_v[where_is[p]].astype(jnp.float32)
    flat = iota3(0) * 1024 + iota3(1) * 128 + iota3(2)
    hits = jnp.zeros((8, 8, 128), jnp.float32)
    for j in range(t_src.shape[0]):
        hits = hits + jnp.where(flat == t_src[j], 1.0, 0.0)

    h = receive(FWD, STRESS)
    rates = velocity_rates([fs[i] for i in range(6)], h)
    for i in range(3):
        fv[i] = fv[i] + rates[i]
    send_velocity(FWD + 1, [fv[i] for i in range(3)])

    h = receive(ADJ + 2, VELOCITY)
    rates = stress_rates([av[i] for i in range(3)], h)
    for i in range(6):
        as_[i] = a0[i] - rates[i]
    send_stress(ADJ + 3, [as_[i] for i in range(6)])

    h = receive(FWD + 1, VELOCITY)
    rates = stress_rates([fv[i] for i in range(3)], h)
    pulse = hits * t_wav[t_plan[0]]
    for i in range(3):
        fs[i] = fs[i] + rates[i] + pulse
    for i in range(3, 6):
        fs[i] = fs[i] + rates[i]
    send_stress(FWD + 2, [fs[i] for i in range(6)])

    h = receive(ADJ + 3, STRESS)
    rates = velocity_rates([as_[i] for i in range(6)], h)
    for i in range(3):
        adj_out[i] = av[i] - rates[i]
    for i in range(6):
        adj_out[3 + i] = as_[i]

    def image(s, a):
        by_lambda = (s[0] + s[1] + s[2]) * (a[0] + a[1] + a[2])
        by_mu = s[0] * a[0] + s[1] * a[1] + s[2] * a[2] + 2.0 * (s[3] * a[3] + s[4] * a[4] + s[5] * a[5])
        return by_lambda, by_mu

    by_lambda, by_mu = image(fs, a0)
    il_out[...] = by_lambda
    im_out[...] = by_mu

    h = receive(FWD + 2, STRESS)
    rates = velocity_rates([fs[i] for i in range(6)], h)
    for i in range(3):
        fv[i] = fv[i] + rates[i]
    send_velocity(FWD + 3, [fv[i] for i in range(3)])

    h = receive(FWD + 3, VELOCITY)
    rates = stress_rates([fv[i] for i in range(3)], h)
    pulse = hits * t_wav[t_plan[1]]
    last = [fs[i] + rates[i] + pulse for i in range(3)] + [fs[i] + rates[i] for i in range(3, 6)]
    by_lambda, by_mu = image(last, a1)
    il_out[...] += by_lambda
    im_out[...] += by_mu

    for copy in (cross_s, cross_v, pair_s, pair_v, relay_s, relay_v):
        copy.wait_send()
    for r in range(8):
        counts = VELOCITY if r in (0, 2, 5, 7) else STRESS
        for d in range(6):
            copy, goes, _ = face(r, d, counts[d])

            @pl.when(goes)
            def _():
                copy.wait_send()


def write_out(adj, il, im, adj_out, il_out, im_out, sem):
    copies = [
        pltpu.make_async_copy(src, dst, sem.at[n])
        for n, (src, dst) in enumerate(((adj, adj_out), (il, il_out), (im, im_out)))
    ]
    for copy in copies:
        copy.start()
    for copy in copies:
        copy.wait()


def solution(mesh):
    sizes = (mesh.shape["gx"], mesh.shape["gy"], mesh.shape["gz"])
    f32, i32, bf16 = jnp.float32, jnp.int32, jnp.bfloat16
    brick = (8, 8, 128)

    def on_device(*args):
        nt, nrec = args[10].shape[-2:]
        nsrc = args[7].shape[-1]
        vmem = pltpu.VMEM
        scratch = [
            vmem(brick, f32),
            vmem(brick, f32),
            vmem(brick, f32),
            vmem((1, nrec), i32),
            vmem((nt, nrec), f32),
            pltpu.SMEM((4, 8), i32),
            pltpu.SMEM((4, 8), i32),
            pltpu.SMEM((nsrc,), i32),
            pltpu.SMEM((nt,), f32),
            pltpu.SMEM((STEPS,), i32),
            vmem((32, 6, 8, 128), bf16),
            vmem((32, 3, 8, 128), bf16),
            vmem((3,) + brick, f32),
            vmem((6,) + brick, f32),
            vmem((3,) + brick, f32),
            vmem((6,) + brick, f32),
            vmem((6,) + brick, f32),
            vmem((6,) + brick, f32),
        ]
        for _ in range(2):
            scratch += [vmem((8, 8, 128), f32)] * 2 + [vmem((8, 2, 8, 1, 128), f32)] * 2 + [vmem((8, 2, 8, 128), f32)] * 2
        dma = pltpu.SemaphoreType.DMA
        scratch += [dma((14,)), dma((8, 6)), dma((8, 6)), dma((6,)), dma((6,))]
        shapes = ((9,) + brick, brick, brick)
        results = pl.pallas_call(
            functools.partial(kernel, sizes),
            out_shape=tuple(pltpu.VMEM(shape, f32) for shape in shapes),
            in_specs=[pl.BlockSpec(memory_space=pl.ANY)] * 12,
            out_specs=(pl.BlockSpec(memory_space=pltpu.VMEM),) * 3,
            scratch_shapes=scratch,
            compiler_params=pltpu.CompilerParams(
                collective_id=0, has_side_effects=True
            ),
            name="window",
        )(*args)
        return pl.pallas_call(
            write_out,
            out_shape=tuple(jax.ShapeDtypeStruct(shape, f32) for shape in shapes),
            in_specs=[pl.BlockSpec(memory_space=pltpu.VMEM)] * 3,
            out_specs=(pl.BlockSpec(memory_space=pl.ANY),) * 3,
            scratch_shapes=[pltpu.SemaphoreType.DMA((3,))],
            compiler_params=pltpu.CompilerParams(vmem_limit_bytes=16 << 20),
            name="write_out",
        )(*results)

    return jax.shard_map(
        on_device,
        mesh=mesh,
        in_specs=(
            P("gz", None, None, "gy", "gx"),
            P("gx", "gy", None, None),
            P("gx", "gy", None, None),
            P(None, "gz", "gy", "gx"),
            P("gz", "gy", "gx"),
            P("gz", "gy", "gx"),
            P("gz", "gy", "gx"),
            P("gz", "gy", "gx", None),
            P(),
            P("gz", "gy", "gx", None),
            P("gz", "gy", "gx", None, None),
            P(),
        ),
        out_specs=(P(None, "gz", "gy", "gx"), P("gz", "gy", "gx"), P("gz", "gy", "gx")),
        check_vma=False,
    )
```

```python
import functools

import jax
import jax.numpy as jnp
from jax import lax
from jax.experimental import pallas as pl
from jax.experimental.pallas import tpu as pltpu
from jax.sharding import PartitionSpec as P

MESH = pl.DeviceIdType.MESH
STEPS = 2

GREETED = ((1, 0, 0), (-1, 0, 0), (0, 1, 0), (0, -1, 0))


def iota3(dim):
    return lax.broadcasted_iota(jnp.int32, (8, 8, 128), dim)


def iota2(dim):
    return lax.broadcasted_iota(jnp.int32, (8, 128), dim)


def pack_columns(fields, lane):
    lanes = iota2(1)
    packed = jnp.zeros((8, 128), jnp.float32)
    for number, field in enumerate(fields):
        for z in range(8):
            at = number * 8 + z
            moved = pltpu.roll(field[z], (at - lane) % 128, 1)
            packed = jnp.where(lanes == at, moved, packed)
    return packed


def unpack_columns(packed, number, lane):
    return jnp.stack([pltpu.roll(packed, (lane - number * 8 - z) % 128, 1) for z in range(8)])


def behind_x(f, face):
    return f - jnp.where(iota3(2) == 0, face, pltpu.roll(f, 1, 2))


def ahead_x(f, face):
    return jnp.where(iota3(2) == 127, face, pltpu.roll(f, 127, 2)) - f


def behind_y(f, face):
    return f - jnp.where(iota3(1) == 0, jnp.broadcast_to(face, (8, 8, 128)), pltpu.roll(f, 1, 1))


def ahead_y(f, face):
    return jnp.where(iota3(1) == 7, jnp.broadcast_to(face, (8, 8, 128)), pltpu.roll(f, 7, 1)) - f


def behind_z(f, face):
    return f - jnp.concatenate([face[None], f[:7]], axis=0)


def ahead_z(f, face):
    return jnp.concatenate([f[1:], face[None]], axis=0) - f


def velocity_rates(s, b, h):
    rx = b * (ahead_x(s[0], h["xr", 0]) + behind_y(s[3], h["yl", 3]) + behind_z(s[4], h["zl", 4]))
    ry = b * (behind_x(s[3], h["xl", 3]) + ahead_y(s[1], h["yr", 1]) + behind_z(s[5], h["zl", 5]))
    rz = b * (behind_x(s[4], h["xl", 4]) + behind_y(s[5], h["yl", 5]) + ahead_z(s[2], h["zr", 2]))
    return rx, ry, rz


def stress_rates(v, lam, mu, h):
    exx, eyy, ezz = behind_x(v[0], h["xl", 0]), behind_y(v[1], h["yl", 1]), behind_z(v[2], h["zl", 2])
    spread = lam * (exx + eyy + ezz)
    twice = 2.0 * mu
    return (
        spread + twice * exx,
        spread + twice * eyy,
        spread + twice * ezz,
        mu * (ahead_y(v[0], h["yr", 0]) + ahead_x(v[1], h["xr", 1])),
        mu * (ahead_z(v[0], h["zr", 0]) + ahead_x(v[2], h["xr", 2])),
        mu * (ahead_z(v[1], h["zr", 1]) + ahead_y(v[2], h["yr", 2])),
    )


class Zeros:
    def __getitem__(self, key):
        side = key[0]
        shape = (8, 1, 128) if side[0] == "y" else (8, 128)
        return jnp.zeros((8, 8, 128) if side[0] == "x" else shape, jnp.float32)


def kernel(
    sizes,
    store,
    hpeer,
    hslot,
    adj_in,
    lam_in,
    mu_in,
    buoy_in,
    src_in,
    wav_in,
    rec_in,
    tr_in,
    plan_in,
    adj_out,
    il_out,
    im_out,
    params,
    rec,
    traces,
    t_peer,
    t_slot,
    t_src,
    t_wav,
    t_plan,
    gath_s,
    gath_v,
    fv,
    fs,
    adj,
    a1,
    a0,
    bx,
    hits,
    s_xl,
    s_xr,
    s_yl,
    s_yr,
    s_zl,
    s_zr,
    r_xl,
    r_xr,
    r_yl,
    r_yr,
    r_zl,
    r_zr,
    f_xl,
    f_xr,
    f_yl,
    f_yr,
    f_zl,
    f_zr,
    g_xl,
    g_xr,
    g_yl,
    g_yr,
    g_zl,
    g_zr,
    exy_mm,
    exy_pp,
    exy_pm,
    exy_mp,
    exz_mm,
    exz_pp,
    exz_pm,
    exz_mp,
    eyz_mm,
    eyz_pp,
    eyz_pm,
    eyz_mp,
    in_sem,
    send_sem,
    recv_sem,
    fsend_sem,
    frecv_sem,
    rs_send,
    rs_recv,
):
    count = dict(zip(("gx", "gy", "gz"), sizes))
    index = {axis: lax.axis_index(axis) for axis in ("gx", "gy", "gz")}
    gz = index["gz"]
    partner = gz + 1 - 2 * lax.rem(gz, 2)
    cross = lax.rem(gz + 2, 4)

    def exists(step):
        found = None
        for axis, d in zip(("gx", "gy", "gz"), step):
            if d:
                here = index[axis] < count[axis] - 1 if d > 0 else index[axis] > 0
                found = here if found is None else jnp.logical_and(found, here)
        return found

    def at(step):
        return {axis: index[axis] + d for axis, d in zip(("gx", "gy", "gz"), step) if d}

    barrier = pltpu.get_barrier_semaphore()

    def greet(where):
        pl.semaphore_signal(barrier, inc=1, device_id=where, device_id_type=MESH)

    greeted = 3
    for step in GREETED:

        @pl.when(exists(step))
        def _():
            greet(at(step))

        greeted = greeted + exists(step).astype(jnp.int32)
    for d in (1, 2, 3):
        greet({"gz": lax.rem(gz + d, 4)})

    def local(src, dst, n):
        return pltpu.make_async_copy(src, dst, in_sem.at[n])

    loads = dict(
        adj=local(adj_in, adj, 0),
        lam=local(lam_in, params.at[0], 1),
        mu=local(mu_in, params.at[1], 1),
        buoy=local(buoy_in, params.at[2], 1),
        rec=local(rec_in.at[0, 0], rec, 2),
        traces=local(tr_in.at[0, 0, 0], traces, 3),
        plan=local(plan_in, t_plan, 4),
        wav=local(wav_in, t_wav, 5),
        src=local(src_in.at[0, 0, 0], t_src, 6),
        peer=local(hpeer.at[0, 0], t_peer, 7),
        slot=local(hslot.at[0, 0], t_slot, 8),
        own_s=local(store.at[:, pl.ds(3, 6), 0], gath_s.at[pl.ds(gz * 8, 8)], 9),
        own_v=local(store.at[:, pl.ds(0, 3), 0], gath_v.at[pl.ds(gz * 8, 8)], 10),
    )
    for copy in loads.values():
        copy.start()

    def edges(e):
        return (
            (exy_mm, (1, 1, 0), f_yr.at[e, pl.ds(0, 1)]),
            (exy_pp, (-1, -1, 0), f_yl.at[e, pl.ds(2, 2)]),
            (exy_pm, (-1, 1, 0), f_yr.at[e, pl.ds(1, 1)]),
            (exy_mp, (1, -1, 0), f_yl.at[e, pl.ds(4, 1)]),
            (exz_mm, (1, 0, 1), f_zr.at[e, pl.ds(0, 1)]),
            (exz_pp, (-1, 0, -1), f_zl.at[e, pl.ds(2, 2)]),
            (exz_pm, (-1, 0, 1), f_zr.at[e, pl.ds(1, 1)]),
            (exz_mp, (1, 0, -1), f_zl.at[e, pl.ds(6, 1)]),
            (eyz_mm, (0, 1, 1), f_zr.at[e, pl.ds(1, 1)]),
            (eyz_pp, (0, -1, -1), f_zl.at[e, pl.ds(4, 2)]),
            (eyz_pm, (0, -1, 1), f_zr.at[e, pl.ds(0, 1)]),
            (eyz_mp, (0, 1, -1), f_zl.at[e, pl.ds(6, 1)]),
        )

    def back(step):
        return tuple(-d for d in step)

    for step, refs in (
        ((-1, 0, 0), (r_xl, g_xl)),
        ((1, 0, 0), (r_xr, g_xr)),
        ((0, -1, 0), (r_yl, g_yl)),
        ((0, 1, 0), (r_yr, g_yr)),
        ((0, 0, -1), (r_zl, g_zl)),
        ((0, 0, 1), (r_zr, g_zr)),
        *((back(step), (ref,)) for ref, step, _ in edges(0)),
    ):

        @pl.when(jnp.logical_not(exists(step)))
        def _():
            for ref in refs:
                ref[...] = jnp.zeros(ref.shape, jnp.float32)

    pl.semaphore_wait(barrier, greeted)

    def remote(src, dst, n, where):
        return pltpu.make_async_remote_copy(
            src_ref=src,
            dst_ref=dst,
            send_sem=rs_send.at[n],
            recv_sem=rs_recv.at[n],
            device_id={"gz": where},
            device_id_type=MESH,
        )

    mine, theirs = pl.ds(gz * 8, 8), pl.ds(cross * 8, 8)
    st_s, st_v = store.at[:, pl.ds(3, 6), 0], store.at[:, pl.ds(0, 3), 0]
    cross_s = remote(st_s, gath_s.at[mine], 0, cross)
    cross_v = remote(st_v, gath_v.at[mine], 1, cross)
    pair_s = remote(st_s, gath_s.at[mine], 2, partner)
    pair_v = remote(st_v, gath_v.at[mine], 3, partner)
    relay_s = remote(gath_s.at[theirs], gath_s.at[theirs], 4, partner)
    relay_v = remote(gath_v.at[theirs], gath_v.at[theirs], 5, partner)
    cross_s.start()
    cross_v.start()
    pair_s.start()
    pair_v.start()

    lam, mu, buoy = params.at[0], params.at[1], params.at[2]
    av, as_ = [adj.at[i] for i in range(3)], [adj.at[3 + i] for i in range(6)]

    ends = (
        ((1, 0, 0), s_xr, r_xl),
        ((-1, 0, 0), s_xl, r_xr),
        ((0, 1, 0), s_yr, r_yl),
        ((0, -1, 0), s_yl, r_yr),
        ((0, 0, 1), s_zr, r_zl),
        ((0, 0, -1), s_zl, r_zr),
    )

    def face(r, d, fields):
        step, source, target = ends[d]
        if d < 2:
            src, dst = source.at[r], target.at[r]
        else:
            src, dst = source.at[r, pl.ds(0, fields)], target.at[r, pl.ds(0, fields)]
        copy = pltpu.make_async_remote_copy(
            src_ref=src,
            dst_ref=dst,
            send_sem=send_sem.at[d],
            recv_sem=recv_sem.at[r % 2, d],
            device_id=at(step),
            device_id_type=MESH,
        )
        return copy, exists(step), exists(back(step))

    COUNTS = ((2, 3), (2, 1), (1, 2), (2, 1))

    def sent(r):
        for d in range(6):
            copy, goes, _ = face(r, d, COUNTS[r][d % 2])

            @pl.when(goes)
            def _():
                copy.wait_send()

    def send_faces(r, up, down):
        (xu, yu, zu), (xd, yd, zd) = up, down
        if r > 0:
            sent(r - 1)

        def start(d):
            copy, goes, _ = face(r, d, COUNTS[r][d % 2])

            @pl.when(goes)
            def _():
                copy.start()

        s_xr[r] = pack_columns(xu, 127)
        s_xl[r] = pack_columns(xd, 0)
        start(0)
        start(1)
        for i, f in enumerate(zu):
            s_zr[r, i] = f[7]
        for i, f in enumerate(zd):
            s_zl[r, i] = f[0]
        start(4)
        start(5)
        for i, f in enumerate(yu):
            s_yr[r, i] = f[:, 7:8, :]
        for i, f in enumerate(yd):
            s_yl[r, i] = f[:, 0:1, :]
        start(2)
        start(3)

    def send_stress(r, s):
        send_faces(r, ((s[3], s[4]), (s[3], s[5]), (s[4], s[5])), ((s[0],), (s[1],), (s[2],)))

    def send_velocity(r, v, more=()):
        send_faces(
            r,
            ((v[0], *more), (v[1], *more), (v[2], *more)),
            ((v[1], v[2], *more), (v[0], v[2], *more), (v[0], v[1], *more)),
        )

    def receive(r):
        for d in range(6):
            copy, _, comes = face(r, d, COUNTS[r][d % 2])

            @pl.when(comes)
            def _():
                copy.wait_recv()

    def stress_faces(r):
        xl, xr = r_xl[r], r_xr[r]
        return {
            ("xr", 0): unpack_columns(xr, 0, 127),
            ("xl", 3): unpack_columns(xl, 0, 0),
            ("xl", 4): unpack_columns(xl, 1, 0),
            ("yl", 3): r_yl[r, 0],
            ("yl", 5): r_yl[r, 1],
            ("yr", 1): r_yr[r, 0],
            ("zl", 4): r_zl[r, 0],
            ("zl", 5): r_zl[r, 1],
            ("zr", 2): r_zr[r, 0],
        }

    def velocity_faces(r):
        xl, xr = r_xl[r], r_xr[r]
        return {
            ("xl", 0): unpack_columns(xl, 0, 0),
            ("xr", 1): unpack_columns(xr, 0, 127),
            ("xr", 2): unpack_columns(xr, 1, 127),
            ("yl", 1): r_yl[r, 0],
            ("yr", 0): r_yr[r, 0],
            ("yr", 2): r_yr[r, 1],
            ("zl", 2): r_zl[r, 0],
            ("zr", 0): r_zr[r, 0],
            ("zr", 1): r_zr[r, 1],
        }

    fends = (
        (g_xl, (1, 0, 0), f_xr),
        (g_xr, (-1, 0, 0), f_xl),
        (g_yl, (0, 1, 0), f_yr),
        (g_yr, (0, -1, 0), f_yl),
        (g_zl, (0, 0, 1), f_zr),
        (g_zr, (0, 0, -1), f_zl),
    )

    def message(e, n):
        if n < 6:
            target, step, source = fends[n]
            src = source.at[e] if n < 2 else source.at[e, pl.ds(0, 3)]
        else:
            target, step, src = edges(e)[n - 6]
        copy = pltpu.make_async_remote_copy(
            src_ref=src,
            dst_ref=target.at[e],
            send_sem=fsend_sem.at[n],
            recv_sem=frecv_sem.at[e, n],
            device_id=at(step),
            device_id_type=MESH,
        )
        return copy, exists(step), exists(back(step))

    def forward_start(e, n):
        copy, goes, _ = message(e, n)

        @pl.when(goes)
        def _():
            copy.start()

    def forward_sent(e):
        for n in range(18):
            copy, goes, _ = message(e, n)

            @pl.when(goes)
            def _():
                copy.wait_send()

    def forward_receive(e):
        for n in range(18):
            copy, _, comes = message(e, n)

            @pl.when(comes)
            def _():
                copy.wait_recv()

    def forward_edges(e):
        if e > 0:
            forward_sent(e - 1)
        f_yr[e, 0] = fs[3, :, 7:8, :]
        f_yr[e, 1] = fs[5, :, 7:8, :]
        for i, f in ((2, 1), (3, 0), (4, 4)):
            f_yl[e, i] = fs[f, :, 0:1, :]
        for n in (6, 7, 8, 9):
            forward_start(e, n)
        f_zr[e, 0] = fs[4, 7]
        f_zr[e, 1] = fs[5, 7]
        for i, f in ((2, 2), (3, 0), (4, 2), (5, 1), (6, 3)):
            f_zl[e, i] = fs[f, 0]
        for n in range(10, 18):
            forward_start(e, n)

    def forward_faces(e):
        rates = velocity_rates([fs[i] for i in range(6)], buoy[...], Zeros())
        for i in range(3):
            fv[i] = fv[i] + rates[i]
        f_xr[e] = pack_columns((fs[3], fs[4], fv[0]), 127)
        f_xl[e] = pack_columns((fs[0], fv[1], fv[2]), 0)
        forward_start(e, 0)
        forward_start(e, 1)
        f_zr[e, 2] = fv[2, 7]
        f_zl[e, 0] = fv[0, 0]
        f_zl[e, 1] = fv[1, 0]
        forward_start(e, 4)
        forward_start(e, 5)
        f_yr[e, 2] = fv[1, :, 7:8, :]
        f_yl[e, 0] = fv[0, :, 0:1, :]
        f_yl[e, 1] = fv[2, :, 0:1, :]
        forward_start(e, 2)
        forward_start(e, 3)

    def forward_step(e):
        xl, xr = g_xl[e], g_xr[e]
        lane3, row3 = iota3(2), iota3(1)
        lane2, row2 = iota2(1), iota2(0)
        z1 = lax.broadcasted_iota(jnp.int32, (8, 1, 128), 0)
        lane1 = lax.broadcasted_iota(jnp.int32, (8, 1, 128), 2)

        def layer(at_z, tile, like):
            return jnp.where(iota3(0) == at_z, tile[None], 0.0) if like == 3 else jnp.where(z1 == at_z, tile, 0.0)

        def first_lane(f, axis):
            return pltpu.roll(f, 1, axis)

        def last_lane(f, axis):
            return pltpu.roll(f, 127, axis)

        mm, pp = first_lane(exy_mm[e, 0], 2), (last_lane(exy_pp[e, 0], 2), last_lane(exy_pp[e, 1], 2))
        pm, mp = last_lane(exy_pm[e, 0], 2), first_lane(exy_mp[e, 0], 2)
        zmm, zpp = first_lane(exz_mm[e, 0], 1), (last_lane(exz_pp[e, 0], 1), last_lane(exz_pp[e, 1], 1))
        zpm, zmp = last_lane(exz_pm[e, 0], 1), first_lane(exz_mp[e, 0], 1)
        all3 = (8, 8, 128)
        nothing = jnp.zeros(all3, jnp.float32)

        def row(at_y, face):
            return jnp.where(row3 == at_y, jnp.broadcast_to(face, all3), nothing)

        b = buoy[...]
        h = {}
        h["xl", 0] = unpack_columns(xl, 2, 0) + bx[0] * (fs[0] - row(0, mm) - layer(0, zmm, 3))
        h["xr", 1] = unpack_columns(xr, 1, 127) + bx[1] * (row(7, pp[0]) - fs[3] - layer(0, zpm, 3))
        h["xr", 2] = unpack_columns(xr, 2, 127) + bx[1] * (layer(7, zpp[0], 3) - fs[4] - row(0, pm))

        def y_layer(at_z, tile, at_y):
            return jnp.where(z1 == at_z, jnp.broadcast_to(tile[at_y : at_y + 1, :][None], (8, 1, 128)), 0.0)

        bym, byp = r_yl[0, 1], r_yr[0, 2]
        h["yl", 1] = g_yl[e, 2] + bym * (
            fs[1, :, 0:1, :] - jnp.where(lane1 == 0, mm, 0.0) - y_layer(0, eyz_mm[e, 0], 7)
        )
        h["yr", 0] = g_yr[e, 0] + byp * (
            jnp.where(lane1 == 127, pp[1], 0.0) - fs[3, :, 7:8, :] - y_layer(0, eyz_pm[e, 0], 0)
        )
        h["yr", 2] = g_yr[e, 1] + byp * (
            y_layer(7, eyz_pp[e, 0], 0) - fs[5, :, 7:8, :] - jnp.where(lane1 == 0, mp, 0.0)
        )

        def y_edge(tile, at_y, from_y):
            return jnp.where(row2 == at_y, jnp.broadcast_to(tile[from_y : from_y + 1, :], (8, 128)), 0.0)

        bzm, bzp = r_zl[0, 1], r_zr[0, 2]
        h["zl", 2] = g_zl[e, 2] + bzm * (fs[2, 0] - jnp.where(lane2 == 0, zmm, 0.0) - y_edge(eyz_mm[e, 0], 0, 7))
        h["zr", 0] = g_zr[e, 0] + bzp * (
            jnp.where(lane2 == 127, zpp[1], 0.0) - fs[4, 7] - y_edge(eyz_mp[e, 0], 0, 7)
        )
        h["zr", 1] = g_zr[e, 1] + bzp * (
            y_edge(eyz_pp[e, 1], 7, 0) - fs[5, 7] - jnp.where(lane2 == 0, zmp, 0.0)
        )

        fv[0] = fv[0] + b * (jnp.where(lane3 == 127, unpack_columns(xr, 0, 127), 0.0) - row(0, g_yl[e, 0]))
        fv[1] = fv[1] + b * (row(7, g_yr[e, 2]) - jnp.where(lane3 == 0, unpack_columns(xl, 0, 0), 0.0))
        fv[2] = fv[2] - b * (jnp.where(lane3 == 0, unpack_columns(xl, 1, 0), 0.0) + row(0, g_yl[e, 1]))
        fv[0, 0] = fv[0, 0] - buoy[0] * g_zl[e, 0]
        fv[1, 0] = fv[1, 0] - buoy[0] * g_zl[e, 1]
        fv[2, 7] = fv[2, 7] + buoy[7] * g_zr[e, 2]
        return stress_rates([fv[i] for i in range(3)], lam[...], mu[...], h)

    loads["adj"].wait()
    pltpu.make_async_copy(params, params, in_sem.at[1]).wait()
    send_velocity(0, [f[...] for f in av], (buoy[...],))

    for name in ("rec", "traces", "plan"):
        loads[name].wait()
    cells = rec[0]
    row_of, x_of = lax.shift_right_logical(cells, 7), lax.bitwise_and(cells, 127)
    rows = lax.broadcasted_iota(jnp.int32, (64, 64), 0)
    hit = rows == jnp.broadcast_to(row_of, (64, 64))
    samples = [jnp.broadcast_to(traces[pl.ds(t_plan[k], 1), :], (64, 64)) for k in range(STEPS)]
    left = jnp.concatenate([jnp.where(hit, samples[k], 0.0) for k in range(STEPS)], axis=0)
    columns = lax.broadcasted_iota(jnp.int32, (128, 64), 0)
    right = jnp.where(columns == jnp.broadcast_to(x_of, (128, 64)), 1.0, 0.0)
    spread = lax.dot_general(
        left, right, (((1,), (1,)), ((), ())), precision=lax.Precision.HIGHEST, preferred_element_type=jnp.float32
    )
    spread = spread.reshape(STEPS, 8, 8, 128)
    for i in range(3):
        a1[i] = as_[i][...] + spread[1]
        a0[i] = spread[0]
    for i in range(3, 6):
        a1[i] = as_[i][...]

    for name in ("wav", "src"):
        loads[name].wait()
    flat = iota3(0) * 1024 + iota3(1) * 128 + iota3(2)
    counted = jnp.zeros((8, 8, 128), jnp.float32)
    for j in range(t_src.shape[0]):
        counted = counted + jnp.where(flat == t_src[j], 1.0, 0.0)
    hits[...] = counted

    receive(0)
    rates = stress_rates([f[...] for f in av], lam[...], mu[...], velocity_faces(0))
    for i in range(6):
        as_[i][...] = a1[i] - rates[i]
    send_stress(1, [f[...] for f in as_])
    bx[0] = unpack_columns(r_xl[0], 1, 0)
    bx[1] = unpack_columns(r_xr[0], 2, 127)

    cross_s.wait_recv()
    relay_s.start()
    cross_v.wait_recv()
    relay_v.start()

    for name in ("peer", "slot", "own_s", "own_v"):
        loads[name].wait()
    pair_s.wait_recv()
    relay_s.wait_recv()
    where_is = [t_peer[gz, p] * 8 + t_slot[gz, p] for p in range(8)]
    for p in range(8):
        fs[:, p] = gath_s[where_is[p]].astype(jnp.float32)
    forward_edges(0)
    pair_v.wait_recv()
    relay_v.wait_recv()
    for p in range(8):
        fv[:, p] = gath_v[where_is[p]].astype(jnp.float32)
    forward_faces(0)

    receive(1)
    rates = velocity_rates([f[...] for f in as_], buoy[...], stress_faces(1))
    for i in range(3):
        av[i][...] = av[i][...] - rates[i]
    send_velocity(2, [f[...] for f in av])
    for i in range(3):
        a0[i] = a0[i] + as_[i][...]
    for i in range(3, 6):
        a0[i] = as_[i][...]

    receive(2)
    rates = stress_rates([f[...] for f in av], lam[...], mu[...], velocity_faces(2))
    for i in range(6):
        as_[i][...] = a0[i] - rates[i]
    send_stress(3, [f[...] for f in as_])

    forward_receive(0)
    rates = forward_step(0)
    pulse = hits[...] * t_wav[t_plan[0]]
    for i in range(3):
        fs[i] = fs[i] + rates[i] + pulse
    for i in range(3, 6):
        fs[i] = fs[i] + rates[i]
    forward_edges(1)
    forward_faces(1)

    def image(s, a):
        by_lambda = (s[0] + s[1] + s[2]) * (a[0] + a[1] + a[2])
        by_mu = s[0] * a[0] + s[1] * a[1] + s[2] * a[2] + 2.0 * (s[3] * a[3] + s[4] * a[4] + s[5] * a[5])
        return by_lambda, by_mu

    by_lambda, by_mu = image(fs, a0)
    il_out[...] = by_lambda
    im_out[...] = by_mu

    receive(3)
    rates = velocity_rates([f[...] for f in as_], buoy[...], stress_faces(3))
    for i in range(3):
        adj_out[i] = av[i][...] - rates[i]
    for i in range(6):
        adj_out[3 + i] = as_[i][...]
    sent(3)
    for copy in (cross_s, cross_v, pair_s, pair_v, relay_s, relay_v):
        copy.wait_send()

    forward_receive(1)
    rates = forward_step(1)
    pulse = hits[...] * t_wav[t_plan[1]]
    last = [fs[i] + rates[i] + pulse for i in range(3)] + [fs[i] + rates[i] for i in range(3, 6)]
    by_lambda, by_mu = image(last, a1)
    il_out[...] += by_lambda
    im_out[...] += by_mu
    forward_sent(1)


def write_out(adj, il, im, adj_out, il_out, im_out, sem):
    copies = [
        pltpu.make_async_copy(src, dst, sem.at[n])
        for n, (src, dst) in enumerate(((adj, adj_out), (il, il_out), (im, im_out)))
    ]
    for copy in copies:
        copy.start()
    for copy in copies:
        copy.wait()


def solution(mesh):
    sizes = (mesh.shape["gx"], mesh.shape["gy"], mesh.shape["gz"])
    f32, i32, bf16 = jnp.float32, jnp.int32, jnp.bfloat16
    brick = (8, 8, 128)

    def on_device(*args):
        nt, nrec = args[10].shape[-2:]
        nsrc = args[7].shape[-1]
        vmem = pltpu.VMEM
        scratch = [
            vmem((3,) + brick, f32),
            vmem((1, nrec), i32),
            vmem((nt, nrec), f32),
            pltpu.SMEM((4, 8), i32),
            pltpu.SMEM((4, 8), i32),
            pltpu.SMEM((nsrc,), i32),
            pltpu.SMEM((nt,), f32),
            pltpu.SMEM((STEPS,), i32),
            vmem((32, 6, 8, 128), bf16),
            vmem((32, 3, 8, 128), bf16),
            vmem((3,) + brick, f32),
            vmem((6,) + brick, f32),
            vmem((9,) + brick, f32),
            vmem((6,) + brick, f32),
            vmem((6,) + brick, f32),
            vmem((2,) + brick, f32),
            vmem(brick, f32),
        ]
        row, tile = (8, 1, 128), (8, 128)
        for _ in range(2):
            scratch += [vmem((4,) + tile, f32)] * 2 + [vmem((4, 3) + row, f32)] * 2 + [vmem((4, 3) + tile, f32)] * 2
        for down_y, down_z in ((5, 7), (3, 3)):
            received = down_y == 3
            scratch += [vmem((2,) + tile, f32)] * 2
            scratch += [vmem((2, 3 if received else 5) + row, f32), vmem((2, 3) + row, f32)]
            scratch += [vmem((2, 3 if received else 7) + tile, f32), vmem((2, 3) + tile, f32)]
        for shape in (row, tile, tile):
            scratch += [vmem((2, fields) + shape, f32) for fields in (1, 2, 1, 1)]
        dma = pltpu.SemaphoreType.DMA
        scratch += [dma((11,)), dma((6,)), dma((2, 6)), dma((18,)), dma((2, 18)), dma((6,)), dma((6,))]
        shapes = ((9,) + brick, brick, brick)
        results = pl.pallas_call(
            functools.partial(kernel, sizes),
            out_shape=tuple(pltpu.VMEM(shape, f32) for shape in shapes),
            in_specs=[pl.BlockSpec(memory_space=pl.ANY)] * 12,
            out_specs=(pl.BlockSpec(memory_space=pltpu.VMEM),) * 3,
            scratch_shapes=scratch,
            compiler_params=pltpu.CompilerParams(
                collective_id=0, has_side_effects=True
            ),
            name="window",
        )(*args)
        return pl.pallas_call(
            write_out,
            out_shape=tuple(jax.ShapeDtypeStruct(shape, f32) for shape in shapes),
            in_specs=[pl.BlockSpec(memory_space=pltpu.VMEM)] * 3,
            out_specs=(pl.BlockSpec(memory_space=pl.ANY),) * 3,
            scratch_shapes=[pltpu.SemaphoreType.DMA((3,))],
            compiler_params=pltpu.CompilerParams(vmem_limit_bytes=16 << 20),
            name="write_out",
        )(*results)

    return jax.shard_map(
        on_device,
        mesh=mesh,
        in_specs=(
            P("gz", None, None, "gy", "gx"),
            P("gx", "gy", None, None),
            P("gx", "gy", None, None),
            P(None, "gz", "gy", "gx"),
            P("gz", "gy", "gx"),
            P("gz", "gy", "gx"),
            P("gz", "gy", "gx"),
            P("gz", "gy", "gx", None),
            P(),
            P("gz", "gy", "gx", None),
            P("gz", "gy", "gx", None, None),
            P(),
        ),
        out_specs=(P(None, "gz", "gy", "gx"), P("gz", "gy", "gx"), P("gz", "gy", "gx")),
        check_vma=False,
    )
```

```python
import functools

import jax
import jax.numpy as jnp
from jax import lax
from jax.experimental import pallas as pl
from jax.experimental.pallas import tpu as pltpu
from jax.sharding import PartitionSpec as P

MESH = pl.DeviceIdType.MESH
STEPS = 2

GREETED = ((1, 0, 0), (-1, 0, 0), (0, 1, 0), (0, -1, 0))


def iota3(dim):
    return lax.broadcasted_iota(jnp.int32, (8, 8, 128), dim)


def iota2(dim):
    return lax.broadcasted_iota(jnp.int32, (8, 128), dim)


def pack_columns(fields, lane):
    lanes = iota2(1)
    packed = jnp.zeros((8, 128), jnp.float32)
    for number, field in enumerate(fields):
        for z in range(8):
            at = number * 8 + z
            moved = pltpu.roll(field[z], (at - lane) % 128, 1)
            packed = jnp.where(lanes == at, moved, packed)
    return packed


def unpack_columns(packed, number, lane):
    return jnp.stack([pltpu.roll(packed, (lane - number * 8 - z) % 128, 1) for z in range(8)])


def behind_x(f, face):
    return f - jnp.where(iota3(2) == 0, face, pltpu.roll(f, 1, 2))


def ahead_x(f, face):
    return jnp.where(iota3(2) == 127, face, pltpu.roll(f, 127, 2)) - f


def behind_y(f, face):
    return f - jnp.where(iota3(1) == 0, jnp.broadcast_to(face, (8, 8, 128)), pltpu.roll(f, 1, 1))


def ahead_y(f, face):
    return jnp.where(iota3(1) == 7, jnp.broadcast_to(face, (8, 8, 128)), pltpu.roll(f, 7, 1)) - f


def behind_z(f, face):
    return f - jnp.concatenate([face[None], f[:7]], axis=0)


def ahead_z(f, face):
    return jnp.concatenate([f[1:], face[None]], axis=0) - f


def velocity_rates(s, b, h):
    rx = b * (ahead_x(s[0], h["xr", 0]) + behind_y(s[3], h["yl", 3]) + behind_z(s[4], h["zl", 4]))
    ry = b * (behind_x(s[3], h["xl", 3]) + ahead_y(s[1], h["yr", 1]) + behind_z(s[5], h["zl", 5]))
    rz = b * (behind_x(s[4], h["xl", 4]) + behind_y(s[5], h["yl", 5]) + ahead_z(s[2], h["zr", 2]))
    return rx, ry, rz


def stress_rates(v, lam, mu, h):
    exx, eyy, ezz = behind_x(v[0], h["xl", 0]), behind_y(v[1], h["yl", 1]), behind_z(v[2], h["zl", 2])
    spread = lam * (exx + eyy + ezz)
    twice = 2.0 * mu
    return (
        spread + twice * exx,
        spread + twice * eyy,
        spread + twice * ezz,
        mu * (ahead_y(v[0], h["yr", 0]) + ahead_x(v[1], h["xr", 1])),
        mu * (ahead_z(v[0], h["zr", 0]) + ahead_x(v[2], h["xr", 2])),
        mu * (ahead_z(v[1], h["zr", 1]) + ahead_y(v[2], h["yr", 2])),
    )


class Zeros:
    def __getitem__(self, key):
        side = key[0]
        shape = (8, 1, 128) if side[0] == "y" else (8, 128)
        return jnp.zeros((8, 8, 128) if side[0] == "x" else shape, jnp.float32)


def kernel(
    sizes,
    store,
    hpeer,
    hslot,
    adj_in,
    lam_in,
    mu_in,
    buoy_in,
    src_in,
    wav_in,
    rec_in,
    tr_in,
    plan_in,
    adj_out,
    il_out,
    im_out,
    params,
    rec,
    traces,
    t_peer,
    t_slot,
    t_src,
    t_wav,
    t_plan,
    gath_s,
    gath_v,
    fv,
    fs,
    adj,
    a1,
    a0,
    bx,
    hits,
    s_xl,
    s_xr,
    s_yl,
    s_yr,
    s_zl,
    s_zr,
    r_xl,
    r_xr,
    r_yl,
    r_yr,
    r_zl,
    r_zr,
    f_xl,
    f_xr,
    f_yl,
    f_yr,
    f_zl,
    f_zr,
    g_xl,
    g_xr,
    g_yl,
    g_yr,
    g_zl,
    g_zr,
    exy_mm,
    exy_pp,
    exy_pm,
    exy_mp,
    exz_mm,
    exz_pp,
    exz_pm,
    exz_mp,
    eyz_mm,
    eyz_pp,
    eyz_pm,
    eyz_mp,
    in_sem,
    send_sem,
    recv_sem,
    fsend_sem,
    frecv_sem,
    rs_send,
    rs_recv,
):
    count = dict(zip(("gx", "gy", "gz"), sizes))
    index = {axis: lax.axis_index(axis) for axis in ("gx", "gy", "gz")}
    gz = index["gz"]
    partner = gz + 1 - 2 * lax.rem(gz, 2)
    cross = lax.rem(gz + 2, 4)

    def exists(step):
        found = None
        for axis, d in zip(("gx", "gy", "gz"), step):
            if d:
                here = index[axis] < count[axis] - 1 if d > 0 else index[axis] > 0
                found = here if found is None else jnp.logical_and(found, here)
        return found

    def at(step):
        return {axis: index[axis] + d for axis, d in zip(("gx", "gy", "gz"), step) if d}

    barrier = pltpu.get_barrier_semaphore()

    def greet(where):
        pl.semaphore_signal(barrier, inc=1, device_id=where, device_id_type=MESH)

    greeted = 3
    for step in GREETED:

        @pl.when(exists(step))
        def _():
            greet(at(step))

        greeted = greeted + exists(step).astype(jnp.int32)
    for d in (1, 2, 3):
        greet({"gz": lax.rem(gz + d, 4)})

    def local(src, dst, n):
        return pltpu.make_async_copy(src, dst, in_sem.at[n])

    loads = dict(
        adj=local(adj_in, adj, 0),
        lam=local(lam_in, params.at[0], 1),
        mu=local(mu_in, params.at[1], 1),
        buoy=local(buoy_in, params.at[2], 1),
        rec=local(rec_in.at[0, 0], rec, 2),
        traces=local(tr_in.at[0, 0, 0], traces, 3),
        plan=local(plan_in, t_plan, 4),
        wav=local(wav_in, t_wav, 5),
        src=local(src_in.at[0, 0, 0], t_src, 6),
        peer=local(hpeer.at[0, 0], t_peer, 7),
        slot=local(hslot.at[0, 0], t_slot, 8),
        own_s=local(store.at[:, pl.ds(3, 6), 0], gath_s.at[pl.ds(gz * 8, 8)], 9),
        own_v=local(store.at[:, pl.ds(0, 3), 0], gath_v.at[pl.ds(gz * 8, 8)], 10),
    )
    for copy in loads.values():
        copy.start()

    def edges(e):
        return (
            (exy_mm, (1, 1, 0), f_yr.at[e, pl.ds(0, 1)]),
            (exy_pp, (-1, -1, 0), f_yl.at[e, pl.ds(2, 2)]),
            (exy_pm, (-1, 1, 0), f_yr.at[e, pl.ds(1, 1)]),
            (exy_mp, (1, -1, 0), f_yl.at[e, pl.ds(4, 1)]),
            (exz_mm, (1, 0, 1), f_zr.at[e, pl.ds(0, 1)]),
            (exz_pp, (-1, 0, -1), f_zl.at[e, pl.ds(2, 2)]),
            (exz_pm, (-1, 0, 1), f_zr.at[e, pl.ds(1, 1)]),
            (exz_mp, (1, 0, -1), f_zl.at[e, pl.ds(6, 1)]),
            (eyz_mm, (0, 1, 1), f_zr.at[e, pl.ds(1, 1)]),
            (eyz_pp, (0, -1, -1), f_zl.at[e, pl.ds(4, 2)]),
            (eyz_pm, (0, -1, 1), f_zr.at[e, pl.ds(0, 1)]),
            (eyz_mp, (0, 1, -1), f_zl.at[e, pl.ds(6, 1)]),
        )

    def back(step):
        return tuple(-d for d in step)

    for step, refs in (
        ((-1, 0, 0), (r_xl, g_xl)),
        ((1, 0, 0), (r_xr, g_xr)),
        ((0, -1, 0), (r_yl, g_yl)),
        ((0, 1, 0), (r_yr, g_yr)),
        ((0, 0, -1), (r_zl, g_zl)),
        ((0, 0, 1), (r_zr, g_zr)),
        *((back(step), (ref,)) for ref, step, _ in edges(0)),
    ):

        @pl.when(jnp.logical_not(exists(step)))
        def _():
            for ref in refs:
                ref[...] = jnp.zeros(ref.shape, jnp.float32)

    pl.semaphore_wait(barrier, greeted)

    def remote(src, dst, n, where):
        return pltpu.make_async_remote_copy(
            src_ref=src,
            dst_ref=dst,
            send_sem=rs_send.at[n],
            recv_sem=rs_recv.at[n],
            device_id={"gz": where},
            device_id_type=MESH,
        )

    mine, theirs = pl.ds(gz * 8, 8), pl.ds(cross * 8, 8)
    st_s, st_v = gath_s.at[mine], gath_v.at[mine]
    loads["own_s"].wait()
    loads["own_v"].wait()
    cross_s = remote(st_s, gath_s.at[mine], 0, cross)
    cross_v = remote(st_v, gath_v.at[mine], 1, cross)
    pair_s = remote(st_s, gath_s.at[mine], 2, partner)
    pair_v = remote(st_v, gath_v.at[mine], 3, partner)
    relay_s = remote(gath_s.at[theirs], gath_s.at[theirs], 4, partner)
    relay_v = remote(gath_v.at[theirs], gath_v.at[theirs], 5, partner)
    cross_s.start()
    pair_s.start()
    pair_v.start()

    lam, mu, buoy = params.at[0], params.at[1], params.at[2]
    av, as_ = [adj.at[i] for i in range(3)], [adj.at[3 + i] for i in range(6)]

    ends = (
        ((1, 0, 0), s_xr, r_xl),
        ((-1, 0, 0), s_xl, r_xr),
        ((0, 1, 0), s_yr, r_yl),
        ((0, -1, 0), s_yl, r_yr),
        ((0, 0, 1), s_zr, r_zl),
        ((0, 0, -1), s_zl, r_zr),
    )

    def face(r, d, fields):
        step, source, target = ends[d]
        if d < 2:
            src, dst = source.at[r], target.at[r]
        else:
            src, dst = source.at[r, pl.ds(0, fields)], target.at[r, pl.ds(0, fields)]
        copy = pltpu.make_async_remote_copy(
            src_ref=src,
            dst_ref=dst,
            send_sem=send_sem.at[d],
            recv_sem=recv_sem.at[r % 2, d],
            device_id=at(step),
            device_id_type=MESH,
        )
        return copy, exists(step), exists(back(step))

    COUNTS = ((2, 3), (2, 1), (1, 2), (2, 1))

    def sent(r):
        for d in range(6):
            copy, goes, _ = face(r, d, COUNTS[r][d % 2])

            @pl.when(goes)
            def _():
                copy.wait_send()

    def send_faces(r, up, down):
        (xu, yu, zu), (xd, yd, zd) = up, down
        if r > 0:
            sent(r - 1)

        def start(d):
            copy, goes, _ = face(r, d, COUNTS[r][d % 2])

            @pl.when(goes)
            def _():
                copy.start()

        s_xr[r] = pack_columns(xu, 127)
        s_xl[r] = pack_columns(xd, 0)
        start(0)
        start(1)
        for i, f in enumerate(zu):
            s_zr[r, i] = f[7]
        for i, f in enumerate(zd):
            s_zl[r, i] = f[0]
        start(4)
        start(5)
        for i, f in enumerate(yu):
            s_yr[r, i] = f[:, 7:8, :]
        for i, f in enumerate(yd):
            s_yl[r, i] = f[:, 0:1, :]
        start(2)
        start(3)

    def send_stress(r, s):
        send_faces(r, ((s[3], s[4]), (s[3], s[5]), (s[4], s[5])), ((s[0],), (s[1],), (s[2],)))

    def send_velocity(r, v, more=()):
        send_faces(
            r,
            ((v[0], *more), (v[1], *more), (v[2], *more)),
            ((v[1], v[2], *more), (v[0], v[2], *more), (v[0], v[1], *more)),
        )

    def receive(r):
        for d in range(6):
            copy, _, comes = face(r, d, COUNTS[r][d % 2])

            @pl.when(comes)
            def _():
                copy.wait_recv()

    def stress_faces(r):
        xl, xr = r_xl[r], r_xr[r]
        return {
            ("xr", 0): unpack_columns(xr, 0, 127),
            ("xl", 3): unpack_columns(xl, 0, 0),
            ("xl", 4): unpack_columns(xl, 1, 0),
            ("yl", 3): r_yl[r, 0],
            ("yl", 5): r_yl[r, 1],
            ("yr", 1): r_yr[r, 0],
            ("zl", 4): r_zl[r, 0],
            ("zl", 5): r_zl[r, 1],
            ("zr", 2): r_zr[r, 0],
        }

    def velocity_faces(r):
        xl, xr = r_xl[r], r_xr[r]
        return {
            ("xl", 0): unpack_columns(xl, 0, 0),
            ("xr", 1): unpack_columns(xr, 0, 127),
            ("xr", 2): unpack_columns(xr, 1, 127),
            ("yl", 1): r_yl[r, 0],
            ("yr", 0): r_yr[r, 0],
            ("yr", 2): r_yr[r, 1],
            ("zl", 2): r_zl[r, 0],
            ("zr", 0): r_zr[r, 0],
            ("zr", 1): r_zr[r, 1],
        }

    fends = (
        (g_xl, (1, 0, 0), f_xr),
        (g_xr, (-1, 0, 0), f_xl),
        (g_yl, (0, 1, 0), f_yr),
        (g_yr, (0, -1, 0), f_yl),
        (g_zl, (0, 0, 1), f_zr),
        (g_zr, (0, 0, -1), f_zl),
    )

    def message(e, n):
        if n < 6:
            target, step, source = fends[n]
            src = source.at[e] if n < 2 else source.at[e, pl.ds(0, 3)]
        else:
            target, step, src = edges(e)[n - 6]
        copy = pltpu.make_async_remote_copy(
            src_ref=src,
            dst_ref=target.at[e],
            send_sem=fsend_sem.at[n],
            recv_sem=frecv_sem.at[e, n],
            device_id=at(step),
            device_id_type=MESH,
        )
        return copy, exists(step), exists(back(step))

    def forward_start(e, n):
        copy, goes, _ = message(e, n)

        @pl.when(goes)
        def _():
            copy.start()

    def forward_sent(e):
        for n in range(18):
            copy, goes, _ = message(e, n)

            @pl.when(goes)
            def _():
                copy.wait_send()

    def forward_receive(e):
        for n in range(18):
            copy, _, comes = message(e, n)

            @pl.when(comes)
            def _():
                copy.wait_recv()

    def forward_edges(e):
        if e > 0:
            forward_sent(e - 1)
        f_yr[e, 0] = fs[3, :, 7:8, :]
        f_yr[e, 1] = fs[5, :, 7:8, :]
        for i, f in ((2, 1), (3, 0), (4, 4)):
            f_yl[e, i] = fs[f, :, 0:1, :]
        for n in (6, 7, 8, 9):
            forward_start(e, n)
        f_zr[e, 0] = fs[4, 7]
        f_zr[e, 1] = fs[5, 7]
        for i, f in ((2, 2), (3, 0), (4, 2), (5, 1), (6, 3)):
            f_zl[e, i] = fs[f, 0]
        for n in range(10, 18):
            forward_start(e, n)

    def forward_faces(e):
        rates = velocity_rates([fs[i] for i in range(6)], buoy[...], Zeros())
        for i in range(3):
            fv[i] = fv[i] + rates[i]
        f_xr[e] = pack_columns((fs[3], fs[4], fv[0]), 127)
        f_xl[e] = pack_columns((fs[0], fv[1], fv[2]), 0)
        forward_start(e, 0)
        forward_start(e, 1)
        f_zr[e, 2] = fv[2, 7]
        f_zl[e, 0] = fv[0, 0]
        f_zl[e, 1] = fv[1, 0]
        forward_start(e, 4)
        forward_start(e, 5)
        f_yr[e, 2] = fv[1, :, 7:8, :]
        f_yl[e, 0] = fv[0, :, 0:1, :]
        f_yl[e, 1] = fv[2, :, 0:1, :]
        forward_start(e, 2)
        forward_start(e, 3)

    def forward_step(e):
        xl, xr = g_xl[e], g_xr[e]
        lane3, row3 = iota3(2), iota3(1)
        lane2, row2 = iota2(1), iota2(0)
        z1 = lax.broadcasted_iota(jnp.int32, (8, 1, 128), 0)
        lane1 = lax.broadcasted_iota(jnp.int32, (8, 1, 128), 2)

        def layer(at_z, tile, like):
            return jnp.where(iota3(0) == at_z, tile[None], 0.0) if like == 3 else jnp.where(z1 == at_z, tile, 0.0)

        def first_lane(f, axis):
            return pltpu.roll(f, 1, axis)

        def last_lane(f, axis):
            return pltpu.roll(f, 127, axis)

        mm, pp = first_lane(exy_mm[e, 0], 2), (last_lane(exy_pp[e, 0], 2), last_lane(exy_pp[e, 1], 2))
        pm, mp = last_lane(exy_pm[e, 0], 2), first_lane(exy_mp[e, 0], 2)
        zmm, zpp = first_lane(exz_mm[e, 0], 1), (last_lane(exz_pp[e, 0], 1), last_lane(exz_pp[e, 1], 1))
        zpm, zmp = last_lane(exz_pm[e, 0], 1), first_lane(exz_mp[e, 0], 1)
        all3 = (8, 8, 128)
        nothing = jnp.zeros(all3, jnp.float32)

        def row(at_y, face):
            return jnp.where(row3 == at_y, jnp.broadcast_to(face, all3), nothing)

        b = buoy[...]
        h = {}
        h["xl", 0] = unpack_columns(xl, 2, 0) + bx[0] * (fs[0] - row(0, mm) - layer(0, zmm, 3))
        h["xr", 1] = unpack_columns(xr, 1, 127) + bx[1] * (row(7, pp[0]) - fs[3] - layer(0, zpm, 3))
        h["xr", 2] = unpack_columns(xr, 2, 127) + bx[1] * (layer(7, zpp[0], 3) - fs[4] - row(0, pm))

        def y_layer(at_z, tile, at_y):
            return jnp.where(z1 == at_z, jnp.broadcast_to(tile[at_y : at_y + 1, :][None], (8, 1, 128)), 0.0)

        bym, byp = r_yl[0, 1], r_yr[0, 2]
        h["yl", 1] = g_yl[e, 2] + bym * (
            fs[1, :, 0:1, :] - jnp.where(lane1 == 0, mm, 0.0) - y_layer(0, eyz_mm[e, 0], 7)
        )
        h["yr", 0] = g_yr[e, 0] + byp * (
            jnp.where(lane1 == 127, pp[1], 0.0) - fs[3, :, 7:8, :] - y_layer(0, eyz_pm[e, 0], 0)
        )
        h["yr", 2] = g_yr[e, 1] + byp * (
            y_layer(7, eyz_pp[e, 0], 0) - fs[5, :, 7:8, :] - jnp.where(lane1 == 0, mp, 0.0)
        )

        def y_edge(tile, at_y, from_y):
            return jnp.where(row2 == at_y, jnp.broadcast_to(tile[from_y : from_y + 1, :], (8, 128)), 0.0)

        bzm, bzp = r_zl[0, 1], r_zr[0, 2]
        h["zl", 2] = g_zl[e, 2] + bzm * (fs[2, 0] - jnp.where(lane2 == 0, zmm, 0.0) - y_edge(eyz_mm[e, 0], 0, 7))
        h["zr", 0] = g_zr[e, 0] + bzp * (
            jnp.where(lane2 == 127, zpp[1], 0.0) - fs[4, 7] - y_edge(eyz_mp[e, 0], 0, 7)
        )
        h["zr", 1] = g_zr[e, 1] + bzp * (
            y_edge(eyz_pp[e, 1], 7, 0) - fs[5, 7] - jnp.where(lane2 == 0, zmp, 0.0)
        )

        fv[0] = fv[0] + b * (jnp.where(lane3 == 127, unpack_columns(xr, 0, 127), 0.0) - row(0, g_yl[e, 0]))
        fv[1] = fv[1] + b * (row(7, g_yr[e, 2]) - jnp.where(lane3 == 0, unpack_columns(xl, 0, 0), 0.0))
        fv[2] = fv[2] - b * (jnp.where(lane3 == 0, unpack_columns(xl, 1, 0), 0.0) + row(0, g_yl[e, 1]))
        fv[0, 0] = fv[0, 0] - buoy[0] * g_zl[e, 0]
        fv[1, 0] = fv[1, 0] - buoy[0] * g_zl[e, 1]
        fv[2, 7] = fv[2, 7] + buoy[7] * g_zr[e, 2]
        return stress_rates([fv[i] for i in range(3)], lam[...], mu[...], h)

    loads["adj"].wait()
    pltpu.make_async_copy(params, params, in_sem.at[1]).wait()
    send_velocity(0, [f[...] for f in av], (buoy[...],))

    for name in ("rec", "traces", "plan"):
        loads[name].wait()
    cells = rec[0]
    row_of, x_of = lax.shift_right_logical(cells, 7), lax.bitwise_and(cells, 127)
    rows = lax.broadcasted_iota(jnp.int32, (64, 64), 0)
    hit = rows == jnp.broadcast_to(row_of, (64, 64))
    samples = [jnp.broadcast_to(traces[pl.ds(t_plan[k], 1), :], (64, 64)) for k in range(STEPS)]
    left = jnp.concatenate([jnp.where(hit, samples[k], 0.0) for k in range(STEPS)], axis=0)
    columns = lax.broadcasted_iota(jnp.int32, (128, 64), 0)
    right = jnp.where(columns == jnp.broadcast_to(x_of, (128, 64)), 1.0, 0.0)
    spread = lax.dot_general(
        left, right, (((1,), (1,)), ((), ())), precision=lax.Precision.HIGHEST, preferred_element_type=jnp.float32
    )
    spread = spread.reshape(STEPS, 8, 8, 128)
    for i in range(3):
        a1[i] = as_[i][...] + spread[1]
        a0[i] = spread[0]
    for i in range(3, 6):
        a1[i] = as_[i][...]

    for name in ("wav", "src"):
        loads[name].wait()
    flat = iota3(0) * 1024 + iota3(1) * 128 + iota3(2)
    counted = jnp.zeros((8, 8, 128), jnp.float32)
    for j in range(t_src.shape[0]):
        counted = counted + jnp.where(flat == t_src[j], 1.0, 0.0)
    hits[...] = counted

    cross_s.wait_send()
    cross_v.start()

    receive(0)
    rates = stress_rates([f[...] for f in av], lam[...], mu[...], velocity_faces(0))
    for i in range(6):
        as_[i][...] = a1[i] - rates[i]
    send_stress(1, [f[...] for f in as_])
    bx[0] = unpack_columns(r_xl[0], 1, 0)
    bx[1] = unpack_columns(r_xr[0], 2, 127)

    cross_s.wait_recv()
    relay_s.start()
    cross_v.wait_recv()
    relay_v.start()

    for name in ("peer", "slot"):
        loads[name].wait()
    pair_s.wait_recv()
    relay_s.wait_recv()
    where_is = [t_peer[gz, p] * 8 + t_slot[gz, p] for p in range(8)]
    for p in range(8):
        fs[:, p] = gath_s[where_is[p]].astype(jnp.float32)
    forward_edges(0)
    pair_v.wait_recv()
    relay_v.wait_recv()
    for p in range(8):
        fv[:, p] = gath_v[where_is[p]].astype(jnp.float32)
    forward_faces(0)

    receive(1)
    rates = velocity_rates([f[...] for f in as_], buoy[...], stress_faces(1))
    for i in range(3):
        av[i][...] = av[i][...] - rates[i]
    send_velocity(2, [f[...] for f in av])
    for i in range(3):
        a0[i] = a0[i] + as_[i][...]
    for i in range(3, 6):
        a0[i] = as_[i][...]

    forward_receive(0)
    rates = forward_step(0)
    pulse = hits[...] * t_wav[t_plan[0]]
    for i in range(3):
        fs[i] = fs[i] + rates[i] + pulse
    for i in range(3, 6):
        fs[i] = fs[i] + rates[i]
    forward_edges(1)
    forward_faces(1)

    receive(2)
    rates = stress_rates([f[...] for f in av], lam[...], mu[...], velocity_faces(2))
    for i in range(6):
        as_[i][...] = a0[i] - rates[i]
    send_stress(3, [f[...] for f in as_])

    def image(s, a):
        by_lambda = (s[0] + s[1] + s[2]) * (a[0] + a[1] + a[2])
        by_mu = s[0] * a[0] + s[1] * a[1] + s[2] * a[2] + 2.0 * (s[3] * a[3] + s[4] * a[4] + s[5] * a[5])
        return by_lambda, by_mu

    by_lambda, by_mu = image(fs, a0)
    il_out[...] = by_lambda
    im_out[...] = by_mu

    receive(3)
    rates = velocity_rates([f[...] for f in as_], buoy[...], stress_faces(3))
    for i in range(3):
        adj_out[i] = av[i][...] - rates[i]
    for i in range(6):
        adj_out[3 + i] = as_[i][...]
    sent(3)
    for copy in (cross_v, pair_s, pair_v, relay_s, relay_v):
        copy.wait_send()

    forward_receive(1)
    rates = forward_step(1)
    pulse = hits[...] * t_wav[t_plan[1]]
    last = [fs[i] + rates[i] + pulse for i in range(3)] + [fs[i] + rates[i] for i in range(3, 6)]
    by_lambda, by_mu = image(last, a1)
    il_out[...] += by_lambda
    im_out[...] += by_mu
    forward_sent(1)


def write_out(adj, il, im, adj_out, il_out, im_out, sem):
    copies = [
        pltpu.make_async_copy(src, dst, sem.at[n])
        for n, (src, dst) in enumerate(((adj, adj_out), (il, il_out), (im, im_out)))
    ]
    for copy in copies:
        copy.start()
    for copy in copies:
        copy.wait()


def solution(mesh):
    sizes = (mesh.shape["gx"], mesh.shape["gy"], mesh.shape["gz"])
    f32, i32, bf16 = jnp.float32, jnp.int32, jnp.bfloat16
    brick = (8, 8, 128)

    def on_device(*args):
        nt, nrec = args[10].shape[-2:]
        nsrc = args[7].shape[-1]
        vmem = pltpu.VMEM
        scratch = [
            vmem((3,) + brick, f32),
            vmem((1, nrec), i32),
            vmem((nt, nrec), f32),
            pltpu.SMEM((4, 8), i32),
            pltpu.SMEM((4, 8), i32),
            pltpu.SMEM((nsrc,), i32),
            pltpu.SMEM((nt,), f32),
            pltpu.SMEM((STEPS,), i32),
            vmem((32, 6, 8, 128), bf16),
            vmem((32, 3, 8, 128), bf16),
            vmem((3,) + brick, f32),
            vmem((6,) + brick, f32),
            vmem((9,) + brick, f32),
            vmem((6,) + brick, f32),
            vmem((6,) + brick, f32),
            vmem((2,) + brick, f32),
            vmem(brick, f32),
        ]
        row, tile = (8, 1, 128), (8, 128)
        for _ in range(2):
            scratch += [vmem((4,) + tile, f32)] * 2 + [vmem((4, 3) + row, f32)] * 2 + [vmem((4, 3) + tile, f32)] * 2
        for down_y, down_z in ((5, 7), (3, 3)):
            received = down_y == 3
            scratch += [vmem((2,) + tile, f32)] * 2
            scratch += [vmem((2, 3 if received else 5) + row, f32), vmem((2, 3) + row, f32)]
            scratch += [vmem((2, 3 if received else 7) + tile, f32), vmem((2, 3) + tile, f32)]
        for shape in (row, tile, tile):
            scratch += [vmem((2, fields) + shape, f32) for fields in (1, 2, 1, 1)]
        dma = pltpu.SemaphoreType.DMA
        scratch += [dma((11,)), dma((6,)), dma((2, 6)), dma((18,)), dma((2, 18)), dma((6,)), dma((6,))]
        shapes = ((9,) + brick, brick, brick)
        results = pl.pallas_call(
            functools.partial(kernel, sizes),
            out_shape=tuple(pltpu.VMEM(shape, f32) for shape in shapes),
            in_specs=[pl.BlockSpec(memory_space=pl.ANY)] * 12,
            out_specs=(pl.BlockSpec(memory_space=pltpu.VMEM),) * 3,
            scratch_shapes=scratch,
            compiler_params=pltpu.CompilerParams(
                collective_id=0, has_side_effects=True
            ),
            name="window",
        )(*args)
        return pl.pallas_call(
            write_out,
            out_shape=tuple(jax.ShapeDtypeStruct(shape, f32) for shape in shapes),
            in_specs=[pl.BlockSpec(memory_space=pltpu.VMEM)] * 3,
            out_specs=(pl.BlockSpec(memory_space=pl.ANY),) * 3,
            scratch_shapes=[pltpu.SemaphoreType.DMA((3,))],
            compiler_params=pltpu.CompilerParams(vmem_limit_bytes=16 << 20),
            name="write_out",
        )(*results)

    return jax.shard_map(
        on_device,
        mesh=mesh,
        in_specs=(
            P("gz", None, None, "gy", "gx"),
            P("gx", "gy", None, None),
            P("gx", "gy", None, None),
            P(None, "gz", "gy", "gx"),
            P("gz", "gy", "gx"),
            P("gz", "gy", "gx"),
            P("gz", "gy", "gx"),
            P("gz", "gy", "gx", None),
            P(),
            P("gz", "gy", "gx", None),
            P("gz", "gy", "gx", None, None),
            P(),
        ),
        out_specs=(P(None, "gz", "gy", "gx"), P("gz", "gy", "gx"), P("gz", "gy", "gx")),
        check_vma=False,
    )
```

```python
import functools

import jax
import jax.numpy as jnp
from jax import lax
from jax.experimental import pallas as pl
from jax.experimental.pallas import tpu as pltpu
from jax.sharding import PartitionSpec as P

MESH = pl.DeviceIdType.MESH
STEPS = 2
CAP = 5

GREETED = ((1, 0, 0), (-1, 0, 0), (0, 1, 0), (0, -1, 0))


def iota3(dim):
    return lax.broadcasted_iota(jnp.int32, (8, 8, 128), dim)


def iota2(dim):
    return lax.broadcasted_iota(jnp.int32, (8, 128), dim)


def pack_columns(fields, lane):
    lanes = iota2(1)
    packed = jnp.zeros((8, 128), jnp.float32)
    for number, field in enumerate(fields):
        for z in range(8):
            at = number * 8 + z
            moved = pltpu.roll(field[z], (at - lane) % 128, 1)
            packed = jnp.where(lanes == at, moved, packed)
    return packed


def unpack_columns(packed, number, lane):
    return jnp.stack([pltpu.roll(packed, (lane - number * 8 - z) % 128, 1) for z in range(8)])


def behind_x(f, face):
    return f - jnp.where(iota3(2) == 0, face, pltpu.roll(f, 1, 2))


def ahead_x(f, face):
    return jnp.where(iota3(2) == 127, face, pltpu.roll(f, 127, 2)) - f


def behind_y(f, face):
    return f - jnp.where(iota3(1) == 0, jnp.broadcast_to(face, (8, 8, 128)), pltpu.roll(f, 1, 1))


def ahead_y(f, face):
    return jnp.where(iota3(1) == 7, jnp.broadcast_to(face, (8, 8, 128)), pltpu.roll(f, 7, 1)) - f


def behind_z(f, face):
    return f - jnp.concatenate([face[None], f[:7]], axis=0)


def ahead_z(f, face):
    return jnp.concatenate([f[1:], face[None]], axis=0) - f


def velocity_rates(s, b, h):
    rx = b * (ahead_x(s[0], h["xr", 0]) + behind_y(s[3], h["yl", 3]) + behind_z(s[4], h["zl", 4]))
    ry = b * (behind_x(s[3], h["xl", 3]) + ahead_y(s[1], h["yr", 1]) + behind_z(s[5], h["zl", 5]))
    rz = b * (behind_x(s[4], h["xl", 4]) + behind_y(s[5], h["yl", 5]) + ahead_z(s[2], h["zr", 2]))
    return rx, ry, rz


def stress_rates(v, lam, mu, h):
    exx, eyy, ezz = behind_x(v[0], h["xl", 0]), behind_y(v[1], h["yl", 1]), behind_z(v[2], h["zl", 2])
    spread = lam * (exx + eyy + ezz)
    twice = 2.0 * mu
    return (
        spread + twice * exx,
        spread + twice * eyy,
        spread + twice * ezz,
        mu * (ahead_y(v[0], h["yr", 0]) + ahead_x(v[1], h["xr", 1])),
        mu * (ahead_z(v[0], h["zr", 0]) + ahead_x(v[2], h["xr", 2])),
        mu * (ahead_z(v[1], h["zr", 1]) + ahead_y(v[2], h["yr", 2])),
    )


class Zeros:
    def __getitem__(self, key):
        side = key[0]
        shape = (8, 1, 128) if side[0] == "y" else (8, 128)
        return jnp.zeros((8, 8, 128) if side[0] == "x" else shape, jnp.float32)


def kernel(
    sizes,
    store,
    hpeer,
    hslot,
    adj_in,
    lam_in,
    mu_in,
    buoy_in,
    src_in,
    wav_in,
    rec_in,
    tr_in,
    plan_in,
    adj_out,
    il_out,
    im_out,
    params,
    rec,
    traces,
    t_peer,
    t_slot,
    t_src,
    t_wav,
    t_plan,
    own_s,
    own_v,
    stage_s,
    stage_v,
    got_s,
    got_v,
    fv,
    fs,
    adj,
    a1,
    a0,
    bx,
    mx,
    lx,
    hits,
    s_xl,
    s_xr,
    s_yl,
    s_yr,
    s_zl,
    s_zr,
    r_xl,
    r_xr,
    r_yl,
    r_yr,
    r_zl,
    r_zr,
    f_xl,
    f_xr,
    f_yl,
    f_yr,
    f_zl,
    f_zr,
    g_xl,
    g_xr,
    g_yl,
    g_yr,
    g_zl,
    g_zr,
    c_xl,
    c_xr,
    c_yl,
    c_yr,
    c_zl,
    c_zr,
    d_xl,
    d_xr,
    d_yl,
    d_yr,
    d_zl,
    d_zr,
    vxy_pm,
    vxy_mp,
    vxz_pm,
    vxz_mp,
    vyz_pm,
    vyz_mp,
    exy_mm,
    exy_pp,
    exy_pm,
    exy_mp,
    exz_mm,
    exz_pp,
    exz_pm,
    exz_mp,
    eyz_mm,
    eyz_pp,
    eyz_pm,
    eyz_mp,
    in_sem,
    send_sem,
    recv_sem,
    asend_sem,
    arecv_sem,
    fsend_sem,
    frecv_sem,
    rs_send,
    rs_recv,
    ready,
):
    count = dict(zip(("gx", "gy", "gz"), sizes))
    index = {axis: lax.axis_index(axis) for axis in ("gx", "gy", "gz")}
    gz = index["gz"]

    def exists(step):
        found = None
        for axis, d in zip(("gx", "gy", "gz"), step):
            if d:
                here = index[axis] < count[axis] - 1 if d > 0 else index[axis] > 0
                found = here if found is None else jnp.logical_and(found, here)
        return found

    def at(step):
        return {axis: index[axis] + d for axis, d in zip(("gx", "gy", "gz"), step) if d}

    barrier = pltpu.get_barrier_semaphore()

    def greet(where):
        pl.semaphore_signal(barrier, inc=1, device_id=where, device_id_type=MESH)

    around = jnp.int32(0)
    for step in GREETED:

        @pl.when(exists(step))
        def _():
            greet(at(step))

        around = around + exists(step).astype(jnp.int32)
    for d in (1, 2, 3):
        greet({"gz": lax.rem(gz + d, 4)})

    def local(src, dst, n):
        return pltpu.make_async_copy(src, dst, in_sem.at[n])

    loads = dict(
        peer=local(hpeer.at[0, 0], t_peer, 7),
        slot=local(hslot.at[0, 0], t_slot, 8),
        own_s=local(store.at[:, pl.ds(3, 6), 0], own_s, 9),
        own_v=local(store.at[:, pl.ds(0, 3), 0], own_v, 10),
        adj=local(adj_in, adj, 0),
        lam=local(lam_in, params.at[0], 1),
        mu=local(mu_in, params.at[1], 1),
        buoy=local(buoy_in, params.at[2], 1),
        rec=local(rec_in.at[0, 0], rec, 2),
        traces=local(tr_in.at[0, 0, 0], traces, 3),
        plan=local(plan_in, t_plan, 4),
        wav=local(wav_in, t_wav, 5),
        src=local(src_in.at[0, 0, 0], t_src, 6),
    )
    for copy in loads.values():
        copy.start()

    def edges(e):
        return (
            (exy_mm, (1, 1, 0), f_yr.at[e, pl.ds(0, 1)]),
            (exy_pp, (-1, -1, 0), f_yl.at[e, pl.ds(2, 2)]),
            (exy_pm, (-1, 1, 0), f_yr.at[e, pl.ds(1, 1)]),
            (exy_mp, (1, -1, 0), f_yl.at[e, pl.ds(4, 1)]),
            (exz_mm, (1, 0, 1), f_zr.at[e, pl.ds(0, 1)]),
            (exz_pp, (-1, 0, -1), f_zl.at[e, pl.ds(2, 2)]),
            (exz_pm, (-1, 0, 1), f_zr.at[e, pl.ds(1, 1)]),
            (exz_mp, (1, 0, -1), f_zl.at[e, pl.ds(6, 1)]),
            (eyz_mm, (0, 1, 1), f_zr.at[e, pl.ds(1, 1)]),
            (eyz_pp, (0, -1, -1), f_zl.at[e, pl.ds(4, 2)]),
            (eyz_pm, (0, -1, 1), f_zr.at[e, pl.ds(0, 1)]),
            (eyz_mp, (0, 1, -1), f_zl.at[e, pl.ds(6, 1)]),
        )

    adjoint_messages = (
        (d_xl, (1, 0, 0), c_xr),
        (d_xr, (-1, 0, 0), c_xl),
        (d_yl, (0, 1, 0), c_yr),
        (d_yr, (0, -1, 0), c_yl),
        (d_zl, (0, 0, 1), c_zr),
        (d_zr, (0, 0, -1), c_zl),
        (vxy_pm, (-1, 1, 0), c_yr.at[0]),
        (vxy_mp, (1, -1, 0), c_yl.at[0]),
        (vxz_pm, (-1, 0, 1), c_zr.at[0]),
        (vxz_mp, (1, 0, -1), c_zl.at[0]),
        (vyz_pm, (0, -1, 1), c_zr.at[0]),
        (vyz_mp, (0, 1, -1), c_zl.at[1]),
    )

    def back(step):
        return tuple(-d for d in step)

    for step, refs in (
        ((-1, 0, 0), (r_xl, g_xl, d_xl)),
        ((1, 0, 0), (r_xr, g_xr, d_xr)),
        ((0, -1, 0), (r_yl, g_yl, d_yl)),
        ((0, 1, 0), (r_yr, g_yr, d_yr)),
        ((0, 0, -1), (r_zl, g_zl, d_zl)),
        ((0, 0, 1), (r_zr, g_zr, d_zr)),
        *((back(step), (ref,)) for ref, step, _ in edges(0)),
        *((back(step), (ref,)) for ref, step, _ in adjoint_messages[6:]),
    ):

        @pl.when(jnp.logical_not(exists(step)))
        def _():
            for ref in refs:
                ref[...] = jnp.zeros(ref.shape, jnp.float32)

    lam, mu, buoy = params.at[0], params.at[1], params.at[2]
    av, as_ = [adj.at[i] for i in range(3)], [adj.at[3 + i] for i in range(6)]

    ends = (
        ((1, 0, 0), s_xr, r_xl),
        ((-1, 0, 0), s_xl, r_xr),
        ((0, 1, 0), s_yr, r_yl),
        ((0, -1, 0), s_yl, r_yr),
        ((0, 0, 1), s_zr, r_zl),
        ((0, 0, -1), s_zl, r_zr),
    )

    def face(r, d, fields):
        step, source, target = ends[d]
        if d < 2:
            src, dst = source.at[r], target.at[r]
        else:
            src, dst = source.at[r, pl.ds(0, fields)], target.at[r, pl.ds(0, fields)]
        copy = pltpu.make_async_remote_copy(
            src_ref=src,
            dst_ref=dst,
            send_sem=send_sem.at[d],
            recv_sem=recv_sem.at[r % 2, d],
            device_id=at(step),
            device_id_type=MESH,
        )
        return copy, exists(step), exists(back(step))

    COUNTS = ((3, 5), (2, 1))

    def sent(r):
        for d in range(6):
            copy, goes, _ = face(r, d, COUNTS[r][d % 2])

            @pl.when(goes)
            def _():
                copy.wait_send()

    def fill_faces(r, up, down):
        (xu, yu, zu), (xd, yd, zd) = up, down
        s_xr[r] = pack_columns(xu, 127)
        s_xl[r] = pack_columns(xd, 0)
        for i, f in enumerate(zu):
            s_zr[r, i] = f[7]
        for i, f in enumerate(zd):
            s_zl[r, i] = f[0]
        for i, f in enumerate(yu):
            s_yr[r, i] = f[:, 7:8, :]
        for i, f in enumerate(yd):
            s_yl[r, i] = f[:, 0:1, :]

    def start_faces(r):
        for d in (0, 1, 4, 5, 2, 3):
            copy, goes, _ = face(r, d, COUNTS[r][d % 2])

            @pl.when(goes)
            def _():
                copy.start()

    def fill_velocity():
        v, b, l, m = [f[...] for f in av], buoy[...], lam[...], mu[...]
        more, most = (b, m), (b, l, m)
        fill_faces(
            0,
            ((v[0], *more), (v[1], *more), (v[2], *more)),
            ((v[1], v[2], *most), (v[0], v[2], *most), (v[0], v[1], *most)),
        )

    def send_velocity(r):
        start_faces(r)

    def send_stress(r, s):
        sent(r - 1)
        fill_faces(r, ((s[3], s[4]), (s[3], s[5]), (s[4], s[5])), ((s[0],), (s[1],), (s[2],)))
        start_faces(r)

    for name in ("peer", "slot", "own_s"):
        loads[name].wait()
    slots = []
    for d in range(4):
        brick = lax.rem(gz + d, 4)
        listed, shift = jnp.int32(0), jnp.int32(0)
        for p in range(8):
            held = t_peer[brick, p] == gz
            listed = jnp.where(held, listed + lax.shift_left(t_slot[brick, p], shift), listed)
            shift = jnp.where(held, shift + 3, shift)
        slots.append([lax.bitwise_and(lax.shift_right_logical(listed, 3 * j), 7) for j in range(CAP)])

    def stage(own, staged, got):
        for d in (2, 1, 3, 0):
            for j in range(CAP):
                if d:
                    staged[(d - 1) * CAP + j] = own[slots[d][j]]
                else:
                    got[3 * CAP + j] = own[slots[d][j]]

    def restore(staged, got, n):
        for d in (2, 1, 3):
            rows = pl.ds((d - 1) * CAP, CAP)
            pltpu.make_async_remote_copy(
                src_ref=staged.at[rows],
                dst_ref=got.at[rows],
                send_sem=rs_send.at[n],
                recv_sem=rs_recv.at[n],
                device_id={"gz": lax.rem(gz + d, 4)},
                device_id_type=MESH,
            ).start()

    def restored(got, n):
        rows = got.at[pl.ds(0, 3 * CAP)]
        pltpu.make_async_copy(rows, rows, rs_recv.at[n]).wait()

    where_is, seen = [], jnp.int32(0)
    for p in range(8):
        holder = t_peer[gz, p]
        at_digit = holder * 4
        before = lax.bitwise_and(lax.shift_right_logical(seen, at_digit), 15)
        where_is.append(lax.bitwise_and(gz - holder + 3, 3) * CAP + jnp.minimum(before, CAP - 1))
        seen = seen + lax.shift_left(jnp.int32(1), at_digit)

    stage(own_s, stage_s, got_s)
    loads["adj"].wait()
    pltpu.make_async_copy(params, params, in_sem.at[1]).wait()
    fill_velocity()
    pl.semaphore_wait(barrier, around + 3)
    send_velocity(0)
    restore(stage_s, got_s, 0)

    for step in GREETED:

        @pl.when(exists(step))
        def _():
            pl.semaphore_signal(ready, inc=1, device_id=at(step), device_id_type=MESH)

    loads["own_v"].wait()
    stage(own_v, stage_v, got_v)

    def receive(r):
        for d in range(6):
            copy, _, comes = face(r, d, COUNTS[r][d % 2])

            @pl.when(comes)
            def _():
                copy.wait_recv()

    def stress_faces(r):
        xl, xr = r_xl[r], r_xr[r]
        return {
            ("xr", 0): unpack_columns(xr, 0, 127),
            ("xl", 3): unpack_columns(xl, 0, 0),
            ("xl", 4): unpack_columns(xl, 1, 0),
            ("yl", 3): r_yl[r, 0],
            ("yl", 5): r_yl[r, 1],
            ("yr", 1): r_yr[r, 0],
            ("zl", 4): r_zl[r, 0],
            ("zl", 5): r_zl[r, 1],
            ("zr", 2): r_zr[r, 0],
        }

    def velocity_faces(r):
        xl, xr = r_xl[r], r_xr[r]
        return {
            ("xl", 0): unpack_columns(xl, 0, 0),
            ("xr", 1): unpack_columns(xr, 0, 127),
            ("xr", 2): unpack_columns(xr, 1, 127),
            ("yl", 1): r_yl[r, 0],
            ("yr", 0): r_yr[r, 0],
            ("yr", 2): r_yr[r, 1],
            ("zl", 2): r_zl[r, 0],
            ("zr", 0): r_zr[r, 0],
            ("zr", 1): r_zr[r, 1],
        }

    fends = (
        (g_xl, (1, 0, 0), f_xr),
        (g_xr, (-1, 0, 0), f_xl),
        (g_yl, (0, 1, 0), f_yr),
        (g_yr, (0, -1, 0), f_yl),
        (g_zl, (0, 0, 1), f_zr),
        (g_zr, (0, 0, -1), f_zl),
    )

    def message(e, n):
        if n < 6:
            target, step, source = fends[n]
            src = source.at[e] if n < 2 else source.at[e, pl.ds(0, 3)]
        else:
            target, step, src = edges(e)[n - 6]
        copy = pltpu.make_async_remote_copy(
            src_ref=src,
            dst_ref=target.at[e],
            send_sem=fsend_sem.at[n],
            recv_sem=frecv_sem.at[e, n],
            device_id=at(step),
            device_id_type=MESH,
        )
        return copy, exists(step), exists(back(step))

    def forward_start(e, n):
        copy, goes, _ = message(e, n)

        @pl.when(goes)
        def _():
            copy.start()

    def forward_sent(e):
        for n in range(18):
            copy, goes, _ = message(e, n)

            @pl.when(goes)
            def _():
                copy.wait_send()

    def forward_receive(e):
        for n in range(18):
            copy, _, comes = message(e, n)

            @pl.when(comes)
            def _():
                copy.wait_recv()

    def forward_edges(e):
        if e > 0:
            forward_sent(e - 1)
        f_yr[e, 0] = fs[3, :, 7:8, :]
        f_yr[e, 1] = fs[5, :, 7:8, :]
        for i, f in ((2, 1), (3, 0), (4, 4)):
            f_yl[e, i] = fs[f, :, 0:1, :]
        for n in (6, 7, 8, 9):
            forward_start(e, n)
        f_zr[e, 0] = fs[4, 7]
        f_zr[e, 1] = fs[5, 7]
        for i, f in ((2, 2), (3, 0), (4, 2), (5, 1), (6, 3)):
            f_zl[e, i] = fs[f, 0]
        for n in range(10, 18):
            forward_start(e, n)

    def forward_faces(e):
        rates = velocity_rates([fs[i] for i in range(6)], buoy[...], Zeros())
        for i in range(3):
            fv[i] = fv[i] + rates[i]
        f_xr[e] = pack_columns((fs[3], fs[4], fv[0]), 127)
        f_xl[e] = pack_columns((fs[0], fv[1], fv[2]), 0)
        forward_start(e, 0)
        forward_start(e, 1)
        f_zr[e, 2] = fv[2, 7]
        f_zl[e, 0] = fv[0, 0]
        f_zl[e, 1] = fv[1, 0]
        forward_start(e, 4)
        forward_start(e, 5)
        f_yr[e, 2] = fv[1, :, 7:8, :]
        f_yl[e, 0] = fv[0, :, 0:1, :]
        f_yl[e, 1] = fv[2, :, 0:1, :]
        forward_start(e, 2)
        forward_start(e, 3)

    def forward_step(e):
        xl, xr = g_xl[e], g_xr[e]
        lane3, row3 = iota3(2), iota3(1)
        lane2, row2 = iota2(1), iota2(0)
        z1 = lax.broadcasted_iota(jnp.int32, (8, 1, 128), 0)
        lane1 = lax.broadcasted_iota(jnp.int32, (8, 1, 128), 2)

        def layer(at_z, tile, like):
            return jnp.where(iota3(0) == at_z, tile[None], 0.0) if like == 3 else jnp.where(z1 == at_z, tile, 0.0)

        def first_lane(f, axis):
            return pltpu.roll(f, 1, axis)

        def last_lane(f, axis):
            return pltpu.roll(f, 127, axis)

        mm, pp = first_lane(exy_mm[e, 0], 2), (last_lane(exy_pp[e, 0], 2), last_lane(exy_pp[e, 1], 2))
        pm, mp = last_lane(exy_pm[e, 0], 2), first_lane(exy_mp[e, 0], 2)
        zmm, zpp = first_lane(exz_mm[e, 0], 1), (last_lane(exz_pp[e, 0], 1), last_lane(exz_pp[e, 1], 1))
        zpm, zmp = last_lane(exz_pm[e, 0], 1), first_lane(exz_mp[e, 0], 1)
        all3 = (8, 8, 128)
        nothing = jnp.zeros(all3, jnp.float32)

        def row(at_y, face):
            return jnp.where(row3 == at_y, jnp.broadcast_to(face, all3), nothing)

        b = buoy[...]
        h = {}
        h["xl", 0] = unpack_columns(xl, 2, 0) + bx[0] * (fs[0] - row(0, mm) - layer(0, zmm, 3))
        h["xr", 1] = unpack_columns(xr, 1, 127) + bx[1] * (row(7, pp[0]) - fs[3] - layer(0, zpm, 3))
        h["xr", 2] = unpack_columns(xr, 2, 127) + bx[1] * (layer(7, zpp[0], 3) - fs[4] - row(0, pm))

        def y_layer(at_z, tile, at_y):
            return jnp.where(z1 == at_z, jnp.broadcast_to(tile[at_y : at_y + 1, :][None], (8, 1, 128)), 0.0)

        bym, byp = r_yl[0, 1], r_yr[0, 2]
        h["yl", 1] = g_yl[e, 2] + bym * (
            fs[1, :, 0:1, :] - jnp.where(lane1 == 0, mm, 0.0) - y_layer(0, eyz_mm[e, 0], 7)
        )
        h["yr", 0] = g_yr[e, 0] + byp * (
            jnp.where(lane1 == 127, pp[1], 0.0) - fs[3, :, 7:8, :] - y_layer(0, eyz_pm[e, 0], 0)
        )
        h["yr", 2] = g_yr[e, 1] + byp * (
            y_layer(7, eyz_pp[e, 0], 0) - fs[5, :, 7:8, :] - jnp.where(lane1 == 0, mp, 0.0)
        )

        def y_edge(tile, at_y, from_y):
            return jnp.where(row2 == at_y, jnp.broadcast_to(tile[from_y : from_y + 1, :], (8, 128)), 0.0)

        bzm, bzp = r_zl[0, 1], r_zr[0, 2]
        h["zl", 2] = g_zl[e, 2] + bzm * (fs[2, 0] - jnp.where(lane2 == 0, zmm, 0.0) - y_edge(eyz_mm[e, 0], 0, 7))
        h["zr", 0] = g_zr[e, 0] + bzp * (
            jnp.where(lane2 == 127, zpp[1], 0.0) - fs[4, 7] - y_edge(eyz_mp[e, 0], 0, 7)
        )
        h["zr", 1] = g_zr[e, 1] + bzp * (
            y_edge(eyz_pp[e, 1], 7, 0) - fs[5, 7] - jnp.where(lane2 == 0, zmp, 0.0)
        )

        fv[0] = fv[0] + b * (jnp.where(lane3 == 127, unpack_columns(xr, 0, 127), 0.0) - row(0, g_yl[e, 0]))
        fv[1] = fv[1] + b * (row(7, g_yr[e, 2]) - jnp.where(lane3 == 0, unpack_columns(xl, 0, 0), 0.0))
        fv[2] = fv[2] - b * (jnp.where(lane3 == 0, unpack_columns(xl, 1, 0), 0.0) + row(0, g_yl[e, 1]))
        fv[0, 0] = fv[0, 0] - buoy[0] * g_zl[e, 0]
        fv[1, 0] = fv[1, 0] - buoy[0] * g_zl[e, 1]
        fv[2, 7] = fv[2, 7] + buoy[7] * g_zr[e, 2]
        return stress_rates([fv[i] for i in range(3)], lam[...], mu[...], h)

    def adjoint_message(n):
        target, step, source = adjoint_messages[n]
        copy = pltpu.make_async_remote_copy(
            src_ref=source,
            dst_ref=target,
            send_sem=asend_sem.at[n],
            recv_sem=arecv_sem.at[n],
            device_id=at(step),
            device_id_type=MESH,
        )
        return copy, exists(step), exists(back(step))

    def adjoint_start(*which):
        for n in which:
            copy, goes, _ = adjoint_message(n)

            @pl.when(goes)
            def _():
                copy.start()

    def adjoint_sent():
        for n in range(12):
            copy, goes, _ = adjoint_message(n)

            @pl.when(goes)
            def _():
                copy.wait_send()

    def adjoint_receive():
        for n in range(12):
            copy, _, comes = adjoint_message(n)

            @pl.when(comes)
            def _():
                copy.wait_recv()

    def adjoint_send():
        c_yr[0] = av[1][:, 7:8, :]
        c_yl[0] = av[0][:, 0:1, :]
        c_yl[1] = av[2][:, 0:1, :]
        adjoint_start(6, 7)
        c_zr[0] = av[2][7]
        c_zl[0] = av[0][0]
        c_zl[1] = av[1][0]
        adjoint_start(8, 9, 10, 11)
        v = [f[...] for f in av]
        rates = stress_rates(v, lam[...], mu[...], Zeros())
        s = [a0[i] - rates[i] for i in range(6)]
        c_xr[...] = pack_columns((v[0], s[3], s[4]), 127)
        c_xl[...] = pack_columns((v[1], v[2], s[0]), 0)
        adjoint_start(0, 1)
        c_zr[1] = s[4][7]
        c_zr[2] = s[5][7]
        c_zl[2] = s[2][0]
        adjoint_start(4, 5)
        c_yr[1] = s[3][:, 7:8, :]
        c_yr[2] = s[5][:, 7:8, :]
        c_yl[2] = s[1][:, 0:1, :]
        adjoint_start(2, 3)

    def adjoint_step():
        v = [f[...] for f in av]
        xl, xr = d_xl[...], d_xr[...]
        lane2, row2 = iota2(1), iota2(0)
        all3 = (8, 8, 128)
        z1 = lax.broadcasted_iota(jnp.int32, (8, 1, 128), 0)
        lane1 = lax.broadcasted_iota(jnp.int32, (8, 1, 128), 2)
        h = {
            ("xl", 0): unpack_columns(xl, 0, 0),
            ("xr", 1): unpack_columns(xr, 0, 127),
            ("xr", 2): unpack_columns(xr, 1, 127),
            ("yl", 1): d_yl[0],
            ("yr", 0): d_yr[0],
            ("yr", 2): d_yr[1],
            ("zl", 2): d_zl[0],
            ("zr", 0): d_zr[0],
            ("zr", 1): d_zr[1],
        }
        rates = stress_rates(v, lam[...], mu[...], h)
        s = [a0[i] - rates[i] for i in range(6)]

        xy_pm, xy_mp = pltpu.roll(vxy_pm[...], 127, 2), pltpu.roll(vxy_mp[...], 1, 2)
        xz_pm, xz_mp = pltpu.roll(vxz_pm[...], 127, 1), pltpu.roll(vxz_mp[...], 1, 1)

        def row(at_y, face):
            return jnp.where(iota3(1) == at_y, jnp.broadcast_to(face, all3), 0.0)

        def layer(at_z, tile):
            return jnp.where(iota3(0) == at_z, tile[None], 0.0)

        def y_layer(at_z, tile, at_y):
            return jnp.where(z1 == at_z, jnp.broadcast_to(tile[at_y : at_y + 1, :][None], (8, 1, 128)), 0.0)

        def y_edge(tile, at_y, from_y):
            return jnp.where(row2 == at_y, jnp.broadcast_to(tile[from_y : from_y + 1, :], (8, 128)), 0.0)

        both = lx[...] + 2.0 * mx[1]
        g = {}
        g["xl", 3] = unpack_columns(xl, 1, 0) - mx[0] * (v[1] + row(7, xy_mp))
        g["xl", 4] = unpack_columns(xl, 2, 0) - mx[0] * (v[2] + layer(7, xz_mp))
        g["xr", 0] = unpack_columns(xr, 2, 127) + both * v[0] + lx[...] * (row(0, xy_pm) + layer(0, xz_pm))
        mu_m, lam_p, mu_p = r_yl[0, 2], r_yr[0, 3], r_yr[0, 4]
        g["yl", 3] = d_yl[1] - mu_m * (v[0][:, 0:1, :] + jnp.where(lane1 == 127, xy_pm, 0.0))
        g["yl", 5] = d_yl[2] - mu_m * (v[2][:, 0:1, :] + y_layer(7, vyz_mp[...], 7))
        g["yr", 1] = (
            d_yr[2]
            + (lam_p + 2.0 * mu_p) * v[1][:, 7:8, :]
            + lam_p * (jnp.where(lane1 == 0, xy_mp, 0.0) + y_layer(0, vyz_pm[...], 0))
        )
        mu_m, lam_p, mu_p = r_zl[0, 2], r_zr[0, 3], r_zr[0, 4]
        g["zl", 4] = d_zl[1] - mu_m * (v[0][0] + jnp.where(lane2 == 127, xz_pm, 0.0))
        g["zl", 5] = d_zl[2] - mu_m * (v[1][0] + y_edge(vyz_pm[...], 7, 0))
        g["zr", 2] = (
            d_zr[2]
            + (lam_p + 2.0 * mu_p) * v[2][7]
            + lam_p * (jnp.where(lane2 == 0, xz_mp, 0.0) + y_edge(vyz_mp[...], 0, 7))
        )
        for i in range(6):
            adj_out[3 + i] = s[i]
        rates = velocity_rates(s, buoy[...], g)
        for i in range(3):
            adj_out[i] = v[i] - rates[i]

    for name in ("rec", "traces", "plan"):
        loads[name].wait()
    cells = rec[0]
    row_of, x_of = lax.shift_right_logical(cells, 7), lax.bitwise_and(cells, 127)
    rows = lax.broadcasted_iota(jnp.int32, (64, 64), 0)
    hit = rows == jnp.broadcast_to(row_of, (64, 64))
    samples = [jnp.broadcast_to(traces[pl.ds(t_plan[k], 1), :], (64, 64)) for k in range(STEPS)]
    left = jnp.concatenate([jnp.where(hit, samples[k], 0.0) for k in range(STEPS)], axis=0)
    columns = lax.broadcasted_iota(jnp.int32, (128, 64), 0)
    right = jnp.where(columns == jnp.broadcast_to(x_of, (128, 64)), 1.0, 0.0)
    spread = lax.dot_general(
        left, right, (((1,), (1,)), ((), ())), precision=lax.Precision.HIGHEST, preferred_element_type=jnp.float32
    )
    spread = spread.reshape(STEPS, 8, 8, 128)
    for i in range(3):
        a1[i] = as_[i][...] + spread[1]
        a0[i] = spread[0]
    for i in range(3, 6):
        a1[i] = as_[i][...]

    for name in ("wav", "src"):
        loads[name].wait()
    flat = iota3(0) * 1024 + iota3(1) * 128 + iota3(2)
    counted = jnp.zeros((8, 8, 128), jnp.float32)
    for j in range(t_src.shape[0]):
        counted = counted + jnp.where(flat == t_src[j], 1.0, 0.0)
    hits[...] = counted

    restore(stage_v, got_v, 1)

    restored(got_s, 0)
    for p in range(8):
        fs[:, p] = got_s[where_is[p]].astype(jnp.float32)
    pl.semaphore_wait(ready, around)
    forward_edges(0)
    receive(0)
    rates = stress_rates([f[...] for f in av], lam[...], mu[...], velocity_faces(0))
    for i in range(6):
        as_[i][...] = a1[i] - rates[i]
    send_stress(1, [f[...] for f in as_])
    bx[0] = unpack_columns(r_xl[0], 1, 0)
    mx[0] = unpack_columns(r_xl[0], 2, 0)
    bx[1] = unpack_columns(r_xr[0], 2, 127)
    lx[...] = unpack_columns(r_xr[0], 3, 127)
    mx[1] = unpack_columns(r_xr[0], 4, 127)

    restored(got_v, 1)
    for p in range(8):
        fv[:, p] = got_v[where_is[p]].astype(jnp.float32)
    forward_faces(0)

    receive(1)
    rates = velocity_rates([f[...] for f in as_], buoy[...], stress_faces(1))
    for i in range(3):
        av[i][...] = av[i][...] - rates[i]
    for i in range(3):
        a0[i] = a0[i] + as_[i][...]
    for i in range(3, 6):
        a0[i] = as_[i][...]
    adjoint_send()

    forward_receive(0)
    rates = forward_step(0)
    pulse = hits[...] * t_wav[t_plan[0]]
    for i in range(3):
        fs[i] = fs[i] + rates[i] + pulse
    for i in range(3, 6):
        fs[i] = fs[i] + rates[i]
    forward_edges(1)
    forward_faces(1)

    def image(s, a):
        by_lambda = (s[0] + s[1] + s[2]) * (a[0] + a[1] + a[2])
        by_mu = s[0] * a[0] + s[1] * a[1] + s[2] * a[2] + 2.0 * (s[3] * a[3] + s[4] * a[4] + s[5] * a[5])
        return by_lambda, by_mu

    by_lambda, by_mu = image(fs, a0)
    il_out[...] = by_lambda
    im_out[...] = by_mu

    adjoint_receive()
    adjoint_step()
    sent(1)
    adjoint_sent()
    for n, staged in enumerate((stage_s, stage_v)):
        pltpu.make_async_copy(staged, staged, rs_send.at[n]).wait()

    forward_receive(1)
    rates = forward_step(1)
    pulse = hits[...] * t_wav[t_plan[1]]
    last = [fs[i] + rates[i] + pulse for i in range(3)] + [fs[i] + rates[i] for i in range(3, 6)]
    by_lambda, by_mu = image(last, a1)
    il_out[...] += by_lambda
    im_out[...] += by_mu
    forward_sent(1)


def write_out(adj, il, im, adj_out, il_out, im_out, sem):
    copies = [
        pltpu.make_async_copy(src, dst, sem.at[n])
        for n, (src, dst) in enumerate(((adj, adj_out), (il, il_out), (im, im_out)))
    ]
    for copy in copies:
        copy.start()
    for copy in copies:
        copy.wait()


def solution(mesh):
    sizes = (mesh.shape["gx"], mesh.shape["gy"], mesh.shape["gz"])
    f32, i32, bf16 = jnp.float32, jnp.int32, jnp.bfloat16
    brick = (8, 8, 128)

    def on_device(*args):
        nt, nrec = args[10].shape[-2:]
        nsrc = args[7].shape[-1]
        vmem = pltpu.VMEM
        scratch = [
            vmem((3,) + brick, f32),
            vmem((1, nrec), i32),
            vmem((nt, nrec), f32),
            pltpu.SMEM((4, 8), i32),
            pltpu.SMEM((4, 8), i32),
            pltpu.SMEM((nsrc,), i32),
            pltpu.SMEM((nt,), f32),
            pltpu.SMEM((STEPS,), i32),
            vmem((8, 6, 8, 128), bf16),
            vmem((8, 3, 8, 128), bf16),
            vmem((3 * CAP, 6, 8, 128), bf16),
            vmem((3 * CAP, 3, 8, 128), bf16),
            vmem((4 * CAP, 6, 8, 128), bf16),
            vmem((4 * CAP, 3, 8, 128), bf16),
            vmem((3,) + brick, f32),
            vmem((6,) + brick, f32),
            vmem((9,) + brick, f32),
            vmem((6,) + brick, f32),
            vmem((6,) + brick, f32),
            vmem((2,) + brick, f32),
            vmem((2,) + brick, f32),
            vmem(brick, f32),
            vmem(brick, f32),
        ]
        row, tile = (8, 1, 128), (8, 128)
        for _ in range(2):
            scratch += [vmem((2,) + tile, f32)] * 2 + [vmem((2, 5) + row, f32)] * 2 + [vmem((2, 5) + tile, f32)] * 2
        for down_y, down_z in ((5, 7), (3, 3)):
            received = down_y == 3
            scratch += [vmem((2,) + tile, f32)] * 2
            scratch += [vmem((2, 3 if received else 5) + row, f32), vmem((2, 3) + row, f32)]
            scratch += [vmem((2, 3 if received else 7) + tile, f32), vmem((2, 3) + tile, f32)]
        for _ in range(2):
            scratch += [vmem(tile, f32)] * 2 + [vmem((3,) + row, f32)] * 2 + [vmem((3,) + tile, f32)] * 2
        scratch += [vmem(row, f32)] * 2 + [vmem(tile, f32)] * 4
        for shape in (row, tile, tile):
            scratch += [vmem((2, fields) + shape, f32) for fields in (1, 2, 1, 1)]
        dma = pltpu.SemaphoreType.DMA
        scratch += [dma((11,)), dma((6,)), dma((2, 6)), dma((12,)), dma((12,)), dma((18,)), dma((2, 18)), dma((2,)), dma((2,)), pltpu.SemaphoreType.REGULAR]
        shapes = ((9,) + brick, brick, brick)
        results = pl.pallas_call(
            functools.partial(kernel, sizes),
            out_shape=tuple(pltpu.VMEM(shape, f32) for shape in shapes),
            in_specs=[pl.BlockSpec(memory_space=pl.ANY)] * 12,
            out_specs=(pl.BlockSpec(memory_space=pltpu.VMEM),) * 3,
            scratch_shapes=scratch,
            compiler_params=pltpu.CompilerParams(
                collective_id=0, has_side_effects=True
            ),
            name="window",
        )(*args)
        return pl.pallas_call(
            write_out,
            out_shape=tuple(jax.ShapeDtypeStruct(shape, f32) for shape in shapes),
            in_specs=[pl.BlockSpec(memory_space=pltpu.VMEM)] * 3,
            out_specs=(pl.BlockSpec(memory_space=pl.ANY),) * 3,
            scratch_shapes=[pltpu.SemaphoreType.DMA((3,))],
            compiler_params=pltpu.CompilerParams(vmem_limit_bytes=16 << 20),
            name="write_out",
        )(*results)

    return jax.shard_map(
        on_device,
        mesh=mesh,
        in_specs=(
            P("gz", None, None, "gy", "gx"),
            P("gx", "gy", None, None),
            P("gx", "gy", None, None),
            P(None, "gz", "gy", "gx"),
            P("gz", "gy", "gx"),
            P("gz", "gy", "gx"),
            P("gz", "gy", "gx"),
            P("gz", "gy", "gx", None),
            P(),
            P("gz", "gy", "gx", None),
            P("gz", "gy", "gx", None, None),
            P(),
        ),
        out_specs=(P(None, "gz", "gy", "gx"), P("gz", "gy", "gx"), P("gz", "gy", "gx")),
        check_vma=False,
    )
```

```python
import functools

import jax
import jax.numpy as jnp
from jax import lax
from jax.experimental import pallas as pl
from jax.experimental.pallas import tpu as pltpu
from jax.sharding import PartitionSpec as P

MESH = pl.DeviceIdType.MESH
STEPS = 2
CAP = 5

GREETED = ((1, 0, 0), (-1, 0, 0), (0, 1, 0), (0, -1, 0))


def iota3(dim):
    return lax.broadcasted_iota(jnp.int32, (8, 8, 128), dim)


def iota2(dim):
    return lax.broadcasted_iota(jnp.int32, (8, 128), dim)


def pack_columns(fields, lane):
    lanes = iota2(1)
    packed = jnp.zeros((8, 128), jnp.float32)
    for number, field in enumerate(fields):
        for z in range(8):
            at = number * 8 + z
            moved = pltpu.roll(field[z], (at - lane) % 128, 1)
            packed = jnp.where(lanes == at, moved, packed)
    return packed


def unpack_columns(packed, number, lane):
    return jnp.stack([pltpu.roll(packed, (lane - number * 8 - z) % 128, 1) for z in range(8)])


def behind_x(f, face):
    return f - jnp.where(iota3(2) == 0, face, pltpu.roll(f, 1, 2))


def ahead_x(f, face):
    return jnp.where(iota3(2) == 127, face, pltpu.roll(f, 127, 2)) - f


def behind_y(f, face):
    return f - jnp.where(iota3(1) == 0, jnp.broadcast_to(face, (8, 8, 128)), pltpu.roll(f, 1, 1))


def ahead_y(f, face):
    return jnp.where(iota3(1) == 7, jnp.broadcast_to(face, (8, 8, 128)), pltpu.roll(f, 7, 1)) - f


def behind_z(f, face):
    return f - jnp.concatenate([face[None], f[:7]], axis=0)


def ahead_z(f, face):
    return jnp.concatenate([f[1:], face[None]], axis=0) - f


def velocity_rates(s, b, h):
    rx = b * (ahead_x(s[0], h["xr", 0]) + behind_y(s[3], h["yl", 3]) + behind_z(s[4], h["zl", 4]))
    ry = b * (behind_x(s[3], h["xl", 3]) + ahead_y(s[1], h["yr", 1]) + behind_z(s[5], h["zl", 5]))
    rz = b * (behind_x(s[4], h["xl", 4]) + behind_y(s[5], h["yl", 5]) + ahead_z(s[2], h["zr", 2]))
    return rx, ry, rz


def stress_rates(v, lam, mu, h):
    exx, eyy, ezz = behind_x(v[0], h["xl", 0]), behind_y(v[1], h["yl", 1]), behind_z(v[2], h["zl", 2])
    spread = lam * (exx + eyy + ezz)
    twice = 2.0 * mu
    return (
        spread + twice * exx,
        spread + twice * eyy,
        spread + twice * ezz,
        mu * (ahead_y(v[0], h["yr", 0]) + ahead_x(v[1], h["xr", 1])),
        mu * (ahead_z(v[0], h["zr", 0]) + ahead_x(v[2], h["xr", 2])),
        mu * (ahead_z(v[1], h["zr", 1]) + ahead_y(v[2], h["yr", 2])),
    )


class Zeros:
    def __getitem__(self, key):
        side = key[0]
        shape = (8, 1, 128) if side[0] == "y" else (8, 128)
        return jnp.zeros((8, 8, 128) if side[0] == "x" else shape, jnp.float32)


class Part:
    def __init__(self, kind, places):
        self.kind, self.places = kind, places

    def __getitem__(self, key):
        e, i = key if isinstance(key, tuple) else (key, 0)
        ref, first, _ = self.places[e]
        return ref[first + i]

    def at(self, e):
        ref, first, count = self.places[e]
        return ref.at[pl.ds(first, count)]


class Exchange:
    def __init__(self, e, buffers, spare, send, recv, messages, to, exists):
        self.e, self.buffers, self.spare, self.send, self.recv = e, buffers, spare, send, recv
        self.messages, self.to, self.exists = messages, to, exists

    def prepare(self):
        for part, step, _ in self.messages:
            target = part.at(self.e)
            _, first, count = part.places[self.e]
            aside = self.spare[part.kind].at[pl.ds(first, count)]

            @pl.when(jnp.logical_not(self.exists(step)))
            def _():
                zeros = self.spare[2 + part.kind].at[pl.ds(0, count)]
                pltpu.make_async_copy(zeros, aside, self.send.at[part.kind]).start()

            @pl.when(jnp.logical_not(self.exists(tuple(-d for d in step))))
            def _():
                zeros = self.spare[2 + part.kind].at[pl.ds(0, count)]
                pltpu.make_async_copy(zeros, target, self.recv.at[part.kind]).start()

    def start(self, *which):
        for n in which:
            part, step, source = self.messages[n]

            @pl.when(self.exists(step))
            def _():
                pltpu.make_async_remote_copy(
                    src_ref=source,
                    dst_ref=part.at(self.e),
                    send_sem=self.send.at[part.kind],
                    recv_sem=self.recv.at[part.kind],
                    device_id=self.to(step),
                    device_id_type=MESH,
                ).start()

    def all_of(self, sems):
        for kind, ref in enumerate(self.buffers):
            pltpu.make_async_copy(ref, ref, sems.at[kind]).wait()

    def sent(self):
        self.all_of(self.send)

    def receive(self):
        self.all_of(self.recv)


def kernel(
    sizes,
    store,
    hpeer,
    hslot,
    adj_in,
    lam_in,
    mu_in,
    buoy_in,
    src_in,
    wav_in,
    rec_in,
    tr_in,
    plan_in,
    adj_out,
    il_out,
    im_out,
    params,
    rec,
    traces,
    t_peer,
    t_slot,
    t_src,
    t_wav,
    t_plan,
    own_s,
    own_v,
    stage_s,
    stage_v,
    got_s,
    got_v,
    fv,
    fs,
    adj,
    a1,
    a0,
    bx,
    mx,
    lx,
    hits,
    s_xl,
    s_xr,
    s_yl,
    s_yr,
    s_zl,
    s_zr,
    r0_tiles,
    r0_rows,
    r1_tiles,
    r1_rows,
    f_xl,
    f_xr,
    f_yl,
    f_yr,
    f_zl,
    f_zr,
    g0_tiles,
    g0_rows,
    g1_tiles,
    g1_rows,
    c_xl,
    c_xr,
    c_yl,
    c_yr,
    c_zl,
    c_zr,
    d_tiles,
    d_rows,
    ar0_tiles,
    ar0_rows,
    ar1_tiles,
    ar1_rows,
    ad_tiles,
    ad_rows,
    ag0_tiles,
    ag0_rows,
    ag1_tiles,
    ag1_rows,
    no_tiles,
    no_rows,
    in_sem,
    send_sem,
    recv_sem,
    fsend_sem,
    frecv_sem,
    rs_send,
    rs_recv,
    ready,
):
    count = dict(zip(("gx", "gy", "gz"), sizes))
    index = {axis: lax.axis_index(axis) for axis in ("gx", "gy", "gz")}
    gz = index["gz"]

    axes = ("gx", "gy", "gz")

    def exists(step):
        found = None
        for axis, d in zip(axes, step):
            if d:
                here = index[axis] < count[axis] - 1 if d > 0 else index[axis] > 0
                found = here if found is None else jnp.logical_and(found, here)
        return found

    def at(step):
        return {axis: index[axis] + d for axis, d in zip(axes, step) if d}

    barrier = pltpu.get_barrier_semaphore()

    def greet(where):
        pl.semaphore_signal(barrier, inc=1, device_id=where, device_id_type=MESH)

    around = jnp.int32(0)
    for step in GREETED:

        @pl.when(exists(step))
        def _():
            greet(at(step))

        around = around + exists(step).astype(jnp.int32)
    for d in (1, 2, 3):
        greet({"gz": lax.rem(gz + d, 4)})

    def local(src, dst, n):
        return pltpu.make_async_copy(src, dst, in_sem.at[n])

    loads = dict(
        peer=local(hpeer.at[0, 0], t_peer, 7),
        slot=local(hslot.at[0, 0], t_slot, 8),
        own_s=local(store.at[:, pl.ds(3, 6), 0], own_s, 9),
        own_v=local(store.at[:, pl.ds(0, 3), 0], own_v, 10),
        adj=local(adj_in, adj, 0),
        lam=local(lam_in, params.at[0], 1),
        mu=local(mu_in, params.at[1], 1),
        buoy=local(buoy_in, params.at[2], 1),
        rec=local(rec_in.at[0, 0], rec, 2),
        traces=local(tr_in.at[0, 0, 0], traces, 3),
        plan=local(plan_in, t_plan, 4),
        wav=local(wav_in, t_wav, 5),
        src=local(src_in.at[0, 0, 0], t_src, 6),
    )
    for copy in loads.values():
        copy.start()

    TILES, ROWS = 0, 1
    first, second, forward0, forward1, last_one = (
        (r0_tiles, r0_rows),
        (r1_tiles, r1_rows),
        (g0_tiles, g0_rows),
        (g1_tiles, g1_rows),
        (d_tiles, d_rows),
    )

    spares = [
        (*aside, no_tiles, no_rows)
        for aside in (
            (ar0_tiles, ar0_rows),
            (ar1_tiles, ar1_rows),
            (ad_tiles, ad_rows),
            (ag0_tiles, ag0_rows),
            (ag1_tiles, ag1_rows),
        )
    ]

    def part(kind, *places):
        return Part(kind, [(buffers[kind], at_row, fields) for buffers, at_row, fields in places])

    r_xl = part(TILES, (first, 0, 1), (second, 0, 1))
    r_xr = part(TILES, (first, 1, 1), (second, 1, 1))
    r_zl = part(TILES, (first, 2, 3), (second, 2, 2))
    r_zr = part(TILES, (first, 5, 5), (second, 4, 1))
    r_yl = part(ROWS, (first, 0, 3), (second, 0, 2))
    r_yr = part(ROWS, (first, 3, 5), (second, 2, 1))

    def adjoint_exchange(r):
        up, down = ((3, 5), (2, 1))[r]
        return Exchange(
            r,
            (first, second)[r],
            spares[r],
            send_sem.at[r],
            recv_sem.at[r],
            (
                (r_xl, (1, 0, 0), s_xr.at[r]),
                (r_xr, (-1, 0, 0), s_xl.at[r]),
                (r_zl, (0, 0, 1), s_zr.at[r, pl.ds(0, up)]),
                (r_zr, (0, 0, -1), s_zl.at[r, pl.ds(0, down)]),
                (r_yl, (0, 1, 0), s_yr.at[r, pl.ds(0, up)]),
                (r_yr, (0, -1, 0), s_yl.at[r, pl.ds(0, down)]),
            ),
            at,
            exists,
        )

    def forward_part(kind, at_row, fields):
        return part(kind, (forward0, at_row, fields), (forward1, at_row, fields))

    g_xl, g_xr = forward_part(TILES, 0, 1), forward_part(TILES, 1, 1)
    g_zl, g_zr = forward_part(TILES, 2, 3), forward_part(TILES, 5, 3)
    exz_mm, exz_pp = forward_part(TILES, 8, 1), forward_part(TILES, 9, 2)
    exz_pm, exz_mp = forward_part(TILES, 11, 1), forward_part(TILES, 12, 1)
    eyz_mm, eyz_pp = forward_part(TILES, 13, 1), forward_part(TILES, 14, 2)
    eyz_pm, eyz_mp = forward_part(TILES, 16, 1), forward_part(TILES, 17, 1)
    g_yl, g_yr = forward_part(ROWS, 0, 3), forward_part(ROWS, 3, 3)
    exy_mm, exy_pp = forward_part(ROWS, 6, 1), forward_part(ROWS, 7, 2)
    exy_pm, exy_mp = forward_part(ROWS, 9, 1), forward_part(ROWS, 10, 1)

    def forward_exchange(e):
        return Exchange(
            e,
            (forward0, forward1)[e],
            spares[3 + e],
            fsend_sem.at[e],
            frecv_sem.at[e],
            (
                (g_xl, (1, 0, 0), f_xr.at[e]),
                (g_xr, (-1, 0, 0), f_xl.at[e]),
                (g_yl, (0, 1, 0), f_yr.at[e, pl.ds(0, 3)]),
                (g_yr, (0, -1, 0), f_yl.at[e, pl.ds(0, 3)]),
                (g_zl, (0, 0, 1), f_zr.at[e, pl.ds(0, 3)]),
                (g_zr, (0, 0, -1), f_zl.at[e, pl.ds(0, 3)]),
                (exy_mm, (1, 1, 0), f_yr.at[e, pl.ds(0, 1)]),
                (exy_pp, (-1, -1, 0), f_yl.at[e, pl.ds(2, 2)]),
                (exy_pm, (-1, 1, 0), f_yr.at[e, pl.ds(1, 1)]),
                (exy_mp, (1, -1, 0), f_yl.at[e, pl.ds(4, 1)]),
                (exz_mm, (1, 0, 1), f_zr.at[e, pl.ds(0, 1)]),
                (exz_pp, (-1, 0, -1), f_zl.at[e, pl.ds(2, 2)]),
                (exz_pm, (-1, 0, 1), f_zr.at[e, pl.ds(1, 1)]),
                (exz_mp, (1, 0, -1), f_zl.at[e, pl.ds(6, 1)]),
                (eyz_mm, (0, 1, 1), f_zr.at[e, pl.ds(1, 1)]),
                (eyz_pp, (0, -1, -1), f_zl.at[e, pl.ds(4, 2)]),
                (eyz_pm, (0, -1, 1), f_zr.at[e, pl.ds(0, 1)]),
                (eyz_mp, (0, 1, -1), f_zl.at[e, pl.ds(6, 1)]),
            ),
            at,
            exists,
        )

    d_xl, d_xr = part(TILES, (last_one, 0, 1)), part(TILES, (last_one, 1, 1))
    d_zl, d_zr = part(TILES, (last_one, 2, 3)), part(TILES, (last_one, 5, 3))
    vxz_pm, vxz_mp = part(TILES, (last_one, 8, 1)), part(TILES, (last_one, 9, 1))
    vyz_pm, vyz_mp = part(TILES, (last_one, 10, 1)), part(TILES, (last_one, 11, 1))
    d_yl, d_yr = part(ROWS, (last_one, 0, 3)), part(ROWS, (last_one, 3, 3))
    vxy_pm, vxy_mp = part(ROWS, (last_one, 6, 1)), part(ROWS, (last_one, 7, 1))
    last_exchange = Exchange(
        0,
        last_one,
        spares[2],
        send_sem.at[2],
        recv_sem.at[2],
        (
            (d_xl, (1, 0, 0), c_xr),
            (d_xr, (-1, 0, 0), c_xl),
            (d_yl, (0, 1, 0), c_yr),
            (d_yr, (0, -1, 0), c_yl),
            (d_zl, (0, 0, 1), c_zr),
            (d_zr, (0, 0, -1), c_zl),
            (vxy_pm, (-1, 1, 0), c_yr.at[pl.ds(0, 1)]),
            (vxy_mp, (1, -1, 0), c_yl.at[pl.ds(0, 1)]),
            (vxz_pm, (-1, 0, 1), c_zr.at[pl.ds(0, 1)]),
            (vxz_mp, (1, 0, -1), c_zl.at[pl.ds(0, 1)]),
            (vyz_pm, (0, -1, 1), c_zr.at[pl.ds(0, 1)]),
            (vyz_mp, (0, 1, -1), c_zl.at[pl.ds(1, 1)]),
        ),
        at,
        exists,
    )

    lam, mu, buoy = params.at[0], params.at[1], params.at[2]
    av, as_ = [adj.at[i] for i in range(3)], [adj.at[3 + i] for i in range(6)]

    def fill_faces(r, up, down):
        (xu, yu, zu), (xd, yd, zd) = up, down
        s_xr[r, 0] = pack_columns(xu, 127)
        s_xl[r, 0] = pack_columns(xd, 0)
        for i, f in enumerate(zu):
            s_zr[r, i] = f[7]
        for i, f in enumerate(zd):
            s_zl[r, i] = f[0]
        for i, f in enumerate(yu):
            s_yr[r, i] = f[:, 7:8, :]
        for i, f in enumerate(yd):
            s_yl[r, i] = f[:, 0:1, :]

    def fill_velocity():
        v, b, l, m = [f[...] for f in av], buoy[...], lam[...], mu[...]
        more, most = (b, m), (b, l, m)
        fill_faces(
            0,
            ((v[0], *more), (v[1], *more), (v[2], *more)),
            ((v[1], v[2], *most), (v[0], v[2], *most), (v[0], v[1], *most)),
        )

    def send_stress(r, s):
        fill_faces(r, ((s[3], s[4]), (s[3], s[5]), (s[4], s[5])), ((s[0],), (s[1],), (s[2],)))
        adjoint_exchange(r).start(*range(6))

    for name in ("peer", "slot", "own_s"):
        loads[name].wait()
    slots = []
    for d in range(4):
        brick = lax.rem(gz + d, 4)
        listed, shift = jnp.int32(0), jnp.int32(0)
        for p in range(8):
            held = t_peer[brick, p] == gz
            listed = jnp.where(held, listed + lax.shift_left(t_slot[brick, p], shift), listed)
            shift = jnp.where(held, shift + 3, shift)
        slots.append([lax.bitwise_and(lax.shift_right_logical(listed, 3 * j), 7) for j in range(CAP)])

    def stage(own, staged, got):
        for d in (2, 1, 3, 0):
            for j in range(CAP):
                if d:
                    staged[(d - 1) * CAP + j] = own[slots[d][j]]
                else:
                    got[3 * CAP + j] = own[slots[d][j]]

    def restore(staged, got, n):
        for d in (2, 1, 3):
            rows = pl.ds((d - 1) * CAP, CAP)
            pltpu.make_async_remote_copy(
                src_ref=staged.at[rows],
                dst_ref=got.at[rows],
                send_sem=rs_send.at[n],
                recv_sem=rs_recv.at[n],
                device_id={"gz": lax.rem(gz + d, 4)},
                device_id_type=MESH,
            ).start()

    def restored(got, n):
        rows = got.at[pl.ds(0, 3 * CAP)]
        pltpu.make_async_copy(rows, rows, rs_recv.at[n]).wait()

    where_is, seen = [], jnp.int32(0)
    for p in range(8):
        holder = t_peer[gz, p]
        at_digit = holder * 4
        before = lax.bitwise_and(lax.shift_right_logical(seen, at_digit), 15)
        where_is.append(lax.bitwise_and(gz - holder + 3, 3) * CAP + jnp.minimum(before, CAP - 1))
        seen = seen + lax.shift_left(jnp.int32(1), at_digit)

    stage(own_s, stage_s, got_s)
    loads["adj"].wait()
    pltpu.make_async_copy(params, params, in_sem.at[1]).wait()
    fill_velocity()
    pl.semaphore_wait(barrier, around + 3)
    adjoint_exchange(0).start(*range(6))
    restore(stage_s, got_s, 0)

    for step in GREETED:

        @pl.when(exists(step))
        def _():
            pl.semaphore_signal(ready, inc=1, device_id=at(step), device_id_type=MESH)

    loads["own_v"].wait()
    stage(own_v, stage_v, got_v)

    def stress_faces(r):
        xl, xr = r_xl[r], r_xr[r]
        return {
            ("xr", 0): unpack_columns(xr, 0, 127),
            ("xl", 3): unpack_columns(xl, 0, 0),
            ("xl", 4): unpack_columns(xl, 1, 0),
            ("yl", 3): r_yl[r, 0],
            ("yl", 5): r_yl[r, 1],
            ("yr", 1): r_yr[r, 0],
            ("zl", 4): r_zl[r, 0],
            ("zl", 5): r_zl[r, 1],
            ("zr", 2): r_zr[r, 0],
        }

    def velocity_faces(r):
        xl, xr = r_xl[r], r_xr[r]
        return {
            ("xl", 0): unpack_columns(xl, 0, 0),
            ("xr", 1): unpack_columns(xr, 0, 127),
            ("xr", 2): unpack_columns(xr, 1, 127),
            ("yl", 1): r_yl[r, 0],
            ("yr", 0): r_yr[r, 0],
            ("yr", 2): r_yr[r, 1],
            ("zl", 2): r_zl[r, 0],
            ("zr", 0): r_zr[r, 0],
            ("zr", 1): r_zr[r, 1],
        }

    def forward_edges(e):
        exchange = forward_exchange(e)
        f_yr[e, 0] = fs[3, :, 7:8, :]
        f_yr[e, 1] = fs[5, :, 7:8, :]
        for i, f in ((2, 1), (3, 0), (4, 4)):
            f_yl[e, i] = fs[f, :, 0:1, :]
        exchange.start(6, 7, 8, 9)
        f_zr[e, 0] = fs[4, 7]
        f_zr[e, 1] = fs[5, 7]
        for i, f in ((2, 2), (3, 0), (4, 2), (5, 1), (6, 3)):
            f_zl[e, i] = fs[f, 0]
        exchange.start(*range(10, 18))

    def forward_faces(e):
        exchange = forward_exchange(e)
        rates = velocity_rates([fs[i] for i in range(6)], buoy[...], Zeros())
        for i in range(3):
            fv[i] = fv[i] + rates[i]
        f_xr[e, 0] = pack_columns((fs[3], fs[4], fv[0]), 127)
        f_xl[e, 0] = pack_columns((fs[0], fv[1], fv[2]), 0)
        exchange.start(0, 1)
        f_zr[e, 2] = fv[2, 7]
        f_zl[e, 0] = fv[0, 0]
        f_zl[e, 1] = fv[1, 0]
        exchange.start(4, 5)
        f_yr[e, 2] = fv[1, :, 7:8, :]
        f_yl[e, 0] = fv[0, :, 0:1, :]
        f_yl[e, 1] = fv[2, :, 0:1, :]
        exchange.start(2, 3)

    def forward_step(e):
        xl, xr = g_xl[e], g_xr[e]
        lane3, row3 = iota3(2), iota3(1)
        lane2, row2 = iota2(1), iota2(0)
        z1 = lax.broadcasted_iota(jnp.int32, (8, 1, 128), 0)
        lane1 = lax.broadcasted_iota(jnp.int32, (8, 1, 128), 2)

        def layer(at_z, tile, like):
            return jnp.where(iota3(0) == at_z, tile[None], 0.0) if like == 3 else jnp.where(z1 == at_z, tile, 0.0)

        def first_lane(f, axis):
            return pltpu.roll(f, 1, axis)

        def last_lane(f, axis):
            return pltpu.roll(f, 127, axis)

        mm, pp = first_lane(exy_mm[e, 0], 2), (last_lane(exy_pp[e, 0], 2), last_lane(exy_pp[e, 1], 2))
        pm, mp = last_lane(exy_pm[e, 0], 2), first_lane(exy_mp[e, 0], 2)
        zmm, zpp = first_lane(exz_mm[e, 0], 1), (last_lane(exz_pp[e, 0], 1), last_lane(exz_pp[e, 1], 1))
        zpm, zmp = last_lane(exz_pm[e, 0], 1), first_lane(exz_mp[e, 0], 1)
        all3 = (8, 8, 128)
        nothing = jnp.zeros(all3, jnp.float32)

        def row(at_y, face):
            return jnp.where(row3 == at_y, jnp.broadcast_to(face, all3), nothing)

        b = buoy[...]
        h = {}
        h["xl", 0] = unpack_columns(xl, 2, 0) + bx[0] * (fs[0] - row(0, mm) - layer(0, zmm, 3))
        h["xr", 1] = unpack_columns(xr, 1, 127) + bx[1] * (row(7, pp[0]) - fs[3] - layer(0, zpm, 3))
        h["xr", 2] = unpack_columns(xr, 2, 127) + bx[1] * (layer(7, zpp[0], 3) - fs[4] - row(0, pm))

        def y_layer(at_z, tile, at_y):
            return jnp.where(z1 == at_z, jnp.broadcast_to(tile[at_y : at_y + 1, :][None], (8, 1, 128)), 0.0)

        bym, byp = r_yl[0, 1], r_yr[0, 2]
        h["yl", 1] = g_yl[e, 2] + bym * (
            fs[1, :, 0:1, :] - jnp.where(lane1 == 0, mm, 0.0) - y_layer(0, eyz_mm[e, 0], 7)
        )
        h["yr", 0] = g_yr[e, 0] + byp * (
            jnp.where(lane1 == 127, pp[1], 0.0) - fs[3, :, 7:8, :] - y_layer(0, eyz_pm[e, 0], 0)
        )
        h["yr", 2] = g_yr[e, 1] + byp * (
            y_layer(7, eyz_pp[e, 0], 0) - fs[5, :, 7:8, :] - jnp.where(lane1 == 0, mp, 0.0)
        )

        def y_edge(tile, at_y, from_y):
            return jnp.where(row2 == at_y, jnp.broadcast_to(tile[from_y : from_y + 1, :], (8, 128)), 0.0)

        bzm, bzp = r_zl[0, 1], r_zr[0, 2]
        h["zl", 2] = g_zl[e, 2] + bzm * (fs[2, 0] - jnp.where(lane2 == 0, zmm, 0.0) - y_edge(eyz_mm[e, 0], 0, 7))
        h["zr", 0] = g_zr[e, 0] + bzp * (
            jnp.where(lane2 == 127, zpp[1], 0.0) - fs[4, 7] - y_edge(eyz_mp[e, 0], 0, 7)
        )
        h["zr", 1] = g_zr[e, 1] + bzp * (
            y_edge(eyz_pp[e, 1], 7, 0) - fs[5, 7] - jnp.where(lane2 == 0, zmp, 0.0)
        )

        fv[0] = fv[0] + b * (jnp.where(lane3 == 127, unpack_columns(xr, 0, 127), 0.0) - row(0, g_yl[e, 0]))
        fv[1] = fv[1] + b * (row(7, g_yr[e, 2]) - jnp.where(lane3 == 0, unpack_columns(xl, 0, 0), 0.0))
        fv[2] = fv[2] - b * (jnp.where(lane3 == 0, unpack_columns(xl, 1, 0), 0.0) + row(0, g_yl[e, 1]))
        fv[0, 0] = fv[0, 0] - buoy[0] * g_zl[e, 0]
        fv[1, 0] = fv[1, 0] - buoy[0] * g_zl[e, 1]
        fv[2, 7] = fv[2, 7] + buoy[7] * g_zr[e, 2]
        return stress_rates([fv[i] for i in range(3)], lam[...], mu[...], h)

    def adjoint_send():
        c_yr[0] = av[1][:, 7:8, :]
        c_yl[0] = av[0][:, 0:1, :]
        c_yl[1] = av[2][:, 0:1, :]
        last_exchange.start(6, 7)
        c_zr[0] = av[2][7]
        c_zl[0] = av[0][0]
        c_zl[1] = av[1][0]
        last_exchange.start(8, 9, 10, 11)
        v = [f[...] for f in av]
        rates = stress_rates(v, lam[...], mu[...], Zeros())
        s = [a0[i] - rates[i] for i in range(6)]
        c_xr[0] = pack_columns((v[0], s[3], s[4]), 127)
        c_xl[0] = pack_columns((v[1], v[2], s[0]), 0)
        last_exchange.start(0, 1)
        c_zr[1] = s[4][7]
        c_zr[2] = s[5][7]
        c_zl[2] = s[2][0]
        last_exchange.start(4, 5)
        c_yr[1] = s[3][:, 7:8, :]
        c_yr[2] = s[5][:, 7:8, :]
        c_yl[2] = s[1][:, 0:1, :]
        last_exchange.start(2, 3)

    def adjoint_step():
        v = [f[...] for f in av]
        xl, xr = d_xl[0], d_xr[0]
        lane2, row2 = iota2(1), iota2(0)
        all3 = (8, 8, 128)
        z1 = lax.broadcasted_iota(jnp.int32, (8, 1, 128), 0)
        lane1 = lax.broadcasted_iota(jnp.int32, (8, 1, 128), 2)
        h = {
            ("xl", 0): unpack_columns(xl, 0, 0),
            ("xr", 1): unpack_columns(xr, 0, 127),
            ("xr", 2): unpack_columns(xr, 1, 127),
            ("yl", 1): d_yl[0, 0],
            ("yr", 0): d_yr[0, 0],
            ("yr", 2): d_yr[0, 1],
            ("zl", 2): d_zl[0, 0],
            ("zr", 0): d_zr[0, 0],
            ("zr", 1): d_zr[0, 1],
        }
        rates = stress_rates(v, lam[...], mu[...], h)
        s = [a0[i] - rates[i] for i in range(6)]

        xy_pm, xy_mp = pltpu.roll(vxy_pm[0], 127, 2), pltpu.roll(vxy_mp[0], 1, 2)
        xz_pm, xz_mp = pltpu.roll(vxz_pm[0], 127, 1), pltpu.roll(vxz_mp[0], 1, 1)

        def row(at_y, face):
            return jnp.where(iota3(1) == at_y, jnp.broadcast_to(face, all3), 0.0)

        def layer(at_z, tile):
            return jnp.where(iota3(0) == at_z, tile[None], 0.0)

        def y_layer(at_z, tile, at_y):
            return jnp.where(z1 == at_z, jnp.broadcast_to(tile[at_y : at_y + 1, :][None], (8, 1, 128)), 0.0)

        def y_edge(tile, at_y, from_y):
            return jnp.where(row2 == at_y, jnp.broadcast_to(tile[from_y : from_y + 1, :], (8, 128)), 0.0)

        both = lx[...] + 2.0 * mx[1]
        g = {}
        g["xl", 3] = unpack_columns(xl, 1, 0) - mx[0] * (v[1] + row(7, xy_mp))
        g["xl", 4] = unpack_columns(xl, 2, 0) - mx[0] * (v[2] + layer(7, xz_mp))
        g["xr", 0] = unpack_columns(xr, 2, 127) + both * v[0] + lx[...] * (row(0, xy_pm) + layer(0, xz_pm))
        mu_m, lam_p, mu_p = r_yl[0, 2], r_yr[0, 3], r_yr[0, 4]
        g["yl", 3] = d_yl[0, 1] - mu_m * (v[0][:, 0:1, :] + jnp.where(lane1 == 127, xy_pm, 0.0))
        g["yl", 5] = d_yl[0, 2] - mu_m * (v[2][:, 0:1, :] + y_layer(7, vyz_mp[0], 7))
        g["yr", 1] = (
            d_yr[0, 2]
            + (lam_p + 2.0 * mu_p) * v[1][:, 7:8, :]
            + lam_p * (jnp.where(lane1 == 0, xy_mp, 0.0) + y_layer(0, vyz_pm[0], 0))
        )
        mu_m, lam_p, mu_p = r_zl[0, 2], r_zr[0, 3], r_zr[0, 4]
        g["zl", 4] = d_zl[0, 1] - mu_m * (v[0][0] + jnp.where(lane2 == 127, xz_pm, 0.0))
        g["zl", 5] = d_zl[0, 2] - mu_m * (v[1][0] + y_edge(vyz_pm[0], 7, 0))
        g["zr", 2] = (
            d_zr[0, 2]
            + (lam_p + 2.0 * mu_p) * v[2][7]
            + lam_p * (jnp.where(lane2 == 0, xz_mp, 0.0) + y_edge(vyz_mp[0], 0, 7))
        )
        for i in range(6):
            adj_out[3 + i] = s[i]
        rates = velocity_rates(s, buoy[...], g)
        for i in range(3):
            adj_out[i] = v[i] - rates[i]

    restore(stage_v, got_v, 1)
    no_tiles[...] = jnp.zeros(no_tiles.shape, jnp.float32)
    no_rows[...] = jnp.zeros(no_rows.shape, jnp.float32)
    exchanges = (adjoint_exchange(0), adjoint_exchange(1), last_exchange, forward_exchange(0), forward_exchange(1))
    for exchange in exchanges:
        exchange.prepare()

    for name in ("rec", "traces", "plan"):
        loads[name].wait()
    cells = rec[0]
    row_of, x_of = lax.shift_right_logical(cells, 7), lax.bitwise_and(cells, 127)
    rows = lax.broadcasted_iota(jnp.int32, (64, 64), 0)
    hit = rows == jnp.broadcast_to(row_of, (64, 64))
    samples = [jnp.broadcast_to(traces[pl.ds(t_plan[k], 1), :], (64, 64)) for k in range(STEPS)]
    left = jnp.concatenate([jnp.where(hit, samples[k], 0.0) for k in range(STEPS)], axis=0)
    columns = lax.broadcasted_iota(jnp.int32, (128, 64), 0)
    right = jnp.where(columns == jnp.broadcast_to(x_of, (128, 64)), 1.0, 0.0)
    spread = lax.dot_general(
        left, right, (((1,), (1,)), ((), ())), precision=lax.Precision.HIGHEST, preferred_element_type=jnp.float32
    )
    spread = spread.reshape(STEPS, 8, 8, 128)
    for i in range(3):
        a1[i] = as_[i][...] + spread[1]
        a0[i] = spread[0]
    for i in range(3, 6):
        a1[i] = as_[i][...]

    for name in ("wav", "src"):
        loads[name].wait()
    flat = iota3(0) * 1024 + iota3(1) * 128 + iota3(2)
    counted = jnp.zeros((8, 8, 128), jnp.float32)
    for j in range(t_src.shape[0]):
        counted = counted + jnp.where(flat == t_src[j], 1.0, 0.0)
    hits[...] = counted


    restored(got_s, 0)
    for p in range(8):
        fs[:, p] = got_s[where_is[p]].astype(jnp.float32)
    pl.semaphore_wait(ready, around)
    forward_edges(0)
    adjoint_exchange(0).receive()
    rates = stress_rates([f[...] for f in av], lam[...], mu[...], velocity_faces(0))
    for i in range(6):
        as_[i][...] = a1[i] - rates[i]
    send_stress(1, [f[...] for f in as_])
    bx[0] = unpack_columns(r_xl[0], 1, 0)
    mx[0] = unpack_columns(r_xl[0], 2, 0)
    bx[1] = unpack_columns(r_xr[0], 2, 127)
    lx[...] = unpack_columns(r_xr[0], 3, 127)
    mx[1] = unpack_columns(r_xr[0], 4, 127)

    restored(got_v, 1)
    for p in range(8):
        fv[:, p] = got_v[where_is[p]].astype(jnp.float32)
    forward_faces(0)

    adjoint_exchange(1).receive()
    rates = velocity_rates([f[...] for f in as_], buoy[...], stress_faces(1))
    for i in range(3):
        av[i][...] = av[i][...] - rates[i]
    for i in range(3):
        a0[i] = a0[i] + as_[i][...]
    for i in range(3, 6):
        a0[i] = as_[i][...]
    adjoint_send()

    forward_exchange(0).receive()
    rates = forward_step(0)
    pulse = hits[...] * t_wav[t_plan[0]]
    for i in range(3):
        fs[i] = fs[i] + rates[i] + pulse
    for i in range(3, 6):
        fs[i] = fs[i] + rates[i]
    forward_edges(1)
    forward_faces(1)

    def image(s, a):
        by_lambda = (s[0] + s[1] + s[2]) * (a[0] + a[1] + a[2])
        by_mu = s[0] * a[0] + s[1] * a[1] + s[2] * a[2] + 2.0 * (s[3] * a[3] + s[4] * a[4] + s[5] * a[5])
        return by_lambda, by_mu

    by_lambda, by_mu = image(fs, a0)
    il_out[...] = by_lambda
    im_out[...] = by_mu

    last_exchange.receive()
    adjoint_step()
    for exchange in exchanges[:4]:
        exchange.sent()
    for n, staged in enumerate((stage_s, stage_v)):
        pltpu.make_async_copy(staged, staged, rs_send.at[n]).wait()

    forward_exchange(1).receive()
    rates = forward_step(1)
    pulse = hits[...] * t_wav[t_plan[1]]
    last = [fs[i] + rates[i] + pulse for i in range(3)] + [fs[i] + rates[i] for i in range(3, 6)]
    by_lambda, by_mu = image(last, a1)
    il_out[...] += by_lambda
    im_out[...] += by_mu
    forward_exchange(1).sent()


def write_out(adj, il, im, adj_out, il_out, im_out, sem):
    copies = [
        pltpu.make_async_copy(src, dst, sem.at[n])
        for n, (src, dst) in enumerate(((adj, adj_out), (il, il_out), (im, im_out)))
    ]
    for copy in copies:
        copy.start()
    for copy in copies:
        copy.wait()


def solution(mesh):
    sizes = (mesh.shape["gx"], mesh.shape["gy"], mesh.shape["gz"])
    f32, i32, bf16 = jnp.float32, jnp.int32, jnp.bfloat16
    brick = (8, 8, 128)

    def on_device(*args):
        nt, nrec = args[10].shape[-2:]
        nsrc = args[7].shape[-1]
        vmem = pltpu.VMEM
        scratch = [
            vmem((3,) + brick, f32),
            vmem((1, nrec), i32),
            vmem((nt, nrec), f32),
            pltpu.SMEM((4, 8), i32),
            pltpu.SMEM((4, 8), i32),
            pltpu.SMEM((nsrc,), i32),
            pltpu.SMEM((nt,), f32),
            pltpu.SMEM((STEPS,), i32),
            vmem((8, 6, 8, 128), bf16),
            vmem((8, 3, 8, 128), bf16),
            vmem((3 * CAP, 6, 8, 128), bf16),
            vmem((3 * CAP, 3, 8, 128), bf16),
            vmem((4 * CAP, 6, 8, 128), bf16),
            vmem((4 * CAP, 3, 8, 128), bf16),
            vmem((3,) + brick, f32),
            vmem((6,) + brick, f32),
            vmem((9,) + brick, f32),
            vmem((6,) + brick, f32),
            vmem((6,) + brick, f32),
            vmem((2,) + brick, f32),
            vmem((2,) + brick, f32),
            vmem(brick, f32),
            vmem(brick, f32),
        ]
        row, tile = (8, 1, 128), (8, 128)
        scratch += [vmem((2, 1) + tile, f32)] * 2 + [vmem((2, 5) + row, f32)] * 2 + [vmem((2, 5) + tile, f32)] * 2
        scratch += [vmem((10,) + tile, f32), vmem((8,) + row, f32), vmem((5,) + tile, f32), vmem((3,) + row, f32)]
        scratch += [vmem((2, 1) + tile, f32)] * 2 + [vmem((2, 5) + row, f32), vmem((2, 3) + row, f32)]
        scratch += [vmem((2, 7) + tile, f32), vmem((2, 3) + tile, f32)]
        scratch += [vmem((18,) + tile, f32), vmem((11,) + row, f32)] * 2
        scratch += [vmem((1,) + tile, f32)] * 2 + [vmem((3,) + row, f32)] * 2 + [vmem((3,) + tile, f32)] * 2
        scratch += [vmem((12,) + tile, f32), vmem((8,) + row, f32)]
        for tiles, rows in ((10, 8), (5, 3), (12, 8), (18, 11), (18, 11), (5, 5)):
            scratch += [vmem((tiles,) + tile, f32), vmem((rows,) + row, f32)]
        dma = pltpu.SemaphoreType.DMA
        scratch += [dma((11,)), dma((3, 2)), dma((3, 2)), dma((2, 2)), dma((2, 2)), dma((2,)), dma((2,)), pltpu.SemaphoreType.REGULAR]
        shapes = ((9,) + brick, brick, brick)
        results = pl.pallas_call(
            functools.partial(kernel, sizes),
            out_shape=tuple(pltpu.VMEM(shape, f32) for shape in shapes),
            in_specs=[pl.BlockSpec(memory_space=pl.ANY)] * 12,
            out_specs=(pl.BlockSpec(memory_space=pltpu.VMEM),) * 3,
            scratch_shapes=scratch,
            compiler_params=pltpu.CompilerParams(
                collective_id=0, has_side_effects=True
            ),
            name="window",
        )(*args)
        return pl.pallas_call(
            write_out,
            out_shape=tuple(jax.ShapeDtypeStruct(shape, f32) for shape in shapes),
            in_specs=[pl.BlockSpec(memory_space=pltpu.VMEM)] * 3,
            out_specs=(pl.BlockSpec(memory_space=pl.ANY),) * 3,
            scratch_shapes=[pltpu.SemaphoreType.DMA((3,))],
            compiler_params=pltpu.CompilerParams(vmem_limit_bytes=16 << 20),
            name="write_out",
        )(*results)

    return jax.shard_map(
        on_device,
        mesh=mesh,
        in_specs=(
            P("gz", None, None, "gy", "gx"),
            P("gx", "gy", None, None),
            P("gx", "gy", None, None),
            P(None, "gz", "gy", "gx"),
            P("gz", "gy", "gx"),
            P("gz", "gy", "gx"),
            P("gz", "gy", "gx"),
            P("gz", "gy", "gx", None),
            P(),
            P("gz", "gy", "gx", None),
            P("gz", "gy", "gx", None, None),
            P(),
        ),
        out_specs=(P(None, "gz", "gy", "gx"), P("gz", "gy", "gx"), P("gz", "gy", "gx")),
        check_vma=False,
    )
```

```python
import functools

import jax
import jax.numpy as jnp
from jax import lax
from jax.experimental import pallas as pl
from jax.experimental.pallas import tpu as pltpu
from jax.sharding import PartitionSpec as P

MESH = pl.DeviceIdType.MESH
STEPS = 2
CAP = 5

GREETED = ((1, 0, 0), (-1, 0, 0), (0, 1, 0), (0, -1, 0))


def iota3(dim):
    return lax.broadcasted_iota(jnp.int32, (8, 8, 128), dim)


def iota2(dim):
    return lax.broadcasted_iota(jnp.int32, (8, 128), dim)


def pack_columns(fields, lane):
    lanes = iota2(1)
    packed = jnp.zeros((8, 128), jnp.float32)
    for number, field in enumerate(fields):
        for z in range(8):
            at = number * 8 + z
            moved = pltpu.roll(field[z], (at - lane) % 128, 1)
            packed = jnp.where(lanes == at, moved, packed)
    return packed


def unpack_columns(packed, number, lane):
    return jnp.stack([pltpu.roll(packed, (lane - number * 8 - z) % 128, 1) for z in range(8)])


def behind_x(f, face):
    return f - jnp.where(iota3(2) == 0, face, pltpu.roll(f, 1, 2))


def ahead_x(f, face):
    return jnp.where(iota3(2) == 127, face, pltpu.roll(f, 127, 2)) - f


def behind_y(f, face):
    return f - jnp.where(iota3(1) == 0, jnp.broadcast_to(face, (8, 8, 128)), pltpu.roll(f, 1, 1))


def ahead_y(f, face):
    return jnp.where(iota3(1) == 7, jnp.broadcast_to(face, (8, 8, 128)), pltpu.roll(f, 7, 1)) - f


def behind_z(f, face):
    return f - jnp.concatenate([face[None], f[:7]], axis=0)


def ahead_z(f, face):
    return jnp.concatenate([f[1:], face[None]], axis=0) - f


def velocity_rates(s, b, h):
    rx = b * (ahead_x(s[0], h["xr", 0]) + behind_y(s[3], h["yl", 3]) + behind_z(s[4], h["zl", 4]))
    ry = b * (behind_x(s[3], h["xl", 3]) + ahead_y(s[1], h["yr", 1]) + behind_z(s[5], h["zl", 5]))
    rz = b * (behind_x(s[4], h["xl", 4]) + behind_y(s[5], h["yl", 5]) + ahead_z(s[2], h["zr", 2]))
    return rx, ry, rz


def stress_rates(v, lam, mu, h):
    exx, eyy, ezz = behind_x(v[0], h["xl", 0]), behind_y(v[1], h["yl", 1]), behind_z(v[2], h["zl", 2])
    spread = lam * (exx + eyy + ezz)
    twice = 2.0 * mu
    return (
        spread + twice * exx,
        spread + twice * eyy,
        spread + twice * ezz,
        mu * (ahead_y(v[0], h["yr", 0]) + ahead_x(v[1], h["xr", 1])),
        mu * (ahead_z(v[0], h["zr", 0]) + ahead_x(v[2], h["xr", 2])),
        mu * (ahead_z(v[1], h["zr", 1]) + ahead_y(v[2], h["yr", 2])),
    )


class Zeros:
    def __getitem__(self, key):
        side = key[0]
        shape = (8, 1, 128) if side[0] == "y" else (8, 128)
        return jnp.zeros((8, 8, 128) if side[0] == "x" else shape, jnp.float32)


class Part:
    def __init__(self, kind, places):
        self.kind, self.places = kind, places

    def __getitem__(self, key):
        e, i = key if isinstance(key, tuple) else (key, 0)
        ref, first, _ = self.places[e]
        return ref[first + i]

    def at(self, e):
        ref, first, count = self.places[e]
        return ref.at[pl.ds(first, count)]


class Exchange:
    def __init__(self, e, buffers, spare, send, recv, messages, to, exists):
        self.e, self.buffers, self.spare, self.send, self.recv = e, buffers, spare, send, recv
        self.messages, self.to, self.exists = messages, to, exists

    def prepare(self):
        for part, step, _ in self.messages:
            target = part.at(self.e)
            _, first, count = part.places[self.e]
            aside = self.spare[part.kind].at[pl.ds(first, count)]

            @pl.when(jnp.logical_not(self.exists(step)))
            def _():
                zeros = self.spare[2 + part.kind].at[pl.ds(0, count)]
                pltpu.make_async_copy(zeros, aside, self.send.at[part.kind]).start()

            @pl.when(jnp.logical_not(self.exists(tuple(-d for d in step))))
            def _():
                zeros = self.spare[2 + part.kind].at[pl.ds(0, count)]
                pltpu.make_async_copy(zeros, target, self.recv.at[part.kind]).start()

    def start(self, *which):
        for n in which:
            part, step, source = self.messages[n]

            @pl.when(self.exists(step))
            def _():
                pltpu.make_async_remote_copy(
                    src_ref=source,
                    dst_ref=part.at(self.e),
                    send_sem=self.send.at[part.kind],
                    recv_sem=self.recv.at[part.kind],
                    device_id=self.to(step),
                    device_id_type=MESH,
                ).start()

    def all_of(self, sems):
        for kind, ref in enumerate(self.buffers):
            pltpu.make_async_copy(ref, ref, sems.at[kind]).wait()

    def sent(self):
        self.all_of(self.send)

    def receive(self):
        self.all_of(self.recv)


def kernel(
    sizes,
    store,
    hpeer,
    hslot,
    adj_in,
    lam_in,
    mu_in,
    buoy_in,
    src_in,
    wav_in,
    rec_in,
    tr_in,
    plan_in,
    adj_out,
    il_out,
    im_out,
    params,
    rec,
    traces,
    t_peer,
    t_slot,
    t_src,
    t_wav,
    t_plan,
    own_s,
    own_v,
    stage_s,
    stage_v,
    got_s,
    got_v,
    fv,
    fs,
    adj,
    a1,
    a0,
    bx,
    mx,
    lx,
    hits,
    s_xl,
    s_xr,
    s_yl,
    s_yr,
    s_zl,
    s_zr,
    r0_tiles,
    r0_rows,
    r1_tiles,
    r1_rows,
    f_xl,
    f_xr,
    f_yl,
    f_yr,
    f_zl,
    f_zr,
    g0_tiles,
    g0_rows,
    g1_tiles,
    g1_rows,
    c_xl,
    c_xr,
    c_yl,
    c_yr,
    c_zl,
    c_zr,
    d_tiles,
    d_rows,
    ar0_tiles,
    ar0_rows,
    ar1_tiles,
    ar1_rows,
    ad_tiles,
    ad_rows,
    ag0_tiles,
    ag0_rows,
    ag1_tiles,
    ag1_rows,
    no_tiles,
    no_rows,
    in_sem,
    send_sem,
    recv_sem,
    fsend_sem,
    frecv_sem,
    rs_send,
    rs_recv,
    ready,
):
    count = dict(zip(("gx", "gy", "gz"), sizes))
    index = {axis: lax.axis_index(axis) for axis in ("gx", "gy", "gz")}
    gz = index["gz"]

    axes = ("gx", "gy", "gz")

    def exists(step):
        found = None
        for axis, d in zip(axes, step):
            if d:
                here = index[axis] < count[axis] - 1 if d > 0 else index[axis] > 0
                found = here if found is None else jnp.logical_and(found, here)
        return found

    def at(step):
        return {axis: index[axis] + d for axis, d in zip(axes, step) if d}

    def local(src, dst, n):
        return pltpu.make_async_copy(src, dst, in_sem.at[n])

    loads = dict(
        peer=local(hpeer.at[0, 0], t_peer, 7),
        slot=local(hslot.at[0, 0], t_slot, 8),
        own_s=local(store.at[:, pl.ds(3, 6), 0], own_s, 9),
        av=local(adj_in.at[pl.ds(0, 3)], adj.at[pl.ds(0, 3)], 0),
        own_v=local(store.at[:, pl.ds(0, 3), 0], own_v, 10),
        as_=local(adj_in.at[pl.ds(3, 6)], adj.at[pl.ds(3, 6)], 11),
        lam=local(lam_in, params.at[0], 1),
        mu=local(mu_in, params.at[1], 1),
        buoy=local(buoy_in, params.at[2], 1),
        rec=local(rec_in.at[0, 0], rec, 2),
        traces=local(tr_in.at[0, 0, 0], traces, 3),
        plan=local(plan_in, t_plan, 4),
        wav=local(wav_in, t_wav, 5),
        src=local(src_in.at[0, 0, 0], t_src, 6),
    )
    for name in ("own_s", "peer", "slot"):
        loads[name].start()

    barrier = pltpu.get_barrier_semaphore()

    def greet(where):
        pl.semaphore_signal(barrier, inc=1, device_id=where, device_id_type=MESH)

    around = jnp.int32(0)
    for step in GREETED:

        @pl.when(exists(step))
        def _():
            greet(at(step))

        around = around + exists(step).astype(jnp.int32)
    for d in (1, 2, 3):
        greet({"gz": lax.rem(gz + d, 4)})

    for name, copy in loads.items():
        if name not in ("own_s", "peer", "slot"):
            copy.start()

    TILES, ROWS = 0, 1
    first, second, forward0, forward1, last_one = (
        (r0_tiles, r0_rows),
        (r1_tiles, r1_rows),
        (g0_tiles, g0_rows),
        (g1_tiles, g1_rows),
        (d_tiles, d_rows),
    )

    spares = [
        (*aside, no_tiles, no_rows)
        for aside in (
            (ar0_tiles, ar0_rows),
            (ar1_tiles, ar1_rows),
            (ad_tiles, ad_rows),
            (ag0_tiles, ag0_rows),
            (ag1_tiles, ag1_rows),
        )
    ]

    def part(kind, *places):
        return Part(kind, [(buffers[kind], at_row, fields) for buffers, at_row, fields in places])

    r_xl = part(TILES, (first, 0, 1), (second, 0, 1))
    r_xr = part(TILES, (first, 1, 1), (second, 1, 1))
    r_zl = part(TILES, (first, 2, 1), (second, 2, 4))
    r_zr = part(TILES, (first, 3, 2), (second, 6, 4))
    r_yl = part(ROWS, (first, 0, 1), (second, 0, 4))
    r_yr = part(ROWS, (first, 1, 2), (second, 4, 4))

    def adjoint_exchange(r):
        up, down = ((1, 2), (4, 4))[r]
        return Exchange(
            r,
            (first, second)[r],
            spares[r],
            send_sem.at[r],
            recv_sem.at[r],
            (
                (r_xl, (1, 0, 0), s_xr.at[r]),
                (r_xr, (-1, 0, 0), s_xl.at[r]),
                (r_zl, (0, 0, 1), s_zr.at[r, pl.ds(0, up)]),
                (r_zr, (0, 0, -1), s_zl.at[r, pl.ds(0, down)]),
                (r_yl, (0, 1, 0), s_yr.at[r, pl.ds(0, up)]),
                (r_yr, (0, -1, 0), s_yl.at[r, pl.ds(0, down)]),
            ),
            at,
            exists,
        )

    def forward_part(kind, at_row, fields):
        return part(kind, (forward0, at_row, fields), (forward1, at_row, fields))

    g_xl, g_xr = forward_part(TILES, 0, 1), forward_part(TILES, 1, 1)
    g_zl, g_zr = forward_part(TILES, 2, 3), forward_part(TILES, 5, 3)
    exz_mm, exz_pp = forward_part(TILES, 8, 1), forward_part(TILES, 9, 2)
    exz_pm, exz_mp = forward_part(TILES, 11, 1), forward_part(TILES, 12, 1)
    eyz_mm, eyz_pp = forward_part(TILES, 13, 1), forward_part(TILES, 14, 2)
    eyz_pm, eyz_mp = forward_part(TILES, 16, 1), forward_part(TILES, 17, 1)
    g_yl, g_yr = forward_part(ROWS, 0, 3), forward_part(ROWS, 3, 3)
    exy_mm, exy_pp = forward_part(ROWS, 6, 1), forward_part(ROWS, 7, 2)
    exy_pm, exy_mp = forward_part(ROWS, 9, 1), forward_part(ROWS, 10, 1)

    def forward_exchange(e):
        return Exchange(
            e,
            (forward0, forward1)[e],
            spares[3 + e],
            fsend_sem.at[e],
            frecv_sem.at[e],
            (
                (g_xl, (1, 0, 0), f_xr.at[e]),
                (g_xr, (-1, 0, 0), f_xl.at[e]),
                (g_yl, (0, 1, 0), f_yr.at[e, pl.ds(0, 3)]),
                (g_yr, (0, -1, 0), f_yl.at[e, pl.ds(0, 3)]),
                (g_zl, (0, 0, 1), f_zr.at[e, pl.ds(0, 3)]),
                (g_zr, (0, 0, -1), f_zl.at[e, pl.ds(0, 3)]),
                (exy_mm, (1, 1, 0), f_yr.at[e, pl.ds(0, 1)]),
                (exy_pp, (-1, -1, 0), f_yl.at[e, pl.ds(2, 2)]),
                (exy_pm, (-1, 1, 0), f_yr.at[e, pl.ds(1, 1)]),
                (exy_mp, (1, -1, 0), f_yl.at[e, pl.ds(4, 1)]),
                (exz_mm, (1, 0, 1), f_zr.at[e, pl.ds(0, 1)]),
                (exz_pp, (-1, 0, -1), f_zl.at[e, pl.ds(2, 2)]),
                (exz_pm, (-1, 0, 1), f_zr.at[e, pl.ds(1, 1)]),
                (exz_mp, (1, 0, -1), f_zl.at[e, pl.ds(6, 1)]),
                (eyz_mm, (0, 1, 1), f_zr.at[e, pl.ds(1, 1)]),
                (eyz_pp, (0, -1, -1), f_zl.at[e, pl.ds(4, 2)]),
                (eyz_pm, (0, -1, 1), f_zr.at[e, pl.ds(0, 1)]),
                (eyz_mp, (0, 1, -1), f_zl.at[e, pl.ds(6, 1)]),
            ),
            at,
            exists,
        )

    d_xl, d_xr = part(TILES, (last_one, 0, 1)), part(TILES, (last_one, 1, 1))
    d_zl, d_zr = part(TILES, (last_one, 2, 3)), part(TILES, (last_one, 5, 3))
    vxz_pm, vxz_mp = part(TILES, (last_one, 8, 1)), part(TILES, (last_one, 9, 1))
    vyz_pm, vyz_mp = part(TILES, (last_one, 10, 1)), part(TILES, (last_one, 11, 1))
    d_yl, d_yr = part(ROWS, (last_one, 0, 3)), part(ROWS, (last_one, 3, 3))
    vxy_pm, vxy_mp = part(ROWS, (last_one, 6, 1)), part(ROWS, (last_one, 7, 1))
    last_exchange = Exchange(
        0,
        last_one,
        spares[2],
        send_sem.at[2],
        recv_sem.at[2],
        (
            (d_xl, (1, 0, 0), c_xr),
            (d_xr, (-1, 0, 0), c_xl),
            (d_yl, (0, 1, 0), c_yr),
            (d_yr, (0, -1, 0), c_yl),
            (d_zl, (0, 0, 1), c_zr),
            (d_zr, (0, 0, -1), c_zl),
            (vxy_pm, (-1, 1, 0), c_yr.at[pl.ds(0, 1)]),
            (vxy_mp, (1, -1, 0), c_yl.at[pl.ds(0, 1)]),
            (vxz_pm, (-1, 0, 1), c_zr.at[pl.ds(0, 1)]),
            (vxz_mp, (1, 0, -1), c_zl.at[pl.ds(0, 1)]),
            (vyz_pm, (0, -1, 1), c_zr.at[pl.ds(0, 1)]),
            (vyz_mp, (0, 1, -1), c_zl.at[pl.ds(1, 1)]),
        ),
        at,
        exists,
    )

    lam, mu, buoy = params.at[0], params.at[1], params.at[2]
    av, as_ = [adj.at[i] for i in range(3)], [adj.at[3 + i] for i in range(6)]

    def fill_faces(r, up, down):
        (xu, yu, zu), (xd, yd, zd) = up, down
        s_xr[r, 0] = pack_columns(xu, 127)
        s_xl[r, 0] = pack_columns(xd, 0)
        for i, f in enumerate(zu):
            s_zr[r, i] = f[7]
        for i, f in enumerate(zd):
            s_zl[r, i] = f[0]
        for i, f in enumerate(yu):
            s_yr[r, i] = f[:, 7:8, :]
        for i, f in enumerate(yd):
            s_yl[r, i] = f[:, 0:1, :]

    def fill_velocity():
        v = [f[...] for f in av]
        fill_faces(0, ((v[0],), (v[1],), (v[2],)), ((v[1], v[2]), (v[0], v[2]), (v[0], v[1])))

    def send_stress(r, s):
        b, l, m = buoy[...], lam[...], mu[...]
        fill_faces(
            r,
            ((s[3], s[4], b, m), (s[3], s[5], b, m), (s[4], s[5], b, m)),
            ((s[0], b, l, m), (s[1], b, l, m), (s[2], b, l, m)),
        )
        adjoint_exchange(r).start(*range(6))

    for name in ("peer", "slot", "own_s"):
        loads[name].wait()
    slots = []
    for d in range(4):
        brick = lax.rem(gz + d, 4)
        listed, shift = jnp.int32(0), jnp.int32(0)
        for p in range(8):
            held = t_peer[brick, p] == gz
            listed = jnp.where(held, listed + lax.shift_left(t_slot[brick, p], shift), listed)
            shift = jnp.where(held, shift + 3, shift)
        slots.append([lax.bitwise_and(lax.shift_right_logical(listed, 3 * j), 7) for j in range(CAP)])

    def stage(own, staged, got):
        for d in (2, 1, 3, 0):
            for j in range(CAP):
                if d:
                    staged[(d - 1) * CAP + j] = own[slots[d][j]]
                else:
                    got[3 * CAP + j] = own[slots[d][j]]

    def restore(staged, got, n):
        odd = lax.rem(gz, 2)
        for d in (2, 3 - 2 * odd, 1 + 2 * odd):
            rows = pl.ds((d - 1) * CAP, CAP)
            pltpu.make_async_remote_copy(
                src_ref=staged.at[rows],
                dst_ref=got.at[rows],
                send_sem=rs_send.at[n],
                recv_sem=rs_recv.at[n],
                device_id={"gz": lax.rem(gz + d, 4)},
                device_id_type=MESH,
            ).start()

    def restored(got, n):
        rows = got.at[pl.ds(0, 3 * CAP)]
        pltpu.make_async_copy(rows, rows, rs_recv.at[n]).wait()

    where_is, seen = [], jnp.int32(0)
    for p in range(8):
        holder = t_peer[gz, p]
        at_digit = holder * 4
        before = lax.bitwise_and(lax.shift_right_logical(seen, at_digit), 15)
        where_is.append(lax.bitwise_and(gz - holder + 3, 3) * CAP + jnp.minimum(before, CAP - 1))
        seen = seen + lax.shift_left(jnp.int32(1), at_digit)

    stage(own_s, stage_s, got_s)
    loads["av"].wait()
    fill_velocity()
    pl.semaphore_wait(barrier, around + 3)
    adjoint_exchange(0).start(0, 1)
    restore(stage_s, got_s, 0)
    adjoint_exchange(0).start(2, 3, 4, 5)

    for step in GREETED:

        @pl.when(exists(step))
        def _():
            pl.semaphore_signal(ready, inc=1, device_id=at(step), device_id_type=MESH)

    loads["own_v"].wait()
    stage(own_v, stage_v, got_v)

    def stress_faces(r):
        xl, xr = r_xl[r], r_xr[r]
        return {
            ("xr", 0): unpack_columns(xr, 0, 127),
            ("xl", 3): unpack_columns(xl, 0, 0),
            ("xl", 4): unpack_columns(xl, 1, 0),
            ("yl", 3): r_yl[r, 0],
            ("yl", 5): r_yl[r, 1],
            ("yr", 1): r_yr[r, 0],
            ("zl", 4): r_zl[r, 0],
            ("zl", 5): r_zl[r, 1],
            ("zr", 2): r_zr[r, 0],
        }

    def velocity_faces(r):
        xl, xr = r_xl[r], r_xr[r]
        return {
            ("xl", 0): unpack_columns(xl, 0, 0),
            ("xr", 1): unpack_columns(xr, 0, 127),
            ("xr", 2): unpack_columns(xr, 1, 127),
            ("yl", 1): r_yl[r, 0],
            ("yr", 0): r_yr[r, 0],
            ("yr", 2): r_yr[r, 1],
            ("zl", 2): r_zl[r, 0],
            ("zr", 0): r_zr[r, 0],
            ("zr", 1): r_zr[r, 1],
        }

    def forward_edges(e):
        exchange = forward_exchange(e)
        f_yr[e, 0] = fs[3, :, 7:8, :]
        f_yr[e, 1] = fs[5, :, 7:8, :]
        for i, f in ((2, 1), (3, 0), (4, 4)):
            f_yl[e, i] = fs[f, :, 0:1, :]
        exchange.start(6, 7, 8, 9)
        f_zr[e, 0] = fs[4, 7]
        f_zr[e, 1] = fs[5, 7]
        for i, f in ((2, 2), (3, 0), (4, 2), (5, 1), (6, 3)):
            f_zl[e, i] = fs[f, 0]
        exchange.start(*range(10, 18))

    def forward_faces(e):
        exchange = forward_exchange(e)
        rates = velocity_rates([fs[i] for i in range(6)], buoy[...], Zeros())
        for i in range(3):
            fv[i] = fv[i] + rates[i]
        f_xr[e, 0] = pack_columns((fs[3], fs[4], fv[0]), 127)
        f_xl[e, 0] = pack_columns((fs[0], fv[1], fv[2]), 0)
        exchange.start(0, 1)
        f_zr[e, 2] = fv[2, 7]
        f_zl[e, 0] = fv[0, 0]
        f_zl[e, 1] = fv[1, 0]
        exchange.start(4, 5)
        f_yr[e, 2] = fv[1, :, 7:8, :]
        f_yl[e, 0] = fv[0, :, 0:1, :]
        f_yl[e, 1] = fv[2, :, 0:1, :]
        exchange.start(2, 3)

    def forward_step(e):
        xl, xr = g_xl[e], g_xr[e]
        lane3, row3 = iota3(2), iota3(1)
        lane2, row2 = iota2(1), iota2(0)
        z1 = lax.broadcasted_iota(jnp.int32, (8, 1, 128), 0)
        lane1 = lax.broadcasted_iota(jnp.int32, (8, 1, 128), 2)

        def layer(at_z, tile, like):
            return jnp.where(iota3(0) == at_z, tile[None], 0.0) if like == 3 else jnp.where(z1 == at_z, tile, 0.0)

        def first_lane(f, axis):
            return pltpu.roll(f, 1, axis)

        def last_lane(f, axis):
            return pltpu.roll(f, 127, axis)

        mm, pp = first_lane(exy_mm[e, 0], 2), (last_lane(exy_pp[e, 0], 2), last_lane(exy_pp[e, 1], 2))
        pm, mp = last_lane(exy_pm[e, 0], 2), first_lane(exy_mp[e, 0], 2)
        zmm, zpp = first_lane(exz_mm[e, 0], 1), (last_lane(exz_pp[e, 0], 1), last_lane(exz_pp[e, 1], 1))
        zpm, zmp = last_lane(exz_pm[e, 0], 1), first_lane(exz_mp[e, 0], 1)
        all3 = (8, 8, 128)
        nothing = jnp.zeros(all3, jnp.float32)

        def row(at_y, face):
            return jnp.where(row3 == at_y, jnp.broadcast_to(face, all3), nothing)

        b = buoy[...]
        h = {}
        h["xl", 0] = unpack_columns(xl, 2, 0) + bx[0] * (fs[0] - row(0, mm) - layer(0, zmm, 3))
        h["xr", 1] = unpack_columns(xr, 1, 127) + bx[1] * (row(7, pp[0]) - fs[3] - layer(0, zpm, 3))
        h["xr", 2] = unpack_columns(xr, 2, 127) + bx[1] * (layer(7, zpp[0], 3) - fs[4] - row(0, pm))

        def y_layer(at_z, tile, at_y):
            return jnp.where(z1 == at_z, jnp.broadcast_to(tile[at_y : at_y + 1, :][None], (8, 1, 128)), 0.0)

        bym, byp = r_yl[1, 2], r_yr[1, 1]
        h["yl", 1] = g_yl[e, 2] + bym * (
            fs[1, :, 0:1, :] - jnp.where(lane1 == 0, mm, 0.0) - y_layer(0, eyz_mm[e, 0], 7)
        )
        h["yr", 0] = g_yr[e, 0] + byp * (
            jnp.where(lane1 == 127, pp[1], 0.0) - fs[3, :, 7:8, :] - y_layer(0, eyz_pm[e, 0], 0)
        )
        h["yr", 2] = g_yr[e, 1] + byp * (
            y_layer(7, eyz_pp[e, 0], 0) - fs[5, :, 7:8, :] - jnp.where(lane1 == 0, mp, 0.0)
        )

        def y_edge(tile, at_y, from_y):
            return jnp.where(row2 == at_y, jnp.broadcast_to(tile[from_y : from_y + 1, :], (8, 128)), 0.0)

        bzm, bzp = r_zl[1, 2], r_zr[1, 1]
        h["zl", 2] = g_zl[e, 2] + bzm * (fs[2, 0] - jnp.where(lane2 == 0, zmm, 0.0) - y_edge(eyz_mm[e, 0], 0, 7))
        h["zr", 0] = g_zr[e, 0] + bzp * (
            jnp.where(lane2 == 127, zpp[1], 0.0) - fs[4, 7] - y_edge(eyz_mp[e, 0], 0, 7)
        )
        h["zr", 1] = g_zr[e, 1] + bzp * (
            y_edge(eyz_pp[e, 1], 7, 0) - fs[5, 7] - jnp.where(lane2 == 0, zmp, 0.0)
        )

        fv[0] = fv[0] + b * (jnp.where(lane3 == 127, unpack_columns(xr, 0, 127), 0.0) - row(0, g_yl[e, 0]))
        fv[1] = fv[1] + b * (row(7, g_yr[e, 2]) - jnp.where(lane3 == 0, unpack_columns(xl, 0, 0), 0.0))
        fv[2] = fv[2] - b * (jnp.where(lane3 == 0, unpack_columns(xl, 1, 0), 0.0) + row(0, g_yl[e, 1]))
        fv[0, 0] = fv[0, 0] - buoy[0] * g_zl[e, 0]
        fv[1, 0] = fv[1, 0] - buoy[0] * g_zl[e, 1]
        fv[2, 7] = fv[2, 7] + buoy[7] * g_zr[e, 2]
        return stress_rates([fv[i] for i in range(3)], lam[...], mu[...], h)

    def adjoint_send():
        c_yr[0] = av[1][:, 7:8, :]
        c_yl[0] = av[0][:, 0:1, :]
        c_yl[1] = av[2][:, 0:1, :]
        last_exchange.start(6, 7)
        c_zr[0] = av[2][7]
        c_zl[0] = av[0][0]
        c_zl[1] = av[1][0]
        last_exchange.start(8, 9, 10, 11)
        v = [f[...] for f in av]
        rates = stress_rates(v, lam[...], mu[...], Zeros())
        s = [a0[i] - rates[i] for i in range(6)]
        c_xr[0] = pack_columns((v[0], s[3], s[4]), 127)
        c_xl[0] = pack_columns((v[1], v[2], s[0]), 0)
        last_exchange.start(0, 1)
        c_zr[1] = s[4][7]
        c_zr[2] = s[5][7]
        c_zl[2] = s[2][0]
        last_exchange.start(4, 5)
        c_yr[1] = s[3][:, 7:8, :]
        c_yr[2] = s[5][:, 7:8, :]
        c_yl[2] = s[1][:, 0:1, :]
        last_exchange.start(2, 3)

    def adjoint_step():
        v = [f[...] for f in av]
        xl, xr = d_xl[0], d_xr[0]
        lane2, row2 = iota2(1), iota2(0)
        all3 = (8, 8, 128)
        z1 = lax.broadcasted_iota(jnp.int32, (8, 1, 128), 0)
        lane1 = lax.broadcasted_iota(jnp.int32, (8, 1, 128), 2)
        h = {
            ("xl", 0): unpack_columns(xl, 0, 0),
            ("xr", 1): unpack_columns(xr, 0, 127),
            ("xr", 2): unpack_columns(xr, 1, 127),
            ("yl", 1): d_yl[0, 0],
            ("yr", 0): d_yr[0, 0],
            ("yr", 2): d_yr[0, 1],
            ("zl", 2): d_zl[0, 0],
            ("zr", 0): d_zr[0, 0],
            ("zr", 1): d_zr[0, 1],
        }
        rates = stress_rates(v, lam[...], mu[...], h)
        s = [a0[i] - rates[i] for i in range(6)]

        xy_pm, xy_mp = pltpu.roll(vxy_pm[0], 127, 2), pltpu.roll(vxy_mp[0], 1, 2)
        xz_pm, xz_mp = pltpu.roll(vxz_pm[0], 127, 1), pltpu.roll(vxz_mp[0], 1, 1)

        def row(at_y, face):
            return jnp.where(iota3(1) == at_y, jnp.broadcast_to(face, all3), 0.0)

        def layer(at_z, tile):
            return jnp.where(iota3(0) == at_z, tile[None], 0.0)

        def y_layer(at_z, tile, at_y):
            return jnp.where(z1 == at_z, jnp.broadcast_to(tile[at_y : at_y + 1, :][None], (8, 1, 128)), 0.0)

        def y_edge(tile, at_y, from_y):
            return jnp.where(row2 == at_y, jnp.broadcast_to(tile[from_y : from_y + 1, :], (8, 128)), 0.0)

        both = lx[...] + 2.0 * mx[1]
        g = {}
        g["xl", 3] = unpack_columns(xl, 1, 0) - mx[0] * (v[1] + row(7, xy_mp))
        g["xl", 4] = unpack_columns(xl, 2, 0) - mx[0] * (v[2] + layer(7, xz_mp))
        g["xr", 0] = unpack_columns(xr, 2, 127) + both * v[0] + lx[...] * (row(0, xy_pm) + layer(0, xz_pm))
        mu_m, lam_p, mu_p = r_yl[1, 3], r_yr[1, 2], r_yr[1, 3]
        g["yl", 3] = d_yl[0, 1] - mu_m * (v[0][:, 0:1, :] + jnp.where(lane1 == 127, xy_pm, 0.0))
        g["yl", 5] = d_yl[0, 2] - mu_m * (v[2][:, 0:1, :] + y_layer(7, vyz_mp[0], 7))
        g["yr", 1] = (
            d_yr[0, 2]
            + (lam_p + 2.0 * mu_p) * v[1][:, 7:8, :]
            + lam_p * (jnp.where(lane1 == 0, xy_mp, 0.0) + y_layer(0, vyz_pm[0], 0))
        )
        mu_m, lam_p, mu_p = r_zl[1, 3], r_zr[1, 2], r_zr[1, 3]
        g["zl", 4] = d_zl[0, 1] - mu_m * (v[0][0] + jnp.where(lane2 == 127, xz_pm, 0.0))
        g["zl", 5] = d_zl[0, 2] - mu_m * (v[1][0] + y_edge(vyz_pm[0], 7, 0))
        g["zr", 2] = (
            d_zr[0, 2]
            + (lam_p + 2.0 * mu_p) * v[2][7]
            + lam_p * (jnp.where(lane2 == 0, xz_mp, 0.0) + y_edge(vyz_mp[0], 0, 7))
        )
        for i in range(6):
            adj_out[3 + i] = s[i]
        rates = velocity_rates(s, buoy[...], g)
        for i in range(3):
            adj_out[i] = v[i] - rates[i]

    restore(stage_v, got_v, 1)
    no_tiles[...] = jnp.zeros(no_tiles.shape, jnp.float32)
    no_rows[...] = jnp.zeros(no_rows.shape, jnp.float32)
    exchanges = (adjoint_exchange(0), adjoint_exchange(1), last_exchange, forward_exchange(0), forward_exchange(1))
    for exchange in exchanges:
        exchange.prepare()

    for name in ("rec", "traces", "plan", "as_"):
        loads[name].wait()
    pltpu.make_async_copy(params, params, in_sem.at[1]).wait()
    cells = rec[0]
    row_of, x_of = lax.shift_right_logical(cells, 7), lax.bitwise_and(cells, 127)
    rows = lax.broadcasted_iota(jnp.int32, (64, 64), 0)
    hit = rows == jnp.broadcast_to(row_of, (64, 64))
    samples = [jnp.broadcast_to(traces[pl.ds(t_plan[k], 1), :], (64, 64)) for k in range(STEPS)]
    left = jnp.concatenate([jnp.where(hit, samples[k], 0.0) for k in range(STEPS)], axis=0)
    columns = lax.broadcasted_iota(jnp.int32, (128, 64), 0)
    right = jnp.where(columns == jnp.broadcast_to(x_of, (128, 64)), 1.0, 0.0)
    spread = lax.dot_general(
        left, right, (((1,), (1,)), ((), ())), precision=lax.Precision.HIGHEST, preferred_element_type=jnp.float32
    )
    spread = spread.reshape(STEPS, 8, 8, 128)
    for i in range(3):
        a1[i] = as_[i][...] + spread[1]
        a0[i] = spread[0]
    for i in range(3, 6):
        a1[i] = as_[i][...]

    for name in ("wav", "src"):
        loads[name].wait()
    flat = iota3(0) * 1024 + iota3(1) * 128 + iota3(2)
    counted = jnp.zeros((8, 8, 128), jnp.float32)
    for j in range(t_src.shape[0]):
        counted = counted + jnp.where(flat == t_src[j], 1.0, 0.0)
    hits[...] = counted


    restored(got_s, 0)
    for p in range(8):
        fs[:, p] = got_s[where_is[p]].astype(jnp.float32)
    pl.semaphore_wait(ready, around)
    forward_edges(0)
    adjoint_exchange(0).receive()
    rates = stress_rates([f[...] for f in av], lam[...], mu[...], velocity_faces(0))
    for i in range(6):
        as_[i][...] = a1[i] - rates[i]
    send_stress(1, [f[...] for f in as_])

    restored(got_v, 1)
    for p in range(8):
        fv[:, p] = got_v[where_is[p]].astype(jnp.float32)
    forward_faces(0)

    adjoint_exchange(1).receive()
    rates = velocity_rates([f[...] for f in as_], buoy[...], stress_faces(1))
    for i in range(3):
        av[i][...] = av[i][...] - rates[i]
    for i in range(3):
        a0[i] = a0[i] + as_[i][...]
    for i in range(3, 6):
        a0[i] = as_[i][...]
    adjoint_send()
    bx[0] = unpack_columns(r_xl[1], 2, 0)
    mx[0] = unpack_columns(r_xl[1], 3, 0)
    bx[1] = unpack_columns(r_xr[1], 1, 127)
    lx[...] = unpack_columns(r_xr[1], 2, 127)
    mx[1] = unpack_columns(r_xr[1], 3, 127)

    forward_exchange(0).receive()
    rates = forward_step(0)
    pulse = hits[...] * t_wav[t_plan[0]]
    for i in range(3):
        fs[i] = fs[i] + rates[i] + pulse
    for i in range(3, 6):
        fs[i] = fs[i] + rates[i]
    forward_edges(1)
    forward_faces(1)

    def image(s, a):
        by_lambda = (s[0] + s[1] + s[2]) * (a[0] + a[1] + a[2])
        by_mu = s[0] * a[0] + s[1] * a[1] + s[2] * a[2] + 2.0 * (s[3] * a[3] + s[4] * a[4] + s[5] * a[5])
        return by_lambda, by_mu

    by_lambda, by_mu = image(fs, a0)
    il_out[...] = by_lambda
    im_out[...] = by_mu

    last_exchange.receive()
    adjoint_step()
    for exchange in exchanges[:4]:
        exchange.sent()
    for n, staged in enumerate((stage_s, stage_v)):
        pltpu.make_async_copy(staged, staged, rs_send.at[n]).wait()

    forward_exchange(1).receive()
    rates = forward_step(1)
    pulse = hits[...] * t_wav[t_plan[1]]
    last = [fs[i] + rates[i] + pulse for i in range(3)] + [fs[i] + rates[i] for i in range(3, 6)]
    by_lambda, by_mu = image(last, a1)
    il_out[...] += by_lambda
    im_out[...] += by_mu
    forward_exchange(1).sent()


def write_out(adj, il, im, adj_out, il_out, im_out, sem):
    copies = [
        pltpu.make_async_copy(src, dst, sem.at[n])
        for n, (src, dst) in enumerate(((adj, adj_out), (il, il_out), (im, im_out)))
    ]
    for copy in copies:
        copy.start()
    for copy in copies:
        copy.wait()


def solution(mesh):
    sizes = (mesh.shape["gx"], mesh.shape["gy"], mesh.shape["gz"])
    f32, i32, bf16 = jnp.float32, jnp.int32, jnp.bfloat16
    brick = (8, 8, 128)

    def on_device(*args):
        nt, nrec = args[10].shape[-2:]
        nsrc = args[7].shape[-1]
        vmem = pltpu.VMEM
        scratch = [
            vmem((3,) + brick, f32),
            vmem((1, nrec), i32),
            vmem((nt, nrec), f32),
            pltpu.SMEM((4, 8), i32),
            pltpu.SMEM((4, 8), i32),
            pltpu.SMEM((nsrc,), i32),
            pltpu.SMEM((nt,), f32),
            pltpu.SMEM((STEPS,), i32),
            vmem((8, 6, 8, 128), bf16),
            vmem((8, 3, 8, 128), bf16),
            vmem((3 * CAP, 6, 8, 128), bf16),
            vmem((3 * CAP, 3, 8, 128), bf16),
            vmem((4 * CAP, 6, 8, 128), bf16),
            vmem((4 * CAP, 3, 8, 128), bf16),
            vmem((3,) + brick, f32),
            vmem((6,) + brick, f32),
            vmem((9,) + brick, f32),
            vmem((6,) + brick, f32),
            vmem((6,) + brick, f32),
            vmem((2,) + brick, f32),
            vmem((2,) + brick, f32),
            vmem(brick, f32),
            vmem(brick, f32),
        ]
        row, tile = (8, 1, 128), (8, 128)
        scratch += [vmem((2, 1) + tile, f32)] * 2 + [vmem((2, 5) + row, f32)] * 2 + [vmem((2, 5) + tile, f32)] * 2
        scratch += [vmem((5,) + tile, f32), vmem((3,) + row, f32), vmem((10,) + tile, f32), vmem((8,) + row, f32)]
        scratch += [vmem((2, 1) + tile, f32)] * 2 + [vmem((2, 5) + row, f32), vmem((2, 3) + row, f32)]
        scratch += [vmem((2, 7) + tile, f32), vmem((2, 3) + tile, f32)]
        scratch += [vmem((18,) + tile, f32), vmem((11,) + row, f32)] * 2
        scratch += [vmem((1,) + tile, f32)] * 2 + [vmem((3,) + row, f32)] * 2 + [vmem((3,) + tile, f32)] * 2
        scratch += [vmem((12,) + tile, f32), vmem((8,) + row, f32)]
        for tiles, rows in ((5, 3), (10, 8), (12, 8), (18, 11), (18, 11), (5, 5)):
            scratch += [vmem((tiles,) + tile, f32), vmem((rows,) + row, f32)]
        dma = pltpu.SemaphoreType.DMA
        scratch += [dma((12,)), dma((3, 2)), dma((3, 2)), dma((2, 2)), dma((2, 2)), dma((2,)), dma((2,)), pltpu.SemaphoreType.REGULAR]
        shapes = ((9,) + brick, brick, brick)
        results = pl.pallas_call(
            functools.partial(kernel, sizes),
            out_shape=tuple(pltpu.VMEM(shape, f32) for shape in shapes),
            in_specs=[pl.BlockSpec(memory_space=pl.ANY)] * 12,
            out_specs=(pl.BlockSpec(memory_space=pltpu.VMEM),) * 3,
            scratch_shapes=scratch,
            compiler_params=pltpu.CompilerParams(
                collective_id=0, has_side_effects=True
            ),
            name="window",
        )(*args)
        return pl.pallas_call(
            write_out,
            out_shape=tuple(jax.ShapeDtypeStruct(shape, f32) for shape in shapes),
            in_specs=[pl.BlockSpec(memory_space=pltpu.VMEM)] * 3,
            out_specs=(pl.BlockSpec(memory_space=pl.ANY),) * 3,
            scratch_shapes=[pltpu.SemaphoreType.DMA((3,))],
            compiler_params=pltpu.CompilerParams(vmem_limit_bytes=16 << 20),
            name="write_out",
        )(*results)

    return jax.shard_map(
        on_device,
        mesh=mesh,
        in_specs=(
            P("gz", None, None, "gy", "gx"),
            P("gx", "gy", None, None),
            P("gx", "gy", None, None),
            P(None, "gz", "gy", "gx"),
            P("gz", "gy", "gx"),
            P("gz", "gy", "gx"),
            P("gz", "gy", "gx"),
            P("gz", "gy", "gx", None),
            P(),
            P("gz", "gy", "gx", None),
            P("gz", "gy", "gx", None, None),
            P(),
        ),
        out_specs=(P(None, "gz", "gy", "gx"), P("gz", "gy", "gx"), P("gz", "gy", "gx")),
        check_vma=False,
    )
```

```python
import functools

import jax
import jax.numpy as jnp
from jax import lax
from jax.experimental import pallas as pl
from jax.experimental.pallas import tpu as pltpu
from jax.sharding import PartitionSpec as P

MESH = pl.DeviceIdType.MESH
STEPS = 2
CAP = 5

GREETED = ((1, 0, 0), (-1, 0, 0), (0, 1, 0), (0, -1, 0))


def iota3(dim):
    return lax.broadcasted_iota(jnp.int32, (8, 8, 128), dim)


def iota2(dim):
    return lax.broadcasted_iota(jnp.int32, (8, 128), dim)


def pack_columns(fields, lane):
    lanes = iota2(1)
    packed = jnp.zeros((8, 128), jnp.float32)
    for number, field in enumerate(fields):
        for z in range(8):
            at = number * 8 + z
            moved = pltpu.roll(field[z], (at - lane) % 128, 1)
            packed = jnp.where(lanes == at, moved, packed)
    return packed


def unpack_columns(packed, number, lane):
    return jnp.stack([pltpu.roll(packed, (lane - number * 8 - z) % 128, 1) for z in range(8)])


def behind_x(f, face):
    return f - jnp.where(iota3(2) == 0, face, pltpu.roll(f, 1, 2))


def ahead_x(f, face):
    return jnp.where(iota3(2) == 127, face, pltpu.roll(f, 127, 2)) - f


def behind_y(f, face):
    return f - jnp.where(iota3(1) == 0, jnp.broadcast_to(face, (8, 8, 128)), pltpu.roll(f, 1, 1))


def ahead_y(f, face):
    return jnp.where(iota3(1) == 7, jnp.broadcast_to(face, (8, 8, 128)), pltpu.roll(f, 7, 1)) - f


def behind_z(f, face):
    return f - jnp.concatenate([face[None], f[:7]], axis=0)


def ahead_z(f, face):
    return jnp.concatenate([f[1:], face[None]], axis=0) - f


def velocity_rates(s, b, h):
    rx = b * (ahead_x(s[0], h["xr", 0]) + behind_y(s[3], h["yl", 3]) + behind_z(s[4], h["zl", 4]))
    ry = b * (behind_x(s[3], h["xl", 3]) + ahead_y(s[1], h["yr", 1]) + behind_z(s[5], h["zl", 5]))
    rz = b * (behind_x(s[4], h["xl", 4]) + behind_y(s[5], h["yl", 5]) + ahead_z(s[2], h["zr", 2]))
    return rx, ry, rz


def stress_rates(v, lam, mu, h):
    exx, eyy, ezz = behind_x(v[0], h["xl", 0]), behind_y(v[1], h["yl", 1]), behind_z(v[2], h["zl", 2])
    spread = lam * (exx + eyy + ezz)
    twice = 2.0 * mu
    return (
        spread + twice * exx,
        spread + twice * eyy,
        spread + twice * ezz,
        mu * (ahead_y(v[0], h["yr", 0]) + ahead_x(v[1], h["xr", 1])),
        mu * (ahead_z(v[0], h["zr", 0]) + ahead_x(v[2], h["xr", 2])),
        mu * (ahead_z(v[1], h["zr", 1]) + ahead_y(v[2], h["yr", 2])),
    )


class Zeros:
    def __getitem__(self, key):
        side = key[0]
        shape = (8, 1, 128) if side[0] == "y" else (8, 128)
        return jnp.zeros((8, 8, 128) if side[0] == "x" else shape, jnp.float32)


class Part:
    def __init__(self, kind, places):
        self.kind, self.places = kind, places

    def __getitem__(self, key):
        e, i = key if isinstance(key, tuple) else (key, 0)
        ref, first, _ = self.places[e]
        return ref[first + i]

    def at(self, e):
        ref, first, count = self.places[e]
        return ref.at[pl.ds(first, count)]


class Exchange:
    def __init__(self, e, buffers, spare, send, recv, messages, to, exists):
        self.e, self.buffers, self.spare, self.send, self.recv = e, buffers, spare, send, recv
        self.messages, self.to, self.exists = messages, to, exists

    def prepare(self):
        for part, step, _ in self.messages:
            target = part.at(self.e)
            _, first, count = part.places[self.e]
            aside = self.spare[part.kind].at[pl.ds(first, count)]

            @pl.when(jnp.logical_not(self.exists(step)))
            def _():
                zeros = self.spare[2 + part.kind].at[pl.ds(0, count)]
                pltpu.make_async_copy(zeros, aside, self.send).start()

            @pl.when(jnp.logical_not(self.exists(tuple(-d for d in step))))
            def _():
                zeros = self.spare[2 + part.kind].at[pl.ds(0, count)]
                pltpu.make_async_copy(zeros, target, self.recv).start()

    def start(self, *which):
        for n in which:
            part, step, source = self.messages[n]

            @pl.when(self.exists(step))
            def _():
                pltpu.make_async_remote_copy(
                    src_ref=source,
                    dst_ref=part.at(self.e),
                    send_sem=self.send,
                    recv_sem=self.recv,
                    device_id=self.to(step),
                    device_id_type=MESH,
                ).start()

    def all_of(self, sems):
        total = sum(ref.shape[0] for ref in self.buffers)
        everything = self.spare[4].at[pl.ds(0, total)]
        pltpu.make_async_copy(everything, everything, sems).wait()

    def sent(self):
        self.all_of(self.send)

    def receive(self):
        self.all_of(self.recv)


def kernel(
    sizes,
    store,
    hpeer,
    hslot,
    adj_in,
    lam_in,
    mu_in,
    buoy_in,
    src_in,
    wav_in,
    rec_in,
    tr_in,
    plan_in,
    adj_out,
    il_out,
    im_out,
    params,
    rec,
    traces,
    t_peer,
    t_slot,
    t_src,
    t_wav,
    t_plan,
    own_s,
    own_v,
    stage_s,
    stage_v,
    got_s,
    got_v,
    fv,
    fs,
    adj,
    a1,
    a0,
    bx,
    mx,
    lx,
    hits,
    s_xl,
    s_xr,
    s_yl,
    s_yr,
    s_zl,
    s_zr,
    r0_tiles,
    r0_rows,
    r1_tiles,
    r1_rows,
    f_xl,
    f_xr,
    f_yl,
    f_yr,
    f_zl,
    f_zr,
    g0_tiles,
    g0_rows,
    g1_tiles,
    g1_rows,
    c_xl,
    c_xr,
    c_yl,
    c_yr,
    c_zl,
    c_zr,
    d_tiles,
    d_rows,
    ar0_tiles,
    ar0_rows,
    ar1_tiles,
    ar1_rows,
    ad_tiles,
    ad_rows,
    ag0_tiles,
    ag0_rows,
    ag1_tiles,
    ag1_rows,
    no_tiles,
    no_rows,
    meter,
    in_sem,
    send_sem,
    recv_sem,
    fsend_sem,
    frecv_sem,
    rs_send,
    rs_recv,
    ready,
):
    count = dict(zip(("gx", "gy", "gz"), sizes))
    index = {axis: lax.axis_index(axis) for axis in ("gx", "gy", "gz")}
    gz = index["gz"]

    axes = ("gx", "gy", "gz")

    def exists(step):
        found = None
        for axis, d in zip(axes, step):
            if d:
                here = index[axis] < count[axis] - 1 if d > 0 else index[axis] > 0
                found = here if found is None else jnp.logical_and(found, here)
        return found

    def at(step):
        return {axis: index[axis] + d for axis, d in zip(axes, step) if d}

    def local(src, dst, n):
        return pltpu.make_async_copy(src, dst, in_sem.at[n])

    loads = dict(
        peer=local(hpeer.at[0, 0], t_peer, 7),
        slot=local(hslot.at[0, 0], t_slot, 8),
        own_s=local(store.at[:, pl.ds(3, 6), 0], own_s, 9),
        av=local(adj_in.at[pl.ds(0, 3)], adj.at[pl.ds(0, 3)], 0),
        own_v=local(store.at[:, pl.ds(0, 3), 0], own_v, 10),
        as_=local(adj_in.at[pl.ds(3, 6)], adj.at[pl.ds(3, 6)], 11),
        lam=local(lam_in, params.at[0], 1),
        mu=local(mu_in, params.at[1], 1),
        buoy=local(buoy_in, params.at[2], 1),
        rec=local(rec_in.at[0, 0], rec, 2),
        traces=local(tr_in.at[0, 0, 0], traces, 3),
        plan=local(plan_in, t_plan, 4),
        wav=local(wav_in, t_wav, 5),
        src=local(src_in.at[0, 0, 0], t_src, 6),
    )
    for name in ("own_s", "peer", "slot"):
        loads[name].start()

    barrier = pltpu.get_barrier_semaphore()

    def greet(where):
        pl.semaphore_signal(barrier, inc=1, device_id=where, device_id_type=MESH)

    around = jnp.int32(0)
    for step in GREETED:

        @pl.when(exists(step))
        def _():
            greet(at(step))

        around = around + exists(step).astype(jnp.int32)
    for d in (1, 2, 3):
        greet({"gz": lax.rem(gz + d, 4)})

    for name, copy in loads.items():
        if name not in ("own_s", "peer", "slot"):
            copy.start()

    TILES, ROWS = 0, 1
    first, second, forward0, forward1, last_one = (
        (r0_tiles, r0_rows),
        (r1_tiles, r1_rows),
        (g0_tiles, g0_rows),
        (g1_tiles, g1_rows),
        (d_tiles, d_rows),
    )

    spares = [
        (*aside, no_tiles, no_rows, meter)
        for aside in (
            (ar0_tiles, ar0_rows),
            (ar1_tiles, ar1_rows),
            (ad_tiles, ad_rows),
            (ag0_tiles, ag0_rows),
            (ag1_tiles, ag1_rows),
        )
    ]

    def part(kind, *places):
        return Part(kind, [(buffers[kind], at_row, fields) for buffers, at_row, fields in places])

    r_xl = part(TILES, (first, 0, 1), (second, 0, 1))
    r_xr = part(TILES, (first, 1, 1), (second, 1, 1))
    r_zl = part(TILES, (first, 2, 1), (second, 2, 4))
    r_zr = part(TILES, (first, 3, 2), (second, 6, 4))
    r_yl = part(ROWS, (first, 0, 1), (second, 0, 4))
    r_yr = part(ROWS, (first, 1, 2), (second, 4, 4))

    def adjoint_exchange(r):
        up, down = ((1, 2), (4, 4))[r]
        return Exchange(
            r,
            (first, second)[r],
            spares[r],
            send_sem.at[r],
            recv_sem.at[r],
            (
                (r_xl, (1, 0, 0), s_xr.at[r]),
                (r_xr, (-1, 0, 0), s_xl.at[r]),
                (r_zl, (0, 0, 1), s_zr.at[r, pl.ds(0, up)]),
                (r_zr, (0, 0, -1), s_zl.at[r, pl.ds(0, down)]),
                (r_yl, (0, 1, 0), s_yr.at[r, pl.ds(0, up)]),
                (r_yr, (0, -1, 0), s_yl.at[r, pl.ds(0, down)]),
            ),
            at,
            exists,
        )

    def forward_part(kind, at_row, fields):
        return part(kind, (forward0, at_row, fields), (forward1, at_row, fields))

    g_xl, g_xr = forward_part(TILES, 0, 1), forward_part(TILES, 1, 1)
    g_zl, g_zr = forward_part(TILES, 2, 3), forward_part(TILES, 5, 3)
    exz_mm, exz_pp = forward_part(TILES, 8, 1), forward_part(TILES, 9, 2)
    exz_pm, exz_mp = forward_part(TILES, 11, 1), forward_part(TILES, 12, 1)
    eyz_mm, eyz_pp = forward_part(TILES, 13, 1), forward_part(TILES, 14, 2)
    eyz_pm, eyz_mp = forward_part(TILES, 16, 1), forward_part(TILES, 17, 1)
    g_yl, g_yr = forward_part(ROWS, 0, 3), forward_part(ROWS, 3, 3)
    exy_mm, exy_pp = forward_part(ROWS, 6, 1), forward_part(ROWS, 7, 2)
    exy_pm, exy_mp = forward_part(ROWS, 9, 1), forward_part(ROWS, 10, 1)

    def forward_exchange(e):
        return Exchange(
            e,
            (forward0, forward1)[e],
            spares[3 + e],
            fsend_sem.at[e],
            frecv_sem.at[e],
            (
                (g_xl, (1, 0, 0), f_xr.at[e]),
                (g_xr, (-1, 0, 0), f_xl.at[e]),
                (g_yl, (0, 1, 0), f_yr.at[e, pl.ds(0, 3)]),
                (g_yr, (0, -1, 0), f_yl.at[e, pl.ds(0, 3)]),
                (g_zl, (0, 0, 1), f_zr.at[e, pl.ds(0, 3)]),
                (g_zr, (0, 0, -1), f_zl.at[e, pl.ds(0, 3)]),
                (exy_mm, (1, 1, 0), f_yr.at[e, pl.ds(0, 1)]),
                (exy_pp, (-1, -1, 0), f_yl.at[e, pl.ds(2, 2)]),
                (exy_pm, (-1, 1, 0), f_yr.at[e, pl.ds(1, 1)]),
                (exy_mp, (1, -1, 0), f_yl.at[e, pl.ds(4, 1)]),
                (exz_mm, (1, 0, 1), f_zr.at[e, pl.ds(0, 1)]),
                (exz_pp, (-1, 0, -1), f_zl.at[e, pl.ds(2, 2)]),
                (exz_pm, (-1, 0, 1), f_zr.at[e, pl.ds(1, 1)]),
                (exz_mp, (1, 0, -1), f_zl.at[e, pl.ds(6, 1)]),
                (eyz_mm, (0, 1, 1), f_zr.at[e, pl.ds(1, 1)]),
                (eyz_pp, (0, -1, -1), f_zl.at[e, pl.ds(4, 2)]),
                (eyz_pm, (0, -1, 1), f_zr.at[e, pl.ds(0, 1)]),
                (eyz_mp, (0, 1, -1), f_zl.at[e, pl.ds(6, 1)]),
            ),
            at,
            exists,
        )

    d_xl, d_xr = part(TILES, (last_one, 0, 1)), part(TILES, (last_one, 1, 1))
    d_zl, d_zr = part(TILES, (last_one, 2, 3)), part(TILES, (last_one, 5, 3))
    vxz_pm, vxz_mp = part(TILES, (last_one, 8, 1)), part(TILES, (last_one, 9, 1))
    vyz_pm, vyz_mp = part(TILES, (last_one, 10, 1)), part(TILES, (last_one, 11, 1))
    d_yl, d_yr = part(ROWS, (last_one, 0, 3)), part(ROWS, (last_one, 3, 3))
    vxy_pm, vxy_mp = part(ROWS, (last_one, 6, 1)), part(ROWS, (last_one, 7, 1))
    last_exchange = Exchange(
        0,
        last_one,
        spares[2],
        send_sem.at[2],
        recv_sem.at[2],
        (
            (d_xl, (1, 0, 0), c_xr),
            (d_xr, (-1, 0, 0), c_xl),
            (d_yl, (0, 1, 0), c_yr),
            (d_yr, (0, -1, 0), c_yl),
            (d_zl, (0, 0, 1), c_zr),
            (d_zr, (0, 0, -1), c_zl),
            (vxy_pm, (-1, 1, 0), c_yr.at[pl.ds(0, 1)]),
            (vxy_mp, (1, -1, 0), c_yl.at[pl.ds(0, 1)]),
            (vxz_pm, (-1, 0, 1), c_zr.at[pl.ds(0, 1)]),
            (vxz_mp, (1, 0, -1), c_zl.at[pl.ds(0, 1)]),
            (vyz_pm, (0, -1, 1), c_zr.at[pl.ds(0, 1)]),
            (vyz_mp, (0, 1, -1), c_zl.at[pl.ds(1, 1)]),
        ),
        at,
        exists,
    )

    lam, mu, buoy = params.at[0], params.at[1], params.at[2]
    av, as_ = [adj.at[i] for i in range(3)], [adj.at[3 + i] for i in range(6)]

    def fill_faces(r, up, down):
        (xu, yu, zu), (xd, yd, zd) = up, down
        s_xr[r, 0] = pack_columns(xu, 127)
        s_xl[r, 0] = pack_columns(xd, 0)
        for i, f in enumerate(zu):
            s_zr[r, i] = f[7]
        for i, f in enumerate(zd):
            s_zl[r, i] = f[0]
        for i, f in enumerate(yu):
            s_yr[r, i] = f[:, 7:8, :]
        for i, f in enumerate(yd):
            s_yl[r, i] = f[:, 0:1, :]

    def fill_velocity():
        v = [f[...] for f in av]
        fill_faces(0, ((v[0],), (v[1],), (v[2],)), ((v[1], v[2]), (v[0], v[2]), (v[0], v[1])))

    def send_stress(r, s):
        b, l, m = buoy[...], lam[...], mu[...]
        fill_faces(
            r,
            ((s[3], s[4], b, m), (s[3], s[5], b, m), (s[4], s[5], b, m)),
            ((s[0], b, l, m), (s[1], b, l, m), (s[2], b, l, m)),
        )
        adjoint_exchange(r).start(*range(6))

    for name in ("peer", "slot", "own_s"):
        loads[name].wait()
    slots = []
    for d in range(4):
        brick = lax.rem(gz + d, 4)
        listed, shift = jnp.int32(0), jnp.int32(0)
        for p in range(8):
            held = t_peer[brick, p] == gz
            listed = jnp.where(held, listed + lax.shift_left(t_slot[brick, p], shift), listed)
            shift = jnp.where(held, shift + 3, shift)
        slots.append([lax.bitwise_and(lax.shift_right_logical(listed, 3 * j), 7) for j in range(CAP)])

    def stage(own, staged, got):
        for d in (2, 1, 3, 0):
            for j in range(CAP):
                if d:
                    staged[(d - 1) * CAP + j] = own[slots[d][j]]
                else:
                    got[3 * CAP + j] = own[slots[d][j]]

    def restore(staged, got, n):
        odd = lax.rem(gz, 2)
        for d in (2, 3 - 2 * odd, 1 + 2 * odd):
            rows = pl.ds((d - 1) * CAP, CAP)
            pltpu.make_async_remote_copy(
                src_ref=staged.at[rows],
                dst_ref=got.at[rows],
                send_sem=rs_send.at[n],
                recv_sem=rs_recv.at[n],
                device_id={"gz": lax.rem(gz + d, 4)},
                device_id_type=MESH,
            ).start()

    def restored(got, n):
        rows = got.at[pl.ds(0, 3 * CAP)]
        pltpu.make_async_copy(rows, rows, rs_recv.at[n]).wait()

    where_is, seen = [], jnp.int32(0)
    for p in range(8):
        holder = t_peer[gz, p]
        at_digit = holder * 4
        before = lax.bitwise_and(lax.shift_right_logical(seen, at_digit), 15)
        where_is.append(lax.bitwise_and(gz - holder + 3, 3) * CAP + jnp.minimum(before, CAP - 1))
        seen = seen + lax.shift_left(jnp.int32(1), at_digit)

    stage(own_s, stage_s, got_s)
    loads["av"].wait()
    fill_velocity()
    pl.semaphore_wait(barrier, around + 3)
    adjoint_exchange(0).start(0, 1)
    restore(stage_s, got_s, 0)
    adjoint_exchange(0).start(2, 3, 4, 5)

    for step in GREETED:

        @pl.when(exists(step))
        def _():
            pl.semaphore_signal(ready, inc=1, device_id=at(step), device_id_type=MESH)

    loads["own_v"].wait()
    stage(own_v, stage_v, got_v)

    def stress_faces(r):
        xl, xr = r_xl[r], r_xr[r]
        return {
            ("xr", 0): unpack_columns(xr, 0, 127),
            ("xl", 3): unpack_columns(xl, 0, 0),
            ("xl", 4): unpack_columns(xl, 1, 0),
            ("yl", 3): r_yl[r, 0],
            ("yl", 5): r_yl[r, 1],
            ("yr", 1): r_yr[r, 0],
            ("zl", 4): r_zl[r, 0],
            ("zl", 5): r_zl[r, 1],
            ("zr", 2): r_zr[r, 0],
        }

    def velocity_faces(r):
        xl, xr = r_xl[r], r_xr[r]
        return {
            ("xl", 0): unpack_columns(xl, 0, 0),
            ("xr", 1): unpack_columns(xr, 0, 127),
            ("xr", 2): unpack_columns(xr, 1, 127),
            ("yl", 1): r_yl[r, 0],
            ("yr", 0): r_yr[r, 0],
            ("yr", 2): r_yr[r, 1],
            ("zl", 2): r_zl[r, 0],
            ("zr", 0): r_zr[r, 0],
            ("zr", 1): r_zr[r, 1],
        }

    def forward_edges(e):
        exchange = forward_exchange(e)
        f_yr[e, 0] = fs[3, :, 7:8, :]
        f_yr[e, 1] = fs[5, :, 7:8, :]
        for i, f in ((2, 1), (3, 0), (4, 4)):
            f_yl[e, i] = fs[f, :, 0:1, :]
        exchange.start(6, 7, 8, 9)
        f_zr[e, 0] = fs[4, 7]
        f_zr[e, 1] = fs[5, 7]
        for i, f in ((2, 2), (3, 0), (4, 2), (5, 1), (6, 3)):
            f_zl[e, i] = fs[f, 0]
        exchange.start(*range(10, 18))

    def forward_faces(e):
        exchange = forward_exchange(e)
        rates = velocity_rates([fs[i] for i in range(6)], buoy[...], Zeros())
        for i in range(3):
            fv[i] = fv[i] + rates[i]
        f_xr[e, 0] = pack_columns((fs[3], fs[4], fv[0]), 127)
        f_xl[e, 0] = pack_columns((fs[0], fv[1], fv[2]), 0)
        exchange.start(0, 1)
        f_zr[e, 2] = fv[2, 7]
        f_zl[e, 0] = fv[0, 0]
        f_zl[e, 1] = fv[1, 0]
        exchange.start(4, 5)
        f_yr[e, 2] = fv[1, :, 7:8, :]
        f_yl[e, 0] = fv[0, :, 0:1, :]
        f_yl[e, 1] = fv[2, :, 0:1, :]
        exchange.start(2, 3)

    def forward_step(e):
        xl, xr = g_xl[e], g_xr[e]
        lane3, row3 = iota3(2), iota3(1)
        lane2, row2 = iota2(1), iota2(0)
        z1 = lax.broadcasted_iota(jnp.int32, (8, 1, 128), 0)
        lane1 = lax.broadcasted_iota(jnp.int32, (8, 1, 128), 2)

        def layer(at_z, tile, like):
            return jnp.where(iota3(0) == at_z, tile[None], 0.0) if like == 3 else jnp.where(z1 == at_z, tile, 0.0)

        def first_lane(f, axis):
            return pltpu.roll(f, 1, axis)

        def last_lane(f, axis):
            return pltpu.roll(f, 127, axis)

        mm, pp = first_lane(exy_mm[e, 0], 2), (last_lane(exy_pp[e, 0], 2), last_lane(exy_pp[e, 1], 2))
        pm, mp = last_lane(exy_pm[e, 0], 2), first_lane(exy_mp[e, 0], 2)
        zmm, zpp = first_lane(exz_mm[e, 0], 1), (last_lane(exz_pp[e, 0], 1), last_lane(exz_pp[e, 1], 1))
        zpm, zmp = last_lane(exz_pm[e, 0], 1), first_lane(exz_mp[e, 0], 1)
        all3 = (8, 8, 128)
        nothing = jnp.zeros(all3, jnp.float32)

        def row(at_y, face):
            return jnp.where(row3 == at_y, jnp.broadcast_to(face, all3), nothing)

        b = buoy[...]
        h = {}
        h["xl", 0] = unpack_columns(xl, 2, 0) + bx[0] * (fs[0] - row(0, mm) - layer(0, zmm, 3))
        h["xr", 1] = unpack_columns(xr, 1, 127) + bx[1] * (row(7, pp[0]) - fs[3] - layer(0, zpm, 3))
        h["xr", 2] = unpack_columns(xr, 2, 127) + bx[1] * (layer(7, zpp[0], 3) - fs[4] - row(0, pm))

        def y_layer(at_z, tile, at_y):
            return jnp.where(z1 == at_z, jnp.broadcast_to(tile[at_y : at_y + 1, :][None], (8, 1, 128)), 0.0)

        bym, byp = r_yl[1, 2], r_yr[1, 1]
        h["yl", 1] = g_yl[e, 2] + bym * (
            fs[1, :, 0:1, :] - jnp.where(lane1 == 0, mm, 0.0) - y_layer(0, eyz_mm[e, 0], 7)
        )
        h["yr", 0] = g_yr[e, 0] + byp * (
            jnp.where(lane1 == 127, pp[1], 0.0) - fs[3, :, 7:8, :] - y_layer(0, eyz_pm[e, 0], 0)
        )
        h["yr", 2] = g_yr[e, 1] + byp * (
            y_layer(7, eyz_pp[e, 0], 0) - fs[5, :, 7:8, :] - jnp.where(lane1 == 0, mp, 0.0)
        )

        def y_edge(tile, at_y, from_y):
            return jnp.where(row2 == at_y, jnp.broadcast_to(tile[from_y : from_y + 1, :], (8, 128)), 0.0)

        bzm, bzp = r_zl[1, 2], r_zr[1, 1]
        h["zl", 2] = g_zl[e, 2] + bzm * (fs[2, 0] - jnp.where(lane2 == 0, zmm, 0.0) - y_edge(eyz_mm[e, 0], 0, 7))
        h["zr", 0] = g_zr[e, 0] + bzp * (
            jnp.where(lane2 == 127, zpp[1], 0.0) - fs[4, 7] - y_edge(eyz_mp[e, 0], 0, 7)
        )
        h["zr", 1] = g_zr[e, 1] + bzp * (
            y_edge(eyz_pp[e, 1], 7, 0) - fs[5, 7] - jnp.where(lane2 == 0, zmp, 0.0)
        )

        fv[0] = fv[0] + b * (jnp.where(lane3 == 127, unpack_columns(xr, 0, 127), 0.0) - row(0, g_yl[e, 0]))
        fv[1] = fv[1] + b * (row(7, g_yr[e, 2]) - jnp.where(lane3 == 0, unpack_columns(xl, 0, 0), 0.0))
        fv[2] = fv[2] - b * (jnp.where(lane3 == 0, unpack_columns(xl, 1, 0), 0.0) + row(0, g_yl[e, 1]))
        fv[0, 0] = fv[0, 0] - buoy[0] * g_zl[e, 0]
        fv[1, 0] = fv[1, 0] - buoy[0] * g_zl[e, 1]
        fv[2, 7] = fv[2, 7] + buoy[7] * g_zr[e, 2]
        return stress_rates([fv[i] for i in range(3)], lam[...], mu[...], h)

    def adjoint_send():
        c_yr[0] = av[1][:, 7:8, :]
        c_yl[0] = av[0][:, 0:1, :]
        c_yl[1] = av[2][:, 0:1, :]
        last_exchange.start(6, 7)
        c_zr[0] = av[2][7]
        c_zl[0] = av[0][0]
        c_zl[1] = av[1][0]
        last_exchange.start(8, 9, 10, 11)
        v = [f[...] for f in av]
        rates = stress_rates(v, lam[...], mu[...], Zeros())
        s = [a0[i] - rates[i] for i in range(6)]
        c_xr[0] = pack_columns((v[0], s[3], s[4]), 127)
        c_xl[0] = pack_columns((v[1], v[2], s[0]), 0)
        last_exchange.start(0, 1)
        c_zr[1] = s[4][7]
        c_zr[2] = s[5][7]
        c_zl[2] = s[2][0]
        last_exchange.start(4, 5)
        c_yr[1] = s[3][:, 7:8, :]
        c_yr[2] = s[5][:, 7:8, :]
        c_yl[2] = s[1][:, 0:1, :]
        last_exchange.start(2, 3)

    def adjoint_step():
        v = [f[...] for f in av]
        xl, xr = d_xl[0], d_xr[0]
        lane2, row2 = iota2(1), iota2(0)
        all3 = (8, 8, 128)
        z1 = lax.broadcasted_iota(jnp.int32, (8, 1, 128), 0)
        lane1 = lax.broadcasted_iota(jnp.int32, (8, 1, 128), 2)
        h = {
            ("xl", 0): unpack_columns(xl, 0, 0),
            ("xr", 1): unpack_columns(xr, 0, 127),
            ("xr", 2): unpack_columns(xr, 1, 127),
            ("yl", 1): d_yl[0, 0],
            ("yr", 0): d_yr[0, 0],
            ("yr", 2): d_yr[0, 1],
            ("zl", 2): d_zl[0, 0],
            ("zr", 0): d_zr[0, 0],
            ("zr", 1): d_zr[0, 1],
        }
        rates = stress_rates(v, lam[...], mu[...], h)
        s = [a0[i] - rates[i] for i in range(6)]

        xy_pm, xy_mp = pltpu.roll(vxy_pm[0], 127, 2), pltpu.roll(vxy_mp[0], 1, 2)
        xz_pm, xz_mp = pltpu.roll(vxz_pm[0], 127, 1), pltpu.roll(vxz_mp[0], 1, 1)

        def row(at_y, face):
            return jnp.where(iota3(1) == at_y, jnp.broadcast_to(face, all3), 0.0)

        def layer(at_z, tile):
            return jnp.where(iota3(0) == at_z, tile[None], 0.0)

        def y_layer(at_z, tile, at_y):
            return jnp.where(z1 == at_z, jnp.broadcast_to(tile[at_y : at_y + 1, :][None], (8, 1, 128)), 0.0)

        def y_edge(tile, at_y, from_y):
            return jnp.where(row2 == at_y, jnp.broadcast_to(tile[from_y : from_y + 1, :], (8, 128)), 0.0)

        both = lx[...] + 2.0 * mx[1]
        g = {}
        g["xl", 3] = unpack_columns(xl, 1, 0) - mx[0] * (v[1] + row(7, xy_mp))
        g["xl", 4] = unpack_columns(xl, 2, 0) - mx[0] * (v[2] + layer(7, xz_mp))
        g["xr", 0] = unpack_columns(xr, 2, 127) + both * v[0] + lx[...] * (row(0, xy_pm) + layer(0, xz_pm))
        mu_m, lam_p, mu_p = r_yl[1, 3], r_yr[1, 2], r_yr[1, 3]
        g["yl", 3] = d_yl[0, 1] - mu_m * (v[0][:, 0:1, :] + jnp.where(lane1 == 127, xy_pm, 0.0))
        g["yl", 5] = d_yl[0, 2] - mu_m * (v[2][:, 0:1, :] + y_layer(7, vyz_mp[0], 7))
        g["yr", 1] = (
            d_yr[0, 2]
            + (lam_p + 2.0 * mu_p) * v[1][:, 7:8, :]
            + lam_p * (jnp.where(lane1 == 0, xy_mp, 0.0) + y_layer(0, vyz_pm[0], 0))
        )
        mu_m, lam_p, mu_p = r_zl[1, 3], r_zr[1, 2], r_zr[1, 3]
        g["zl", 4] = d_zl[0, 1] - mu_m * (v[0][0] + jnp.where(lane2 == 127, xz_pm, 0.0))
        g["zl", 5] = d_zl[0, 2] - mu_m * (v[1][0] + y_edge(vyz_pm[0], 7, 0))
        g["zr", 2] = (
            d_zr[0, 2]
            + (lam_p + 2.0 * mu_p) * v[2][7]
            + lam_p * (jnp.where(lane2 == 0, xz_mp, 0.0) + y_edge(vyz_mp[0], 0, 7))
        )
        for i in range(6):
            adj_out[3 + i] = s[i]
        rates = velocity_rates(s, buoy[...], g)
        for i in range(3):
            adj_out[i] = v[i] - rates[i]

    restore(stage_v, got_v, 1)
    no_tiles[...] = jnp.zeros(no_tiles.shape, jnp.float32)
    no_rows[...] = jnp.zeros(no_rows.shape, jnp.float32)
    exchanges = (adjoint_exchange(0), adjoint_exchange(1), last_exchange, forward_exchange(0), forward_exchange(1))
    for exchange in exchanges:
        exchange.prepare()

    for name in ("rec", "traces", "plan", "as_"):
        loads[name].wait()
    pltpu.make_async_copy(params, params, in_sem.at[1]).wait()
    cells = rec[0]
    row_of, x_of = lax.shift_right_logical(cells, 7), lax.bitwise_and(cells, 127)
    rows = lax.broadcasted_iota(jnp.int32, (64, 64), 0)
    hit = rows == jnp.broadcast_to(row_of, (64, 64))
    samples = [jnp.broadcast_to(traces[pl.ds(t_plan[k], 1), :], (64, 64)) for k in range(STEPS)]
    left = jnp.concatenate([jnp.where(hit, samples[k], 0.0) for k in range(STEPS)], axis=0)
    columns = lax.broadcasted_iota(jnp.int32, (128, 64), 0)
    right = jnp.where(columns == jnp.broadcast_to(x_of, (128, 64)), 1.0, 0.0)
    spread = lax.dot_general(
        left, right, (((1,), (1,)), ((), ())), precision=lax.Precision.HIGHEST, preferred_element_type=jnp.float32
    )
    spread = spread.reshape(STEPS, 8, 8, 128)
    for i in range(3):
        a1[i] = as_[i][...] + spread[1]
        a0[i] = spread[0]
    for i in range(3, 6):
        a1[i] = as_[i][...]

    for name in ("wav", "src"):
        loads[name].wait()
    flat = iota3(0) * 1024 + iota3(1) * 128 + iota3(2)
    counted = jnp.zeros((8, 8, 128), jnp.float32)
    for j in range(t_src.shape[0]):
        counted = counted + jnp.where(flat == t_src[j], 1.0, 0.0)
    hits[...] = counted


    restored(got_s, 0)
    for p in range(8):
        fs[:, p] = got_s[where_is[p]].astype(jnp.float32)
    pl.semaphore_wait(ready, around)
    forward_edges(0)
    adjoint_exchange(0).receive()
    rates = stress_rates([f[...] for f in av], lam[...], mu[...], velocity_faces(0))
    for i in range(6):
        as_[i][...] = a1[i] - rates[i]
    send_stress(1, [f[...] for f in as_])

    restored(got_v, 1)
    for p in range(8):
        fv[:, p] = got_v[where_is[p]].astype(jnp.float32)
    forward_faces(0)

    adjoint_exchange(1).receive()
    rates = velocity_rates([f[...] for f in as_], buoy[...], stress_faces(1))
    for i in range(3):
        av[i][...] = av[i][...] - rates[i]
    for i in range(3):
        a0[i] = a0[i] + as_[i][...]
    for i in range(3, 6):
        a0[i] = as_[i][...]
    adjoint_send()
    bx[0] = unpack_columns(r_xl[1], 2, 0)
    mx[0] = unpack_columns(r_xl[1], 3, 0)
    bx[1] = unpack_columns(r_xr[1], 1, 127)
    lx[...] = unpack_columns(r_xr[1], 2, 127)
    mx[1] = unpack_columns(r_xr[1], 3, 127)

    forward_exchange(0).receive()
    rates = forward_step(0)
    pulse = hits[...] * t_wav[t_plan[0]]
    for i in range(3):
        fs[i] = fs[i] + rates[i] + pulse
    for i in range(3, 6):
        fs[i] = fs[i] + rates[i]
    forward_edges(1)
    forward_faces(1)

    def image(s, a):
        by_lambda = (s[0] + s[1] + s[2]) * (a[0] + a[1] + a[2])
        by_mu = s[0] * a[0] + s[1] * a[1] + s[2] * a[2] + 2.0 * (s[3] * a[3] + s[4] * a[4] + s[5] * a[5])
        return by_lambda, by_mu

    by_lambda, by_mu = image(fs, a0)
    il_out[...] = by_lambda
    im_out[...] = by_mu

    last_exchange.receive()
    adjoint_step()
    for exchange in exchanges[:4]:
        exchange.sent()
    for n, staged in enumerate((stage_s, stage_v)):
        pltpu.make_async_copy(staged, staged, rs_send.at[n]).wait()

    forward_exchange(1).receive()
    rates = forward_step(1)
    pulse = hits[...] * t_wav[t_plan[1]]
    last = [fs[i] + rates[i] + pulse for i in range(3)] + [fs[i] + rates[i] for i in range(3, 6)]
    by_lambda, by_mu = image(last, a1)
    il_out[...] += by_lambda
    im_out[...] += by_mu
    forward_exchange(1).sent()


def write_out(adj, il, im, adj_out, il_out, im_out, sem):
    copies = [
        pltpu.make_async_copy(src, dst, sem.at[n])
        for n, (src, dst) in enumerate(((adj, adj_out), (il, il_out), (im, im_out)))
    ]
    for copy in copies:
        copy.start()
    for copy in copies:
        copy.wait()


def solution(mesh):
    sizes = (mesh.shape["gx"], mesh.shape["gy"], mesh.shape["gz"])
    f32, i32, bf16 = jnp.float32, jnp.int32, jnp.bfloat16
    brick = (8, 8, 128)

    def on_device(*args):
        nt, nrec = args[10].shape[-2:]
        nsrc = args[7].shape[-1]
        vmem = pltpu.VMEM
        scratch = [
            vmem((3,) + brick, f32),
            vmem((1, nrec), i32),
            vmem((nt, nrec), f32),
            pltpu.SMEM((4, 8), i32),
            pltpu.SMEM((4, 8), i32),
            pltpu.SMEM((nsrc,), i32),
            pltpu.SMEM((nt,), f32),
            pltpu.SMEM((STEPS,), i32),
            vmem((8, 6, 8, 128), bf16),
            vmem((8, 3, 8, 128), bf16),
            vmem((3 * CAP, 6, 8, 128), bf16),
            vmem((3 * CAP, 3, 8, 128), bf16),
            vmem((4 * CAP, 6, 8, 128), bf16),
            vmem((4 * CAP, 3, 8, 128), bf16),
            vmem((3,) + brick, f32),
            vmem((6,) + brick, f32),
            vmem((9,) + brick, f32),
            vmem((6,) + brick, f32),
            vmem((6,) + brick, f32),
            vmem((2,) + brick, f32),
            vmem((2,) + brick, f32),
            vmem(brick, f32),
            vmem(brick, f32),
        ]
        row, tile = (8, 1, 128), (8, 128)
        scratch += [vmem((2, 1) + tile, f32)] * 2 + [vmem((2, 5) + row, f32)] * 2 + [vmem((2, 5) + tile, f32)] * 2
        scratch += [vmem((5,) + tile, f32), vmem((3,) + row, f32), vmem((10,) + tile, f32), vmem((8,) + row, f32)]
        scratch += [vmem((2, 1) + tile, f32)] * 2 + [vmem((2, 5) + row, f32), vmem((2, 3) + row, f32)]
        scratch += [vmem((2, 7) + tile, f32), vmem((2, 3) + tile, f32)]
        scratch += [vmem((18,) + tile, f32), vmem((11,) + row, f32)] * 2
        scratch += [vmem((1,) + tile, f32)] * 2 + [vmem((3,) + row, f32)] * 2 + [vmem((3,) + tile, f32)] * 2
        scratch += [vmem((12,) + tile, f32), vmem((8,) + row, f32)]
        for tiles, rows in ((5, 3), (10, 8), (12, 8), (18, 11), (18, 11), (5, 5)):
            scratch += [vmem((tiles,) + tile, f32), vmem((rows,) + row, f32)]
        scratch += [vmem((29,) + tile, f32)]
        dma = pltpu.SemaphoreType.DMA
        scratch += [dma((12,)), dma((3,)), dma((3,)), dma((2,)), dma((2,)), dma((2,)), dma((2,)), pltpu.SemaphoreType.REGULAR]
        shapes = ((9,) + brick, brick, brick)
        results = pl.pallas_call(
            functools.partial(kernel, sizes),
            out_shape=tuple(pltpu.VMEM(shape, f32) for shape in shapes),
            in_specs=[pl.BlockSpec(memory_space=pl.ANY)] * 12,
            out_specs=(pl.BlockSpec(memory_space=pltpu.VMEM),) * 3,
            scratch_shapes=scratch,
            compiler_params=pltpu.CompilerParams(
                collective_id=0, has_side_effects=True
            ),
            name="window",
        )(*args)
        return pl.pallas_call(
            write_out,
            out_shape=tuple(jax.ShapeDtypeStruct(shape, f32) for shape in shapes),
            in_specs=[pl.BlockSpec(memory_space=pltpu.VMEM)] * 3,
            out_specs=(pl.BlockSpec(memory_space=pl.ANY),) * 3,
            scratch_shapes=[pltpu.SemaphoreType.DMA((3,))],
            compiler_params=pltpu.CompilerParams(vmem_limit_bytes=16 << 20),
            name="write_out",
        )(*results)

    return jax.shard_map(
        on_device,
        mesh=mesh,
        in_specs=(
            P("gz", None, None, "gy", "gx"),
            P("gx", "gy", None, None),
            P("gx", "gy", None, None),
            P(None, "gz", "gy", "gx"),
            P("gz", "gy", "gx"),
            P("gz", "gy", "gx"),
            P("gz", "gy", "gx"),
            P("gz", "gy", "gx", None),
            P(),
            P("gz", "gy", "gx", None),
            P("gz", "gy", "gx", None, None),
            P(),
        ),
        out_specs=(P(None, "gz", "gy", "gx"), P("gz", "gy", "gx"), P("gz", "gy", "gx")),
        check_vma=False,
    )
```

```python
import functools

import jax
import jax.numpy as jnp
from jax import lax
from jax.experimental import pallas as pl
from jax.experimental.pallas import tpu as pltpu
from jax.sharding import PartitionSpec as P

MESH = pl.DeviceIdType.MESH
STEPS = 2
CAP = 5

GREETED = ((1, 0, 0), (-1, 0, 0), (0, 1, 0), (0, -1, 0))


def iota3(dim):
    return lax.broadcasted_iota(jnp.int32, (8, 8, 128), dim)


def iota2(dim):
    return lax.broadcasted_iota(jnp.int32, (8, 128), dim)


def pack_columns(fields, lane):
    lanes = iota2(1)
    packed = jnp.zeros((8, 128), jnp.float32)
    for number, field in enumerate(fields):
        for z in range(8):
            at = number * 8 + z
            moved = pltpu.roll(field[z], (at - lane) % 128, 1)
            packed = jnp.where(lanes == at, moved, packed)
    return packed


def unpack_columns(packed, number, lane):
    return jnp.stack([pltpu.roll(packed, (lane - number * 8 - z) % 128, 1) for z in range(8)])


def behind_x(f, face):
    return f - jnp.where(iota3(2) == 0, face, pltpu.roll(f, 1, 2))


def ahead_x(f, face):
    return jnp.where(iota3(2) == 127, face, pltpu.roll(f, 127, 2)) - f


def behind_y(f, face):
    return f - jnp.where(iota3(1) == 0, jnp.broadcast_to(face, (8, 8, 128)), pltpu.roll(f, 1, 1))


def ahead_y(f, face):
    return jnp.where(iota3(1) == 7, jnp.broadcast_to(face, (8, 8, 128)), pltpu.roll(f, 7, 1)) - f


def behind_z(f, face):
    return f - jnp.concatenate([face[None], f[:7]], axis=0)


def ahead_z(f, face):
    return jnp.concatenate([f[1:], face[None]], axis=0) - f


def velocity_rates(s, b, h):
    rx = b * (ahead_x(s[0], h["xr", 0]) + behind_y(s[3], h["yl", 3]) + behind_z(s[4], h["zl", 4]))
    ry = b * (behind_x(s[3], h["xl", 3]) + ahead_y(s[1], h["yr", 1]) + behind_z(s[5], h["zl", 5]))
    rz = b * (behind_x(s[4], h["xl", 4]) + behind_y(s[5], h["yl", 5]) + ahead_z(s[2], h["zr", 2]))
    return rx, ry, rz


def stress_rates(v, lam, mu, h):
    exx, eyy, ezz = behind_x(v[0], h["xl", 0]), behind_y(v[1], h["yl", 1]), behind_z(v[2], h["zl", 2])
    spread = lam * (exx + eyy + ezz)
    twice = 2.0 * mu
    return (
        spread + twice * exx,
        spread + twice * eyy,
        spread + twice * ezz,
        mu * (ahead_y(v[0], h["yr", 0]) + ahead_x(v[1], h["xr", 1])),
        mu * (ahead_z(v[0], h["zr", 0]) + ahead_x(v[2], h["xr", 2])),
        mu * (ahead_z(v[1], h["zr", 1]) + ahead_y(v[2], h["yr", 2])),
    )


class Zeros:
    def __getitem__(self, key):
        side = key[0]
        shape = (8, 1, 128) if side[0] == "y" else (8, 128)
        return jnp.zeros((8, 8, 128) if side[0] == "x" else shape, jnp.float32)


class Part:
    def __init__(self, kind, places):
        self.kind, self.places = kind, places

    def __getitem__(self, key):
        e, i = key if isinstance(key, tuple) else (key, 0)
        ref, first, _ = self.places[e]
        return ref[first + i]

    def at(self, e):
        ref, first, count = self.places[e]
        return ref.at[pl.ds(first, count)]


class Exchange:
    def __init__(self, e, buffers, spare, send, recv, messages, to, exists):
        self.e, self.buffers, self.spare, self.send, self.recv = e, buffers, spare, send, recv
        self.messages, self.to, self.exists = messages, to, exists

    def prepare(self):
        for part, step, _ in self.messages:
            target = part.at(self.e)
            _, first, count = part.places[self.e]
            aside = self.spare[part.kind].at[pl.ds(first, count)]

            @pl.when(jnp.logical_not(self.exists(step)))
            def _():
                zeros = self.spare[2 + part.kind].at[pl.ds(0, count)]
                pltpu.make_async_copy(zeros, aside, self.send).start()

            @pl.when(jnp.logical_not(self.exists(tuple(-d for d in step))))
            def _():
                zeros = self.spare[2 + part.kind].at[pl.ds(0, count)]
                pltpu.make_async_copy(zeros, target, self.recv).start()

    def start(self, *which):
        for n in which:
            part, step, source = self.messages[n]

            @pl.when(self.exists(step))
            def _():
                pltpu.make_async_remote_copy(
                    src_ref=source,
                    dst_ref=part.at(self.e),
                    send_sem=self.send,
                    recv_sem=self.recv,
                    device_id=self.to(step),
                    device_id_type=MESH,
                ).start()

    def all_of(self, sems):
        total = sum(ref.shape[0] for ref in self.buffers)
        everything = self.spare[4].at[pl.ds(0, total)]
        pltpu.make_async_copy(everything, everything, sems).wait()

    def receive(self):
        self.all_of(self.recv)


def kernel(
    sizes,
    store,
    hpeer,
    hslot,
    adj_in,
    lam_in,
    mu_in,
    buoy_in,
    src_in,
    wav_in,
    rec_in,
    tr_in,
    plan_in,
    adj_out,
    il_out,
    im_out,
    params,
    rec,
    traces,
    t_peer,
    t_slot,
    t_src,
    t_wav,
    t_plan,
    own_s,
    own_v,
    stage_s,
    stage_v,
    got_s,
    got_v,
    fv,
    fs,
    adj,
    a1,
    a0,
    bx,
    mx,
    lx,
    hits,
    s_xl,
    s_xr,
    s_yl,
    s_yr,
    s_zl,
    s_zr,
    r0_tiles,
    r0_rows,
    r1_tiles,
    r1_rows,
    f_xl,
    f_xr,
    f_yl,
    f_yr,
    f_zl,
    f_zr,
    g0_tiles,
    g0_rows,
    g1_tiles,
    g1_rows,
    c_xl,
    c_xr,
    c_yl,
    c_yr,
    c_zl,
    c_zr,
    d_tiles,
    d_rows,
    ar0_tiles,
    ar0_rows,
    ar1_tiles,
    ar1_rows,
    ad_tiles,
    ad_rows,
    ag0_tiles,
    ag0_rows,
    ag1_tiles,
    ag1_rows,
    no_tiles,
    no_rows,
    meter,
    in_sem,
    send_sem,
    recv_sem,
    frecv_sem,
    rs_send,
    rs_recv,
    ready,
):
    count = dict(zip(("gx", "gy", "gz"), sizes))
    index = {axis: lax.axis_index(axis) for axis in ("gx", "gy", "gz")}
    gz = index["gz"]

    axes = ("gx", "gy", "gz")

    def exists(step):
        found = None
        for axis, d in zip(axes, step):
            if d:
                here = index[axis] < count[axis] - 1 if d > 0 else index[axis] > 0
                found = here if found is None else jnp.logical_and(found, here)
        return found

    def at(step):
        return {axis: index[axis] + d for axis, d in zip(axes, step) if d}

    def local(src, dst, n):
        return pltpu.make_async_copy(src, dst, in_sem.at[n])

    loads = dict(
        peer=local(hpeer.at[0, 0], t_peer, 7),
        slot=local(hslot.at[0, 0], t_slot, 8),
        own_s=local(store.at[:, pl.ds(3, 6), 0], own_s, 9),
        av=local(adj_in.at[pl.ds(0, 3)], adj.at[pl.ds(0, 3)], 0),
        own_v=local(store.at[:, pl.ds(0, 3), 0], own_v, 10),
        as_=local(adj_in.at[pl.ds(3, 6)], adj.at[pl.ds(3, 6)], 11),
        lam=local(lam_in, params.at[0], 1),
        mu=local(mu_in, params.at[1], 1),
        buoy=local(buoy_in, params.at[2], 1),
        rec=local(rec_in.at[0, 0], rec, 2),
        traces=local(tr_in.at[0, 0, 0], traces, 3),
        plan=local(plan_in, t_plan, 4),
        wav=local(wav_in, t_wav, 5),
        src=local(src_in.at[0, 0, 0], t_src, 6),
    )
    for name in ("own_s", "peer", "slot"):
        loads[name].start()

    barrier = pltpu.get_barrier_semaphore()

    def greet(where):
        pl.semaphore_signal(barrier, inc=1, device_id=where, device_id_type=MESH)

    around = jnp.int32(0)
    for step in GREETED:

        @pl.when(exists(step))
        def _():
            greet(at(step))

        around = around + exists(step).astype(jnp.int32)
    for d in (1, 2, 3):
        greet({"gz": lax.rem(gz + d, 4)})

    for name, copy in loads.items():
        if name not in ("own_s", "peer", "slot"):
            copy.start()

    TILES, ROWS = 0, 1
    first, second, forward0, forward1, last_one = (
        (r0_tiles, r0_rows),
        (r1_tiles, r1_rows),
        (g0_tiles, g0_rows),
        (g1_tiles, g1_rows),
        (d_tiles, d_rows),
    )

    spares = [
        (*aside, no_tiles, no_rows, meter)
        for aside in (
            (ar0_tiles, ar0_rows),
            (ar1_tiles, ar1_rows),
            (ad_tiles, ad_rows),
            (ag0_tiles, ag0_rows),
            (ag1_tiles, ag1_rows),
        )
    ]

    def part(kind, *places):
        return Part(kind, [(buffers[kind], at_row, fields) for buffers, at_row, fields in places])

    r_xl = part(TILES, (first, 0, 1), (second, 0, 1))
    r_xr = part(TILES, (first, 1, 1), (second, 1, 1))
    r_zl = part(TILES, (first, 2, 1), (second, 2, 4))
    r_zr = part(TILES, (first, 3, 2), (second, 6, 4))
    r_yl = part(ROWS, (first, 0, 1), (second, 0, 4))
    r_yr = part(ROWS, (first, 1, 2), (second, 4, 4))

    def adjoint_exchange(r):
        up, down = ((1, 2), (4, 4))[r]
        return Exchange(
            r,
            (first, second)[r],
            spares[r],
            send_sem.at[0],
            recv_sem.at[r],
            (
                (r_xl, (1, 0, 0), s_xr.at[r]),
                (r_xr, (-1, 0, 0), s_xl.at[r]),
                (r_zl, (0, 0, 1), s_zr.at[r, pl.ds(0, up)]),
                (r_zr, (0, 0, -1), s_zl.at[r, pl.ds(0, down)]),
                (r_yl, (0, 1, 0), s_yr.at[r, pl.ds(0, up)]),
                (r_yr, (0, -1, 0), s_yl.at[r, pl.ds(0, down)]),
            ),
            at,
            exists,
        )

    def forward_part(kind, at_row, fields):
        return part(kind, (forward0, at_row, fields), (forward1, at_row, fields))

    g_xl, g_xr = forward_part(TILES, 0, 1), forward_part(TILES, 1, 1)
    g_zl, g_zr = forward_part(TILES, 2, 3), forward_part(TILES, 5, 3)
    exz_mm, exz_pp = forward_part(TILES, 8, 1), forward_part(TILES, 9, 2)
    exz_pm, exz_mp = forward_part(TILES, 11, 1), forward_part(TILES, 12, 1)
    eyz_mm, eyz_pp = forward_part(TILES, 13, 1), forward_part(TILES, 14, 2)
    eyz_pm, eyz_mp = forward_part(TILES, 16, 1), forward_part(TILES, 17, 1)
    g_yl, g_yr = forward_part(ROWS, 0, 3), forward_part(ROWS, 3, 3)
    exy_mm, exy_pp = forward_part(ROWS, 6, 1), forward_part(ROWS, 7, 2)
    exy_pm, exy_mp = forward_part(ROWS, 9, 1), forward_part(ROWS, 10, 1)

    def forward_exchange(e):
        return Exchange(
            e,
            (forward0, forward1)[e],
            spares[3 + e],
            send_sem.at[0],
            frecv_sem.at[e],
            (
                (g_xl, (1, 0, 0), f_xr.at[e]),
                (g_xr, (-1, 0, 0), f_xl.at[e]),
                (g_yl, (0, 1, 0), f_yr.at[e, pl.ds(0, 3)]),
                (g_yr, (0, -1, 0), f_yl.at[e, pl.ds(0, 3)]),
                (g_zl, (0, 0, 1), f_zr.at[e, pl.ds(0, 3)]),
                (g_zr, (0, 0, -1), f_zl.at[e, pl.ds(0, 3)]),
                (exy_mm, (1, 1, 0), f_yr.at[e, pl.ds(0, 1)]),
                (exy_pp, (-1, -1, 0), f_yl.at[e, pl.ds(2, 2)]),
                (exy_pm, (-1, 1, 0), f_yr.at[e, pl.ds(1, 1)]),
                (exy_mp, (1, -1, 0), f_yl.at[e, pl.ds(4, 1)]),
                (exz_mm, (1, 0, 1), f_zr.at[e, pl.ds(0, 1)]),
                (exz_pp, (-1, 0, -1), f_zl.at[e, pl.ds(2, 2)]),
                (exz_pm, (-1, 0, 1), f_zr.at[e, pl.ds(1, 1)]),
                (exz_mp, (1, 0, -1), f_zl.at[e, pl.ds(6, 1)]),
                (eyz_mm, (0, 1, 1), f_zr.at[e, pl.ds(1, 1)]),
                (eyz_pp, (0, -1, -1), f_zl.at[e, pl.ds(4, 2)]),
                (eyz_pm, (0, -1, 1), f_zr.at[e, pl.ds(0, 1)]),
                (eyz_mp, (0, 1, -1), f_zl.at[e, pl.ds(6, 1)]),
            ),
            at,
            exists,
        )

    d_xl, d_xr = part(TILES, (last_one, 0, 1)), part(TILES, (last_one, 1, 1))
    d_zl, d_zr = part(TILES, (last_one, 2, 3)), part(TILES, (last_one, 5, 3))
    vxz_pm, vxz_mp = part(TILES, (last_one, 8, 1)), part(TILES, (last_one, 9, 1))
    vyz_pm, vyz_mp = part(TILES, (last_one, 10, 1)), part(TILES, (last_one, 11, 1))
    d_yl, d_yr = part(ROWS, (last_one, 0, 3)), part(ROWS, (last_one, 3, 3))
    vxy_pm, vxy_mp = part(ROWS, (last_one, 6, 1)), part(ROWS, (last_one, 7, 1))
    last_exchange = Exchange(
        0,
        last_one,
        spares[2],
        send_sem.at[0],
        recv_sem.at[2],
        (
            (d_xl, (1, 0, 0), c_xr),
            (d_xr, (-1, 0, 0), c_xl),
            (d_yl, (0, 1, 0), c_yr),
            (d_yr, (0, -1, 0), c_yl),
            (d_zl, (0, 0, 1), c_zr),
            (d_zr, (0, 0, -1), c_zl),
            (vxy_pm, (-1, 1, 0), c_yr.at[pl.ds(0, 1)]),
            (vxy_mp, (1, -1, 0), c_yl.at[pl.ds(0, 1)]),
            (vxz_pm, (-1, 0, 1), c_zr.at[pl.ds(0, 1)]),
            (vxz_mp, (1, 0, -1), c_zl.at[pl.ds(0, 1)]),
            (vyz_pm, (0, -1, 1), c_zr.at[pl.ds(0, 1)]),
            (vyz_mp, (0, 1, -1), c_zl.at[pl.ds(1, 1)]),
        ),
        at,
        exists,
    )

    lam, mu, buoy = params.at[0], params.at[1], params.at[2]
    av, as_ = [adj.at[i] for i in range(3)], [adj.at[3 + i] for i in range(6)]

    def fill_faces(r, up, down):
        (xu, yu, zu), (xd, yd, zd) = up, down
        s_xr[r, 0] = pack_columns(xu, 127)
        s_xl[r, 0] = pack_columns(xd, 0)
        for i, f in enumerate(zu):
            s_zr[r, i] = f[7]
        for i, f in enumerate(zd):
            s_zl[r, i] = f[0]
        for i, f in enumerate(yu):
            s_yr[r, i] = f[:, 7:8, :]
        for i, f in enumerate(yd):
            s_yl[r, i] = f[:, 0:1, :]

    def fill_velocity():
        v = [f[...] for f in av]
        fill_faces(0, ((v[0],), (v[1],), (v[2],)), ((v[1], v[2]), (v[0], v[2]), (v[0], v[1])))

    def send_stress(r, s):
        b, l, m = buoy[...], lam[...], mu[...]
        fill_faces(
            r,
            ((s[3], s[4], b, m), (s[3], s[5], b, m), (s[4], s[5], b, m)),
            ((s[0], b, l, m), (s[1], b, l, m), (s[2], b, l, m)),
        )
        adjoint_exchange(r).start(*range(6))

    for name in ("peer", "slot", "own_s"):
        loads[name].wait()
    slots = []
    for d in range(4):
        brick = lax.rem(gz + d, 4)
        listed, shift = jnp.int32(0), jnp.int32(0)
        for p in range(8):
            held = t_peer[brick, p] == gz
            listed = jnp.where(held, listed + lax.shift_left(t_slot[brick, p], shift), listed)
            shift = jnp.where(held, shift + 3, shift)
        slots.append([lax.bitwise_and(lax.shift_right_logical(listed, 3 * j), 7) for j in range(CAP)])

    def stage(own, staged, got):
        for d in (2, 1, 3, 0):
            for j in range(CAP):
                if d:
                    staged[(d - 1) * CAP + j] = own[slots[d][j]]
                else:
                    got[3 * CAP + j] = own[slots[d][j]]

    def restore(staged, got, n):
        odd = lax.rem(gz, 2)
        for d in (2, 3 - 2 * odd, 1 + 2 * odd):
            rows = pl.ds((d - 1) * CAP, CAP)
            pltpu.make_async_remote_copy(
                src_ref=staged.at[rows],
                dst_ref=got.at[rows],
                send_sem=rs_send.at[n],
                recv_sem=rs_recv.at[n],
                device_id={"gz": lax.rem(gz + d, 4)},
                device_id_type=MESH,
            ).start()

    def restored(got, n):
        rows = got.at[pl.ds(0, 3 * CAP)]
        pltpu.make_async_copy(rows, rows, rs_recv.at[n]).wait()

    where_is, seen = [], jnp.int32(0)
    for p in range(8):
        holder = t_peer[gz, p]
        at_digit = holder * 4
        before = lax.bitwise_and(lax.shift_right_logical(seen, at_digit), 15)
        where_is.append(lax.bitwise_and(gz - holder + 3, 3) * CAP + jnp.minimum(before, CAP - 1))
        seen = seen + lax.shift_left(jnp.int32(1), at_digit)

    stage(own_s, stage_s, got_s)
    loads["av"].wait()
    fill_velocity()
    pl.semaphore_wait(barrier, around + 3)
    adjoint_exchange(0).start(0, 1)
    restore(stage_s, got_s, 0)
    adjoint_exchange(0).start(2, 3, 4, 5)

    for step in GREETED:

        @pl.when(exists(step))
        def _():
            pl.semaphore_signal(ready, inc=1, device_id=at(step), device_id_type=MESH)

    loads["own_v"].wait()
    stage(own_v, stage_v, got_v)

    def stress_faces(r):
        xl, xr = r_xl[r], r_xr[r]
        return {
            ("xr", 0): unpack_columns(xr, 0, 127),
            ("xl", 3): unpack_columns(xl, 0, 0),
            ("xl", 4): unpack_columns(xl, 1, 0),
            ("yl", 3): r_yl[r, 0],
            ("yl", 5): r_yl[r, 1],
            ("yr", 1): r_yr[r, 0],
            ("zl", 4): r_zl[r, 0],
            ("zl", 5): r_zl[r, 1],
            ("zr", 2): r_zr[r, 0],
        }

    def velocity_faces(r):
        xl, xr = r_xl[r], r_xr[r]
        return {
            ("xl", 0): unpack_columns(xl, 0, 0),
            ("xr", 1): unpack_columns(xr, 0, 127),
            ("xr", 2): unpack_columns(xr, 1, 127),
            ("yl", 1): r_yl[r, 0],
            ("yr", 0): r_yr[r, 0],
            ("yr", 2): r_yr[r, 1],
            ("zl", 2): r_zl[r, 0],
            ("zr", 0): r_zr[r, 0],
            ("zr", 1): r_zr[r, 1],
        }

    def forward_edges(e):
        exchange = forward_exchange(e)
        f_yr[e, 0] = fs[3, :, 7:8, :]
        f_yr[e, 1] = fs[5, :, 7:8, :]
        for i, f in ((2, 1), (3, 0), (4, 4)):
            f_yl[e, i] = fs[f, :, 0:1, :]
        exchange.start(6, 7, 8, 9)
        f_zr[e, 0] = fs[4, 7]
        f_zr[e, 1] = fs[5, 7]
        for i, f in ((2, 2), (3, 0), (4, 2), (5, 1), (6, 3)):
            f_zl[e, i] = fs[f, 0]
        exchange.start(*range(10, 18))

    def forward_faces(e):
        exchange = forward_exchange(e)
        rates = velocity_rates([fs[i] for i in range(6)], buoy[...], Zeros())
        for i in range(3):
            fv[i] = fv[i] + rates[i]
        f_xr[e, 0] = pack_columns((fs[3], fs[4], fv[0]), 127)
        f_xl[e, 0] = pack_columns((fs[0], fv[1], fv[2]), 0)
        exchange.start(0, 1)
        f_zr[e, 2] = fv[2, 7]
        f_zl[e, 0] = fv[0, 0]
        f_zl[e, 1] = fv[1, 0]
        exchange.start(4, 5)
        f_yr[e, 2] = fv[1, :, 7:8, :]
        f_yl[e, 0] = fv[0, :, 0:1, :]
        f_yl[e, 1] = fv[2, :, 0:1, :]
        exchange.start(2, 3)

    def forward_step(e):
        xl, xr = g_xl[e], g_xr[e]
        lane3, row3 = iota3(2), iota3(1)
        lane2, row2 = iota2(1), iota2(0)
        z1 = lax.broadcasted_iota(jnp.int32, (8, 1, 128), 0)
        lane1 = lax.broadcasted_iota(jnp.int32, (8, 1, 128), 2)

        def layer(at_z, tile, like):
            return jnp.where(iota3(0) == at_z, tile[None], 0.0) if like == 3 else jnp.where(z1 == at_z, tile, 0.0)

        def first_lane(f, axis):
            return pltpu.roll(f, 1, axis)

        def last_lane(f, axis):
            return pltpu.roll(f, 127, axis)

        mm, pp = first_lane(exy_mm[e, 0], 2), (last_lane(exy_pp[e, 0], 2), last_lane(exy_pp[e, 1], 2))
        pm, mp = last_lane(exy_pm[e, 0], 2), first_lane(exy_mp[e, 0], 2)
        zmm, zpp = first_lane(exz_mm[e, 0], 1), (last_lane(exz_pp[e, 0], 1), last_lane(exz_pp[e, 1], 1))
        zpm, zmp = last_lane(exz_pm[e, 0], 1), first_lane(exz_mp[e, 0], 1)
        all3 = (8, 8, 128)
        nothing = jnp.zeros(all3, jnp.float32)

        def row(at_y, face):
            return jnp.where(row3 == at_y, jnp.broadcast_to(face, all3), nothing)

        b = buoy[...]
        h = {}
        h["xl", 0] = unpack_columns(xl, 2, 0) + bx[0] * (fs[0] - row(0, mm) - layer(0, zmm, 3))
        h["xr", 1] = unpack_columns(xr, 1, 127) + bx[1] * (row(7, pp[0]) - fs[3] - layer(0, zpm, 3))
        h["xr", 2] = unpack_columns(xr, 2, 127) + bx[1] * (layer(7, zpp[0], 3) - fs[4] - row(0, pm))

        def y_layer(at_z, tile, at_y):
            return jnp.where(z1 == at_z, jnp.broadcast_to(tile[at_y : at_y + 1, :][None], (8, 1, 128)), 0.0)

        bym, byp = r_yl[1, 2], r_yr[1, 1]
        h["yl", 1] = g_yl[e, 2] + bym * (
            fs[1, :, 0:1, :] - jnp.where(lane1 == 0, mm, 0.0) - y_layer(0, eyz_mm[e, 0], 7)
        )
        h["yr", 0] = g_yr[e, 0] + byp * (
            jnp.where(lane1 == 127, pp[1], 0.0) - fs[3, :, 7:8, :] - y_layer(0, eyz_pm[e, 0], 0)
        )
        h["yr", 2] = g_yr[e, 1] + byp * (
            y_layer(7, eyz_pp[e, 0], 0) - fs[5, :, 7:8, :] - jnp.where(lane1 == 0, mp, 0.0)
        )

        def y_edge(tile, at_y, from_y):
            return jnp.where(row2 == at_y, jnp.broadcast_to(tile[from_y : from_y + 1, :], (8, 128)), 0.0)

        bzm, bzp = r_zl[1, 2], r_zr[1, 1]
        h["zl", 2] = g_zl[e, 2] + bzm * (fs[2, 0] - jnp.where(lane2 == 0, zmm, 0.0) - y_edge(eyz_mm[e, 0], 0, 7))
        h["zr", 0] = g_zr[e, 0] + bzp * (
            jnp.where(lane2 == 127, zpp[1], 0.0) - fs[4, 7] - y_edge(eyz_mp[e, 0], 0, 7)
        )
        h["zr", 1] = g_zr[e, 1] + bzp * (
            y_edge(eyz_pp[e, 1], 7, 0) - fs[5, 7] - jnp.where(lane2 == 0, zmp, 0.0)
        )

        fv[0] = fv[0] + b * (jnp.where(lane3 == 127, unpack_columns(xr, 0, 127), 0.0) - row(0, g_yl[e, 0]))
        fv[1] = fv[1] + b * (row(7, g_yr[e, 2]) - jnp.where(lane3 == 0, unpack_columns(xl, 0, 0), 0.0))
        fv[2] = fv[2] - b * (jnp.where(lane3 == 0, unpack_columns(xl, 1, 0), 0.0) + row(0, g_yl[e, 1]))
        fv[0, 0] = fv[0, 0] - buoy[0] * g_zl[e, 0]
        fv[1, 0] = fv[1, 0] - buoy[0] * g_zl[e, 1]
        fv[2, 7] = fv[2, 7] + buoy[7] * g_zr[e, 2]
        return stress_rates([fv[i] for i in range(3)], lam[...], mu[...], h)

    def adjoint_send():
        c_yr[0] = av[1][:, 7:8, :]
        c_yl[0] = av[0][:, 0:1, :]
        c_yl[1] = av[2][:, 0:1, :]
        last_exchange.start(6, 7)
        c_zr[0] = av[2][7]
        c_zl[0] = av[0][0]
        c_zl[1] = av[1][0]
        last_exchange.start(8, 9, 10, 11)
        v = [f[...] for f in av]
        rates = stress_rates(v, lam[...], mu[...], Zeros())
        s = [a0[i] - rates[i] for i in range(6)]
        c_xr[0] = pack_columns((v[0], s[3], s[4]), 127)
        c_xl[0] = pack_columns((v[1], v[2], s[0]), 0)
        last_exchange.start(0, 1)
        c_zr[1] = s[4][7]
        c_zr[2] = s[5][7]
        c_zl[2] = s[2][0]
        last_exchange.start(4, 5)
        c_yr[1] = s[3][:, 7:8, :]
        c_yr[2] = s[5][:, 7:8, :]
        c_yl[2] = s[1][:, 0:1, :]
        last_exchange.start(2, 3)

    def adjoint_step():
        v = [f[...] for f in av]
        xl, xr = d_xl[0], d_xr[0]
        lane2, row2 = iota2(1), iota2(0)
        all3 = (8, 8, 128)
        z1 = lax.broadcasted_iota(jnp.int32, (8, 1, 128), 0)
        lane1 = lax.broadcasted_iota(jnp.int32, (8, 1, 128), 2)
        h = {
            ("xl", 0): unpack_columns(xl, 0, 0),
            ("xr", 1): unpack_columns(xr, 0, 127),
            ("xr", 2): unpack_columns(xr, 1, 127),
            ("yl", 1): d_yl[0, 0],
            ("yr", 0): d_yr[0, 0],
            ("yr", 2): d_yr[0, 1],
            ("zl", 2): d_zl[0, 0],
            ("zr", 0): d_zr[0, 0],
            ("zr", 1): d_zr[0, 1],
        }
        rates = stress_rates(v, lam[...], mu[...], h)
        s = [a0[i] - rates[i] for i in range(6)]

        xy_pm, xy_mp = pltpu.roll(vxy_pm[0], 127, 2), pltpu.roll(vxy_mp[0], 1, 2)
        xz_pm, xz_mp = pltpu.roll(vxz_pm[0], 127, 1), pltpu.roll(vxz_mp[0], 1, 1)

        def row(at_y, face):
            return jnp.where(iota3(1) == at_y, jnp.broadcast_to(face, all3), 0.0)

        def layer(at_z, tile):
            return jnp.where(iota3(0) == at_z, tile[None], 0.0)

        def y_layer(at_z, tile, at_y):
            return jnp.where(z1 == at_z, jnp.broadcast_to(tile[at_y : at_y + 1, :][None], (8, 1, 128)), 0.0)

        def y_edge(tile, at_y, from_y):
            return jnp.where(row2 == at_y, jnp.broadcast_to(tile[from_y : from_y + 1, :], (8, 128)), 0.0)

        both = lx[...] + 2.0 * mx[1]
        g = {}
        g["xl", 3] = unpack_columns(xl, 1, 0) - mx[0] * (v[1] + row(7, xy_mp))
        g["xl", 4] = unpack_columns(xl, 2, 0) - mx[0] * (v[2] + layer(7, xz_mp))
        g["xr", 0] = unpack_columns(xr, 2, 127) + both * v[0] + lx[...] * (row(0, xy_pm) + layer(0, xz_pm))
        mu_m, lam_p, mu_p = r_yl[1, 3], r_yr[1, 2], r_yr[1, 3]
        g["yl", 3] = d_yl[0, 1] - mu_m * (v[0][:, 0:1, :] + jnp.where(lane1 == 127, xy_pm, 0.0))
        g["yl", 5] = d_yl[0, 2] - mu_m * (v[2][:, 0:1, :] + y_layer(7, vyz_mp[0], 7))
        g["yr", 1] = (
            d_yr[0, 2]
            + (lam_p + 2.0 * mu_p) * v[1][:, 7:8, :]
            + lam_p * (jnp.where(lane1 == 0, xy_mp, 0.0) + y_layer(0, vyz_pm[0], 0))
        )
        mu_m, lam_p, mu_p = r_zl[1, 3], r_zr[1, 2], r_zr[1, 3]
        g["zl", 4] = d_zl[0, 1] - mu_m * (v[0][0] + jnp.where(lane2 == 127, xz_pm, 0.0))
        g["zl", 5] = d_zl[0, 2] - mu_m * (v[1][0] + y_edge(vyz_pm[0], 7, 0))
        g["zr", 2] = (
            d_zr[0, 2]
            + (lam_p + 2.0 * mu_p) * v[2][7]
            + lam_p * (jnp.where(lane2 == 0, xz_mp, 0.0) + y_edge(vyz_mp[0], 0, 7))
        )
        for i in range(6):
            adj_out[3 + i] = s[i]
        rates = velocity_rates(s, buoy[...], g)
        for i in range(3):
            adj_out[i] = v[i] - rates[i]

    restore(stage_v, got_v, 1)
    no_tiles[...] = jnp.zeros(no_tiles.shape, jnp.float32)
    no_rows[...] = jnp.zeros(no_rows.shape, jnp.float32)
    exchanges = (adjoint_exchange(0), adjoint_exchange(1), last_exchange, forward_exchange(0), forward_exchange(1))
    for exchange in exchanges:
        exchange.prepare()

    for name in ("rec", "traces", "plan", "as_"):
        loads[name].wait()
    pltpu.make_async_copy(params, params, in_sem.at[1]).wait()
    cells = rec[0]
    row_of, x_of = lax.shift_right_logical(cells, 7), lax.bitwise_and(cells, 127)
    rows = lax.broadcasted_iota(jnp.int32, (64, 64), 0)
    hit = rows == jnp.broadcast_to(row_of, (64, 64))
    samples = [jnp.broadcast_to(traces[pl.ds(t_plan[k], 1), :], (64, 64)) for k in range(STEPS)]
    left = jnp.concatenate([jnp.where(hit, samples[k], 0.0) for k in range(STEPS)], axis=0)
    columns = lax.broadcasted_iota(jnp.int32, (128, 64), 0)
    right = jnp.where(columns == jnp.broadcast_to(x_of, (128, 64)), 1.0, 0.0)
    spread = lax.dot_general(
        left, right, (((1,), (1,)), ((), ())), precision=lax.Precision.HIGHEST, preferred_element_type=jnp.float32
    )
    spread = spread.reshape(STEPS, 8, 8, 128)
    for i in range(3):
        a1[i] = as_[i][...] + spread[1]
        a0[i] = spread[0]
    for i in range(3, 6):
        a1[i] = as_[i][...]

    for name in ("wav", "src"):
        loads[name].wait()
    flat = iota3(0) * 1024 + iota3(1) * 128 + iota3(2)
    counted = jnp.zeros((8, 8, 128), jnp.float32)
    for j in range(t_src.shape[0]):
        counted = counted + jnp.where(flat == t_src[j], 1.0, 0.0)
    hits[...] = counted


    restored(got_s, 0)
    for p in range(8):
        fs[:, p] = got_s[where_is[p]].astype(jnp.float32)
    pl.semaphore_wait(ready, around)
    forward_edges(0)
    adjoint_exchange(0).receive()
    rates = stress_rates([f[...] for f in av], lam[...], mu[...], velocity_faces(0))
    for i in range(6):
        as_[i][...] = a1[i] - rates[i]
    send_stress(1, [f[...] for f in as_])

    restored(got_v, 1)
    for p in range(8):
        fv[:, p] = got_v[where_is[p]].astype(jnp.float32)
    forward_faces(0)

    adjoint_exchange(1).receive()
    rates = velocity_rates([f[...] for f in as_], buoy[...], stress_faces(1))
    for i in range(3):
        av[i][...] = av[i][...] - rates[i]
    for i in range(3):
        a0[i] = a0[i] + as_[i][...]
    for i in range(3, 6):
        a0[i] = as_[i][...]
    adjoint_send()
    bx[0] = unpack_columns(r_xl[1], 2, 0)
    mx[0] = unpack_columns(r_xl[1], 3, 0)
    bx[1] = unpack_columns(r_xr[1], 1, 127)
    lx[...] = unpack_columns(r_xr[1], 2, 127)
    mx[1] = unpack_columns(r_xr[1], 3, 127)

    forward_exchange(0).receive()
    rates = forward_step(0)
    pulse = hits[...] * t_wav[t_plan[0]]
    for i in range(3):
        fs[i] = fs[i] + rates[i] + pulse
    for i in range(3, 6):
        fs[i] = fs[i] + rates[i]
    forward_edges(1)
    forward_faces(1)

    def image(s, a):
        by_lambda = (s[0] + s[1] + s[2]) * (a[0] + a[1] + a[2])
        by_mu = s[0] * a[0] + s[1] * a[1] + s[2] * a[2] + 2.0 * (s[3] * a[3] + s[4] * a[4] + s[5] * a[5])
        return by_lambda, by_mu

    by_lambda, by_mu = image(fs, a0)
    il_out[...] = by_lambda
    im_out[...] = by_mu

    last_exchange.receive()
    adjoint_step()
    for n, staged in enumerate((stage_s, stage_v)):
        pltpu.make_async_copy(staged, staged, rs_send.at[n]).wait()

    forward_exchange(1).receive()
    rates = forward_step(1)
    pulse = hits[...] * t_wav[t_plan[1]]
    last = [fs[i] + rates[i] + pulse for i in range(3)] + [fs[i] + rates[i] for i in range(3, 6)]
    by_lambda, by_mu = image(last, a1)
    il_out[...] += by_lambda
    im_out[...] += by_mu
    pltpu.make_async_copy(meter, meter, send_sem.at[0]).wait()


def write_out(adj, il, im, adj_out, il_out, im_out, sem):
    copies = [
        pltpu.make_async_copy(src, dst, sem.at[n])
        for n, (src, dst) in enumerate(((adj, adj_out), (il, il_out), (im, im_out)))
    ]
    for copy in copies:
        copy.start()
    for copy in copies:
        copy.wait()


def solution(mesh):
    sizes = (mesh.shape["gx"], mesh.shape["gy"], mesh.shape["gz"])
    f32, i32, bf16 = jnp.float32, jnp.int32, jnp.bfloat16
    brick = (8, 8, 128)

    def on_device(*args):
        nt, nrec = args[10].shape[-2:]
        nsrc = args[7].shape[-1]
        vmem = pltpu.VMEM
        scratch = [
            vmem((3,) + brick, f32),
            vmem((1, nrec), i32),
            vmem((nt, nrec), f32),
            pltpu.SMEM((4, 8), i32),
            pltpu.SMEM((4, 8), i32),
            pltpu.SMEM((nsrc,), i32),
            pltpu.SMEM((nt,), f32),
            pltpu.SMEM((STEPS,), i32),
            vmem((8, 6, 8, 128), bf16),
            vmem((8, 3, 8, 128), bf16),
            vmem((3 * CAP, 6, 8, 128), bf16),
            vmem((3 * CAP, 3, 8, 128), bf16),
            vmem((4 * CAP, 6, 8, 128), bf16),
            vmem((4 * CAP, 3, 8, 128), bf16),
            vmem((3,) + brick, f32),
            vmem((6,) + brick, f32),
            vmem((9,) + brick, f32),
            vmem((6,) + brick, f32),
            vmem((6,) + brick, f32),
            vmem((2,) + brick, f32),
            vmem((2,) + brick, f32),
            vmem(brick, f32),
            vmem(brick, f32),
        ]
        row, tile = (8, 1, 128), (8, 128)
        scratch += [vmem((2, 1) + tile, f32)] * 2 + [vmem((2, 5) + row, f32)] * 2 + [vmem((2, 5) + tile, f32)] * 2
        scratch += [vmem((5,) + tile, f32), vmem((3,) + row, f32), vmem((10,) + tile, f32), vmem((8,) + row, f32)]
        scratch += [vmem((2, 1) + tile, f32)] * 2 + [vmem((2, 5) + row, f32), vmem((2, 3) + row, f32)]
        scratch += [vmem((2, 7) + tile, f32), vmem((2, 3) + tile, f32)]
        scratch += [vmem((18,) + tile, f32), vmem((11,) + row, f32)] * 2
        scratch += [vmem((1,) + tile, f32)] * 2 + [vmem((3,) + row, f32)] * 2 + [vmem((3,) + tile, f32)] * 2
        scratch += [vmem((12,) + tile, f32), vmem((8,) + row, f32)]
        for tiles, rows in ((5, 3), (10, 8), (12, 8), (18, 11), (18, 11), (5, 5)):
            scratch += [vmem((tiles,) + tile, f32), vmem((rows,) + row, f32)]
        scratch += [vmem((104,) + tile, f32)]
        dma = pltpu.SemaphoreType.DMA
        scratch += [dma((12,)), dma((1,)), dma((3,)), dma((2,)), dma((2,)), dma((2,)), pltpu.SemaphoreType.REGULAR]
        shapes = ((9,) + brick, brick, brick)
        results = pl.pallas_call(
            functools.partial(kernel, sizes),
            out_shape=tuple(pltpu.VMEM(shape, f32) for shape in shapes),
            in_specs=[pl.BlockSpec(memory_space=pl.ANY)] * 12,
            out_specs=(pl.BlockSpec(memory_space=pltpu.VMEM),) * 3,
            scratch_shapes=scratch,
            compiler_params=pltpu.CompilerParams(
                collective_id=0, has_side_effects=True
            ),
            name="window",
        )(*args)
        return pl.pallas_call(
            write_out,
            out_shape=tuple(jax.ShapeDtypeStruct(shape, f32) for shape in shapes),
            in_specs=[pl.BlockSpec(memory_space=pltpu.VMEM)] * 3,
            out_specs=(pl.BlockSpec(memory_space=pl.ANY),) * 3,
            scratch_shapes=[pltpu.SemaphoreType.DMA((3,))],
            compiler_params=pltpu.CompilerParams(vmem_limit_bytes=16 << 20),
            name="write_out",
        )(*results)

    return jax.shard_map(
        on_device,
        mesh=mesh,
        in_specs=(
            P("gz", None, None, "gy", "gx"),
            P("gx", "gy", None, None),
            P("gx", "gy", None, None),
            P(None, "gz", "gy", "gx"),
            P("gz", "gy", "gx"),
            P("gz", "gy", "gx"),
            P("gz", "gy", "gx"),
            P("gz", "gy", "gx", None),
            P(),
            P("gz", "gy", "gx", None),
            P("gz", "gy", "gx", None, None),
            P(),
        ),
        out_specs=(P(None, "gz", "gy", "gx"), P("gz", "gy", "gx"), P("gz", "gy", "gx")),
        check_vma=False,
    )
```
